32 devices in a mesh: groups: 2 (over y), blk: 4 (over z), leaf: 2 (over x), sample: 2 (over core).
Axes of the slice: x: 2, y: 2, z: 4, core: 2. Of those that a mesh axis runs over, the one named last changes fastest.
Arguments:
- residual: float32 [256, 128, 256], P(('groups', 'blk', 'leaf'), 'sample'), parts along dimension 0, may hold values from -60 to 60
- direction: bfloat16 [256, 128, 256], P(('groups', 'blk', 'leaf'), 'sample'), parts along dimension 0, may hold values from -60 to 60
- step: float32 [256], P(('groups', 'sample')), parts along dimension 0, may hold values from 0.2 to 0.8
- coords: bfloat16 [256, 3, 256], P(('groups', 'blk', 'leaf')), parts along dimension 0, may hold values from 0 to 1
- order: int32 [256, 256], P(('groups', 'blk', 'leaf')), parts along dimension 0, may hold values from 0 to 255, each once within a row
- basis: bfloat16 [256, 64, 256], P(('groups', 'blk', 'leaf')), parts along dimension 0, may hold values from -0.5 to 0.5
- leaf_transfer: bfloat16 [256, 64, 64], P(('groups', 'blk', 'leaf')), parts along dimension 0, may hold values from -0.75 to 0.75
- node_transfer: bfloat16 [16, 64, 64], P(('groups', 'blk', 'leaf')), parts along dimension 0, may hold values from -0.75 to 0.75
- near_list: int32 [256, 12], P(('groups', 'blk', 'leaf')), parts along dimension 0, may hold values from 0 to 127, as said below
- coupling_list: int32 [256, 8], P(('groups', 'blk', 'leaf')), parts along dimension 0, may hold values from 0 to 127, as said below
- coupling: bfloat16 [256, 8, 64, 64], P(('groups', 'blk', 'leaf')), parts along dimension 0, may hold values from -0.25 to 0.25
- top_list: int32 [8, 4], P(('groups', 'blk')), parts along dimension 0, may hold values from 0 to 3, as said below
- top_coupling: bfloat16 [8, 4, 64, 64], P(('groups', 'blk')), parts along dimension 0, may hold values from -0.0625 to 0.0625
Outputs:
- residual_next: float32 [256, 128, 256], P(('groups', 'blk', 'leaf'), 'sample'), parts along dimension 0
- direction_next: bfloat16 [256, 128, 256], P(('groups', 'blk', 'leaf'), 'sample'), parts along dimension 0
The draws below stay inside these ranges and needn't reach their ends.
There are 2 independent parts, one for each index of `groups`. The reference program is written for one: setup_inputs(seed, part) draws one part's arguments, and reference() takes and returns one part's arrays. A program takes and returns all parts, laid end to end along the dimension named above; each array names one. Nothing has to cross between parts.
Inputs may be any that keep to these rules, and one draw needn't show every extreme that they name: `near_list`: entry 0 of leaf g is g itself; the other entries are distinct leaves other than g, each at most 16 positions from g around the cycle of 128 leaves; some leaf names both g - 16 and g + 16 (mod 128). `coupling_list`: the entries of leaf g are distinct leaves of the aligned blocks of 16 leaves just before and just after g's own block, around the cycle of 128 leaves, each more than 16 positions from g. `top_list`: the entries of top cluster b name clusters other than b; they may repeat.
All inputs are finite; a program needn't handle non-finite values.
Results may differ from the reference program's by a relative error of at most 0.0065.
Values may be sent and summed in bfloat16 or wider, within the bound.
No kernel may reach another device: no remote copies, remote signals or barrier semaphores. Data moves between devices by JAX's collectives and lax.ppermute only.
A program may use at most 64 MiB of HBM per device.

```python
import math
import jax
import jax.numpy as jnp
from jax import lax

LEAF_PTS = 256
RANK = 64
SAMPLES = 128
LEAF_DEV = 16
NNEAR = 12
NCPL = 8
SUBTREES = 2
CLUSTERS = 4
NODES = 8
NLEAF = 128
NTOP = 4


def scaled_field(key):
    key_base, key_rough, key_column = jax.random.split(key, 3)
    rising = 10.0 ** (jnp.arange(NLEAF, dtype=jnp.float32) / NLEAF - 0.5)
    rough_rows = jax.random.uniform(key_rough, (NLEAF, 1, LEAF_PTS), jnp.float32, 0.5, 1.5)
    column = 10.0 ** jax.random.uniform(key_column, (1, SAMPLES, 1), jnp.float32, -0.5, 0.5)
    base_field = jax.random.normal(key_base, (NLEAF, SAMPLES, LEAF_PTS), jnp.float32)
    base_field = jnp.clip(base_field, -4.0, 4.0)
    return base_field * rising[:, None, None] * rough_rows * column


def draw_residual(key, part):
    return scaled_field(jax.random.fold_in(key, 11))


def draw_direction(key, part):
    return scaled_field(jax.random.fold_in(key, 23)).astype(jnp.bfloat16)


def draw_near_list(key, part):
    reach = LEAF_DEV
    key_scores, key_leaf = jax.random.split(jax.random.fold_in(key, 37))
    candidate = jnp.arange(2 * reach, dtype=jnp.int32)[None, :]
    scores = jax.random.randint(key_scores, (NLEAF, 2 * reach), 0, 1 << 20) * (4 * reach) + candidate
    chosen_leaf = jax.random.randint(key_leaf, (), 0, NLEAF)
    leaf_ids = jnp.arange(NLEAF, dtype=jnp.int32)[:, None]
    forced = (leaf_ids == chosen_leaf) & ((candidate == 0) | (candidate == 2 * reach - 1))
    scores = jnp.where(forced, candidate - 4 * reach, scores)
    picked = jnp.argsort(scores, axis=1)[:, :NNEAR - 1].astype(jnp.int32)
    offsets = jnp.where(picked < reach, picked - reach, picked - reach + 1)
    others = jnp.mod(leaf_ids + offsets, NLEAF)
    return jnp.concatenate([leaf_ids, others], axis=1).astype(jnp.int32)


def draw_coupling_list(key, part):
    reach = LEAF_DEV
    count = reach - 1
    leaf_ids = jnp.arange(NLEAF, dtype=jnp.int32)[:, None]
    local_slot = leaf_ids % reach
    block_id = leaf_ids // reach
    candidate = jnp.arange(count, dtype=jnp.int32)[None, :]
    is_after = candidate < count - local_slot
    next_names = (block_id + 1) * reach + local_slot + 1 + candidate
    prev_names = (block_id - 1) * reach + candidate - (count - local_slot)
    names = jnp.mod(jnp.where(is_after, next_names, prev_names), NLEAF)
    scores = jax.random.randint(jax.random.fold_in(key, 41), (NLEAF, count), 0, 1 << 20) * (2 * reach) + candidate
    picked = jnp.argsort(scores, axis=1)[:, :NCPL]
    return jnp.take_along_axis(names, picked, axis=1).astype(jnp.int32)


def draw_top_list(key, part):
    offsets = jax.random.randint(jax.random.fold_in(key, 53), (CLUSTERS, NTOP), 1, CLUSTERS)
    return jnp.mod(jnp.arange(CLUSTERS, dtype=jnp.int32)[:, None] + offsets, CLUSTERS).astype(jnp.int32)


def block_levels(stream_key, extent, cuts, least, largest):
    gain = 1.0
    for position, parts in cuts:
        draws = jax.random.uniform(jax.random.fold_in(jax.random.fold_in(stream_key, 6), position), (parts,), jnp.float32, least / len(cuts), largest / len(cuts))
        gain = gain * jnp.repeat(jnp.exp(draws), extent[position] // parts).reshape((-1,) + (1,) * (len(extent) - 1 - position))
    return gain


def bell_draw(key, extent, scale, limit, pieces=(), held_as=jnp.bfloat16):
    values = jax.random.normal(key, extent, jnp.float32) * scale
    if len(pieces) > 0:
        values = block_levels(key, extent, pieces, -0.22, 0.18) * values
    return jnp.clip(values, min=-limit, max=limit).astype(held_as)


def setup_inputs(seed: int = 0, part: int = 0) -> dict:
    key_of = jax.random.split(jax.random.key(seed), 14)
    part_splits = jax.random.split(jax.random.fold_in(key_of[13], part), 14)
    residual = draw_residual(jax.random.fold_in(jax.random.fold_in(key_of[13], part), 71), part)
    direction = draw_direction(jax.random.fold_in(jax.random.fold_in(key_of[13], part), 71), part)
    step = jnp.clip(jnp.exp(math.log(0.8) - 1.3862944 * jax.random.uniform(part_splits[2], (SAMPLES,), jnp.float32) ** block_levels(part_splits[2], (SAMPLES,), ((0, 2),), -0.2, 0.2)), 0.2, 0.8)
    coords = jnp.clip(1.0 * jax.random.uniform(part_splits[3], (NLEAF, 3, LEAF_PTS), jnp.float32) ** block_levels(part_splits[3], (NLEAF, 3, LEAF_PTS), ((0, 8),), -0.2, 0.2), 0.0, 1.0).astype(jnp.bfloat16)
    order = jax.vmap(lambda own: jax.random.permutation(own, LEAF_PTS))(jax.random.split(part_splits[4], NLEAF)).reshape((NLEAF, LEAF_PTS)).astype(jnp.int32)
    basis = bell_draw(part_splits[5], (NLEAF, RANK, LEAF_PTS), (2 * RANK) ** -0.5, 0.5, ((0, 8),))
    leaf_transfer = bell_draw(part_splits[6], (NLEAF, RANK, RANK), RANK ** -0.5, 0.75, ((0, 8),))
    node_transfer = bell_draw(part_splits[7], (NODES, RANK, RANK), RANK ** -0.5, 0.75, ((0, 8),))
    near_list = draw_near_list(jax.random.fold_in(jax.random.fold_in(key_of[13], part), 71), part)
    coupling_list = draw_coupling_list(jax.random.fold_in(jax.random.fold_in(key_of[13], part), 71), part)
    coupling = bell_draw(part_splits[10], (NLEAF, NCPL, RANK, RANK), (RANK * NCPL) ** -0.5, 0.25, ((0, 8),))
    top_list = draw_top_list(jax.random.fold_in(jax.random.fold_in(key_of[13], part), 71), part)
    top_coupling = bell_draw(part_splits[12], (CLUSTERS, NTOP, RANK, RANK), (RANK * NTOP * LEAF_DEV * SUBTREES) ** -0.5, 0.0625, ((0, 4),))
    return dict(residual=residual, direction=direction, step=step, coords=coords, order=order, basis=basis, leaf_transfer=leaf_transfer, node_transfer=node_transfer, near_list=near_list, coupling_list=coupling_list, coupling=coupling, top_list=top_list, top_coupling=top_coupling)


ROOT_THREE = math.sqrt(3.0)
LENGTH = 0.3
AMPLITUDE = 0.25
NUGGET = 0.5

def matern(own_offsets, near_offsets, gap_leaves, spread):
    gap_x = own_offsets[0][:, None] - near_offsets[0][None, :] + gap_leaves.astype(jnp.float32) * spread
    gap_y = own_offsets[1][:, None] - near_offsets[1][None, :]
    gap_z = own_offsets[2][:, None] - near_offsets[2][None, :]
    scaled = jnp.sqrt(gap_x * gap_x + gap_y * gap_y + gap_z * gap_z) * (ROOT_THREE / LENGTH)
    return AMPLITUDE * (1.0 + scaled) * jnp.exp(-scaled)

def tile_block(own_offsets, near_offsets, gap_leaves, spread):
    inner = jax.vmap(matern, in_axes=(None, 0, 0, None))
    return jax.vmap(inner, in_axes=(0, 0, 0, None))(own_offsets, near_offsets, gap_leaves, spread)

def reference(residual, direction, step, coords, order, basis, leaf_transfer, node_transfer, near_list, coupling_list, coupling, top_list, top_coupling):
    spread = 0.5 / LEAF_DEV
    offsets_all = coords.astype(jnp.float32)
    inverse = jnp.argsort(order, axis=1).astype(jnp.int32)
    natural_values = jnp.take_along_axis(basis, inverse[:, None, :], axis=2)
    expansion_weights = jnp.einsum('grp,gsp->gsr', natural_values.astype(jnp.float32), direction.astype(jnp.float32)).astype(jnp.bfloat16)
    grouped = expansion_weights.astype(jnp.float32).reshape(NODES, LEAF_DEV, SAMPLES, RANK)
    transfers = leaf_transfer.astype(jnp.float32).reshape(NODES, LEAF_DEV, RANK, RANK)
    node_coef = jnp.einsum('nlrk,nlsk->nsr', transfers, grouped).astype(jnp.bfloat16)
    lifted = jnp.einsum('nrk,nsk->nsr', node_transfer.astype(jnp.float32), node_coef.astype(jnp.float32))
    top_node = lax.optimization_barrier(jnp.sum(lifted.reshape(CLUSTERS, SUBTREES, SAMPLES, RANK), axis=1)).astype(jnp.bfloat16)
    chosen = top_node[top_list]
    incoming = jnp.einsum('bkrj,bksj->bsr', top_coupling.astype(jnp.float32), chosen.astype(jnp.float32)).astype(jnp.bfloat16)
    spread_in = jnp.repeat(incoming, SUBTREES, axis=0)
    down_coef = jnp.einsum('nrk,nsr->nsk', node_transfer.astype(jnp.float32), spread_in.astype(jnp.float32)).astype(jnp.bfloat16)

    def per_node(node_index):
        first_leaf = node_index * LEAF_DEV
        leaf_ids = first_leaf + jnp.arange(LEAF_DEV, dtype=jnp.int32)
        near_ids = lax.dynamic_slice_in_dim(near_list, first_leaf, LEAF_DEV, 0)
        pairing_index = lax.dynamic_slice_in_dim(coupling_list, first_leaf, LEAF_DEV, 0)
        own_offsets = lax.dynamic_slice_in_dim(offsets_all, first_leaf, LEAF_DEV, 0)
        gap_leaves = jnp.mod(leaf_ids[:, None] - near_ids + NLEAF // 2, NLEAF) - NLEAF // 2
        kernel_tiles = tile_block(own_offsets, offsets_all[near_ids], gap_leaves, spread).astype(jnp.bfloat16)
        near_part = jnp.einsum('lkab,lksb->lsa', kernel_tiles.astype(jnp.float32), direction[near_ids].astype(jnp.float32))
        block_transfer = lax.dynamic_slice_in_dim(leaf_transfer, first_leaf, LEAF_DEV, 0).astype(jnp.float32)
        down_here = lax.dynamic_index_in_dim(down_coef, node_index, 0, keepdims=False).astype(jnp.float32)
        upward_gathered = jnp.einsum('lrk,sr->lsk', block_transfer, down_here)
        coupling_block_matrix = lax.dynamic_slice_in_dim(coupling, first_leaf, LEAF_DEV, 0).astype(jnp.float32)
        upward_gathered = upward_gathered + jnp.einsum('ohvd,ohgd->ogv', coupling_block_matrix, expansion_weights[pairing_index].astype(jnp.float32))
        upward_gathered = upward_gathered.astype(jnp.bfloat16)
        natural_block_values = lax.dynamic_slice_in_dim(natural_values, first_leaf, LEAF_DEV, 0).astype(jnp.float32)
        distant_part = jnp.einsum('bfw,baf->baw', natural_block_values, upward_gathered.astype(jnp.float32))
        own_direction = lax.dynamic_slice_in_dim(direction, first_leaf, LEAF_DEV, 0).astype(jnp.float32)
        return NUGGET * own_direction + near_part + distant_part
    product_image = lax.map(per_node, jnp.arange(NODES, dtype=jnp.int32)).reshape(NLEAF, SAMPLES, LEAF_PTS)
    residual_next = residual - step[None, :, None] * product_image
    old_sq = lax.optimization_barrier(jnp.sum(residual * residual, axis=(0, 2)))
    new_sq = lax.optimization_barrier(jnp.sum(residual_next * residual_next, axis=(0, 2)))
    direction_next = (residual_next + (new_sq / old_sq)[None, :, None] * direction.astype(jnp.float32)).astype(jnp.bfloat16)
    return (residual_next, direction_next)
```

```python
import functools
import math

import jax
import jax.numpy as jnp
from jax import lax
from jax.experimental import pallas as pl
from jax.experimental.pallas import tpu as pltpu
from jax.sharding import PartitionSpec as P

LEAF_DEV = 16

ROOT_THREE = math.sqrt(3.0)
LENGTH = 0.3
AMPLITUDE = 0.25
NUGGET = 0.5
SPREAD = 0.5 / LEAF_DEV
KAPPA = (ROOT_THREE / LENGTH) ** 2
LOG2E = 1.4426950408889634

RING = ("blk", "leaf")
BF = jnp.bfloat16
F32 = jnp.float32
MIB = 1 << 20


def shifted(array, axis, by):
    if isinstance(axis, tuple):
        count = math.prod(lax.axis_size(name) for name in axis)
    else:
        count = lax.axis_size(axis)
    return lax.ppermute(array, axis, [(i, (i + by) % count) for i in range(count)])


def partner(array):
    return lax.ppermute(array, "sample", [(0, 1), (1, 0)])


def thirds(value):
    high = value.astype(BF).astype(F32)
    rest = value - high
    middle = rest.astype(BF).astype(F32)
    return high, middle, rest - middle


def nt(left, right):
    return lax.dot_general(left, right, (((1,), (1,)), ((), ())), preferred_element_type=F32)


def nn(left, right):
    return jnp.dot(left, right, preferred_element_type=F32)


def call(kernel, outs, flops, moved, vmem=40, **kwargs):
    return pl.pallas_call(
        kernel,
        out_shape=outs,
        compiler_params=pltpu.CompilerParams(vmem_limit_bytes=vmem * MIB),
        cost_estimate=pl.CostEstimate(flops=flops, bytes_accessed=moved, transcendentals=0),
        **kwargs,
    )


def up_kernel(order, basis, direction, leaf_transfer, node_transfer, natural, coef, lifted):
    leaves, rank, points = basis.shape
    samples = direction.shape[1]
    rows = lax.broadcasted_iota(jnp.int32, (points, points), 0)
    node = jnp.zeros((samples, rank), F32)
    for g in range(leaves):
        place = jnp.where(rows == order[g : g + 1, :], 1.0, 0.0).astype(BF)
        own = nt(basis[g], place).astype(BF)
        natural[g] = own
        weights = nt(direction[g], own).astype(BF)
        coef[g] = weights
        node = node + nt(weights, leaf_transfer[g])
    lifted[...] = nt(node.astype(BF), node_transfer[0])


def features(offsets):
    x, y, z = (offsets[i : i + 1, :] for i in range(3))
    square = thirds(KAPPA * (x * x + y * y + z * z))
    row = lax.broadcasted_iota(jnp.int32, (8, x.shape[1]), 0)
    packed = jnp.zeros((8, x.shape[1]), F32)
    for i, value in enumerate((x, y, z, jnp.ones_like(x)) + square):
        packed = jnp.where(row == i, value, packed)
    return packed.astype(BF)


def tile_kernel(near, prev, own, after, tiles, spread_x):
    half = tiles.shape[0] * pl.num_programs(0)
    entries = near.shape[1]
    points = own.shape[2]
    leaves = own.shape[0]
    total = leaves * lax.axis_size("blk") * lax.axis_size("leaf")
    device = lax.axis_index("blk") * lax.axis_size("leaf") + lax.axis_index("leaf")
    anchor = (device - 1) * leaves

    @pl.when(pl.program_id(0) == 0)
    def _():
        lane = lax.broadcasted_iota(jnp.int32, (8, 128), 1)
        source = jnp.where(
            lane < 9,
            lane // 3,
            jnp.where(lane < 12, lane - 5, jnp.where(lane < 16, 7, jnp.where(lane < 64, 3, 0))),
        )
        source = jnp.where(lane < 112, source, 7)
        row = lax.broadcasted_iota(jnp.int32, (8, 128), 0)
        pick = jnp.where((row == source) & (row < 7), 1.0, 0.0).astype(BF)
        for side, ref in enumerate((prev, own, after)):
            for j in range(leaves):
                feats = features(ref[j].astype(F32))
                spread_x[side * leaves + j] = lax.dot_general(
                    feats, pick, (((0,), (0,)), ((), ())), preferred_element_type=F32
                ).astype(BF)

    g = lax.axis_index("sample") * half + pl.program_id(0)
    offsets = own[g].astype(F32)
    x, y, z = (offsets[i : i + 1, :] for i in range(3))
    row = lax.broadcasted_iota(jnp.int32, (16, points), 0)
    first = jnp.where((row >= 9) & (row < 12), 1.0, jnp.zeros((16, points), F32))
    at = 0
    for value in (x, y, z):
        for part in thirds(value * (-2.0 * KAPPA)):
            first = jnp.where(row == at, part, first)
            at += 1
    slots = []
    gap = jnp.zeros((16, points), F32)
    for e in range(entries):
        slot = lax.rem(near[g, e] - anchor + 2 * total, total)
        slots.append(slot)
        gap = jnp.where(row == e, (leaves + g - slot).astype(F32) * SPREAD, gap)
    moved = x + gap
    fixed = thirds(KAPPA * (moved * moved + y * y + z * z))
    gaps = thirds(gap * (-2.0 * KAPPA))
    weights = jnp.concatenate(
        [part.astype(BF) for part in (first,) + fixed + gaps + (jnp.zeros((16, points), F32),)],
        axis=0,
    )
    lane = lax.broadcasted_iota(jnp.int32, (1, 128), 1)
    for e in range(entries):
        keep = jnp.where((lane < 16) | (lane % 16 == e), 1.0, 0.0).astype(BF)
        square = jnp.maximum(nn(spread_x[slots[e]] * keep, weights), 1e-30)
        scaled = square * lax.rsqrt(square)
        value = (1.0 + scaled) * jnp.exp2(scaled * (-LOG2E))
        tiles[0, e * points : (e + 1) * points, :] = value.astype(BF)


def down_kernel(
    top_list,
    coupling_list,
    tops,
    top_coupling,
    node_transfer,
    leaf_transfer,
    before,
    after,
    coupling,
    natural,
    direction,
    base,
    window,
):
    leaves, samples, points = direction.shape
    rank = natural.shape[1]
    clusters = lax.axis_size("blk")
    here = lax.axis_index("blk")
    total = leaves * clusters * lax.axis_size("leaf")
    anchor = (here * lax.axis_size("leaf") + lax.axis_index("leaf") - 1) * leaves
    window[:leaves] = before[...]
    window[leaves:] = after[...]
    incoming = jnp.zeros((samples, rank), F32)
    for e in range(top_list.shape[1]):
        place = lax.rem(here - top_list[0, e] + clusters, clusters)
        incoming = incoming + nt(tops[place], top_coupling[0, e])
    down = nn(incoming.astype(BF), node_transfer[0]).astype(BF)
    for g in range(leaves):
        inward = nn(down, leaf_transfer[g])
        for c in range(coupling_list.shape[1]):
            slot = lax.rem(coupling_list[g, c] - anchor + 2 * total, total)
            slot = jnp.where(slot >= 2 * leaves, slot - leaves, slot)
            slot = jnp.minimum(slot, 2 * leaves - 1)
            inward = inward + nt(window[slot], coupling[g, c])
        far = nn(inward.astype(BF), natural[g])
        base[g] = NUGGET * direction[g].astype(F32) + far


def near_kernel(near, *refs):
    pieces, (tiles, kept, given, window, sems) = refs[:6], refs[6:]
    leaves = window.shape[0] // 3
    samples = kept.shape[1]
    points = kept.shape[2]
    total = leaves * lax.axis_size("blk") * lax.axis_size("leaf")
    device = lax.axis_index("blk") * lax.axis_size("leaf") + lax.axis_index("leaf")
    anchor = (device - 1) * leaves

    @pl.when(pl.program_id(0) == 0)
    def _():
        copies = []
        for i, piece in enumerate(pieces):
            side, columns = i // 2, i % 2
            copies.append(
                pltpu.make_async_copy(
                    piece,
                    window.at[
                        side * leaves : (side + 1) * leaves,
                        columns * samples : (columns + 1) * samples,
                    ],
                    sems.at[i],
                )
            )
        for copy in copies:
            copy.start()
        for copy in copies:
            copy.wait()

    g = lax.axis_index("sample") * pl.num_programs(0) + pl.program_id(0)
    values = []
    for e in range(near.shape[1]):
        values.append(window[lax.rem(near[g, e] - anchor + 2 * total, total)])
    field = nn(jnp.concatenate(values, axis=1), tiles[0]) * AMPLITUDE
    kept[0] = field[:samples]
    given[0] = field[samples:].astype(BF)


def residual_kernel(core, step, base, kept, received, residual, updated, norms):
    block = pl.program_id(0)
    mine = block // (pl.num_programs(0) // 2) == core[0]

    @pl.when(block == 0)
    def _():
        norms[...] = jnp.zeros_like(norms)

    def finish(near):
        old = residual[...]
        new = old - step[...][None] * (base[...] + near)
        updated[...] = new
        norms[0] += jnp.sum(jnp.sum(old * old, axis=0), axis=1, keepdims=True)
        norms[1] += jnp.sum(jnp.sum(new * new, axis=0), axis=1, keepdims=True)

    @pl.when(mine)
    def _():
        finish(kept[...])

    @pl.when(jnp.logical_not(mine))
    def _():
        finish(received[...].astype(F32))


def on_device(
    residual,
    direction,
    step,
    coords,
    order,
    basis,
    leaf_transfer,
    node_transfer,
    near_list,
    coupling_list,
    coupling,
    top_list,
    top_coupling,
):
    leaves, samples, points = direction.shape
    rank = basis.shape[1]
    entries = near_list.shape[1]
    half = leaves // 2
    blk_count = lax.axis_size("blk")
    leaf_count = lax.axis_size("leaf")
    shape = jax.ShapeDtypeStruct
    smem = pl.BlockSpec(memory_space=pltpu.SMEM)
    vmem = pl.BlockSpec(memory_space=pltpu.VMEM)
    anywhere = pl.BlockSpec(memory_space=pl.ANY)

    coords_prev = shifted(coords, RING, 1)
    coords_after = shifted(coords, RING, -1)
    direction_prev = shifted(direction, RING, 1)
    direction_after = shifted(direction, RING, -1)
    direction_other = partner(direction)

    natural, coef, lifted = call(
        up_kernel,
        (
            shape((leaves, rank, points), BF),
            shape((leaves, samples, rank), BF),
            shape((samples, rank), F32),
        ),
        4 * leaves * rank * points * points,
        6 * MIB,
        in_specs=[vmem] * 5,
        out_specs=(vmem,) * 3,
    )(order, basis, direction, leaf_transfer, node_transfer)

    coef_prev = shifted(coef, RING, 1)
    coef_after = shifted(coef, RING, -1)
    top = lifted
    for by in range(1, leaf_count):
        top = top + shifted(lifted, "leaf", by)
    top = top.astype(BF)
    if blk_count <= 8:
        tops = jnp.stack([top] + [shifted(top, "blk", by) for by in range(1, blk_count)])
    else:
        tops = lax.all_gather(top[None], "blk", axis=0, tiled=True)
        places = jnp.mod(lax.axis_index("blk") - jnp.arange(blk_count, dtype=jnp.int32), blk_count)
        tops = tops[places]

    tiles = call(
        tile_kernel,
        shape((half, entries * points, points), BF),
        40 * half * entries * points * points,
        half * entries * points * points * 2,
        grid=(half,),
        in_specs=[smem] + [vmem] * 3,
        out_specs=pl.BlockSpec((1, entries * points, points), lambda i: (i, 0, 0)),
        scratch_shapes=[pltpu.VMEM((3 * leaves, points, 128), BF)],
    )(near_list, coords_prev, coords, coords_after)

    base = call(
        down_kernel,
        shape((leaves, samples, points), F32),
        2 * leaves * samples * rank * (points + 9 * rank),
        8 * MIB,
        in_specs=[smem] * 2 + [vmem] * 9,
        out_specs=vmem,
        scratch_shapes=[pltpu.VMEM((2 * leaves, samples, rank), BF)],
    )(
        top_list,
        coupling_list,
        tops,
        top_coupling,
        node_transfer,
        leaf_transfer,
        coef_prev,
        coef_after,
        coupling,
        natural,
        direction,
    )

    own = pl.BlockSpec((1, samples, points), lambda i: (i, 0, 0))
    kept, given = call(
        near_kernel,
        (shape((half, samples, points), F32), shape((half, samples, points), BF)),
        4 * half * entries * samples * points * points,
        half * entries * points * points * 2,
        grid=(half,),
        in_specs=[smem]
        + [anywhere] * 6
        + [pl.BlockSpec((1, entries * points, points), lambda i: (i, 0, 0))],
        out_specs=(own, own),
        scratch_shapes=[
            pltpu.VMEM((3 * leaves, 2 * samples, points), BF),
            pltpu.SemaphoreType.DMA((6,)),
        ],
    )(
        near_list,
        direction_prev,
        partner(direction_prev),
        direction,
        direction_other,
        direction_after,
        partner(direction_after),
        tiles,
    )
    received = partner(given)

    side = lax.axis_index("sample").astype(jnp.int32).reshape(1)
    steps = 4
    chunk = leaves // steps
    slab = pl.BlockSpec((chunk, samples, points), lambda i, core: (i, 0, 0))
    per_side = steps // 2

    def of_side(flip):
        def index(i, core):
            owner = core[0] if not flip else 1 - core[0]
            return (jnp.clip(i - owner * per_side, 0, per_side - 1), 0, 0)

        return pl.BlockSpec((chunk, samples, points), index)

    residual_next, norms = pl.pallas_call(
        residual_kernel,
        out_shape=(shape((leaves, samples, points), F32), shape((2, samples, 1), F32)),
        grid_spec=pltpu.PrefetchScalarGridSpec(
            num_scalar_prefetch=1,
            grid=(steps,),
            in_specs=[
                pl.BlockSpec((samples, 1), lambda i, core: (0, 0)),
                slab,
                of_side(False),
                of_side(True),
                slab,
            ],
            out_specs=(slab, pl.BlockSpec((2, samples, 1), lambda i, core: (0, 0, 0))),
        ),
        cost_estimate=pl.CostEstimate(flops=4 * MIB, bytes_accessed=5 * MIB, transcendentals=0),
    )(side, step[:, None], base, kept, received, residual)

    devices = blk_count * leaf_count
    shared = jnp.broadcast_to(norms.reshape(1, 2, samples), (devices, 2, samples))
    sums = jnp.sum(lax.all_to_all(shared, RING, 0, 0), axis=0)
    ratio = sums[1] / sums[0]
    direction_next = (residual_next + ratio[None, :, None] * direction.astype(F32)).astype(BF)
    return (residual_next, direction_next)


def solution(mesh):
    in_specs = (
        P(("groups", "blk", "leaf"), "sample", None),
        P(("groups", "blk", "leaf"), "sample", None),
        P(("groups", "sample")),
        P(("groups", "blk", "leaf"), None, None),
        P(("groups", "blk", "leaf"), None),
        P(("groups", "blk", "leaf"), None, None),
        P(("groups", "blk", "leaf"), None, None),
        P(("groups", "blk", "leaf"), None, None),
        P(("groups", "blk", "leaf"), None),
        P(("groups", "blk", "leaf"), None),
        P(("groups", "blk", "leaf"), None, None, None),
        P(("groups", "blk"), None),
        P(("groups", "blk"), None, None, None),
    )
    out_specs = (
        P(("groups", "blk", "leaf"), "sample", None),
        P(("groups", "blk", "leaf"), "sample", None),
    )
    return jax.shard_map(
        on_device, mesh=mesh, in_specs=in_specs, out_specs=out_specs, check_vma=False
    )
```

```python
import functools
import math

import jax
import jax.numpy as jnp
from jax import lax
from jax.experimental import pallas as pl
from jax.experimental.pallas import tpu as pltpu
from jax.sharding import PartitionSpec as P

LEAF_DEV = 16

ROOT_THREE = math.sqrt(3.0)
LENGTH = 0.3
AMPLITUDE = 0.25
NUGGET = 0.5
SPREAD = 0.5 / LEAF_DEV
KAPPA = (ROOT_THREE / LENGTH) ** 2
LOG2E = 1.4426950408889634

RING = ("blk", "leaf")
BF = jnp.bfloat16
F32 = jnp.float32
MIB = 1 << 20


def shifted(array, axis, by):
    if isinstance(axis, tuple):
        count = math.prod(lax.axis_size(name) for name in axis)
    else:
        count = lax.axis_size(axis)
    return lax.ppermute(array, axis, [(i, (i + by) % count) for i in range(count)])


def partner(array):
    return lax.ppermute(array, "sample", [(0, 1), (1, 0)])


def ordered(array, *first):
    return lax.optimization_barrier((array,) + first)[0]


def column(row):
    size = row.shape[1]
    shape = (size, size)
    here = lax.broadcasted_iota(jnp.int32, shape, 0) == lax.broadcasted_iota(jnp.int32, shape, 1)
    return jnp.sum(jnp.where(here, row, 0.0), axis=1, keepdims=True)


def thirds(value):
    high = value.astype(BF).astype(F32)
    rest = value - high
    middle = rest.astype(BF).astype(F32)
    return high, middle, rest - middle


def nt(left, right):
    return lax.dot_general(left, right, (((1,), (1,)), ((), ())), preferred_element_type=F32)


def nn(left, right):
    return jnp.dot(left, right, preferred_element_type=F32)


def call(kernel, outs, flops, moved, vmem=40, **kwargs):
    return pl.pallas_call(
        kernel,
        out_shape=outs,
        compiler_params=pltpu.CompilerParams(vmem_limit_bytes=vmem * MIB),
        cost_estimate=pl.CostEstimate(flops=flops, bytes_accessed=moved, transcendentals=0),
        **kwargs,
    )


def up_kernel(order, basis, direction, leaf_transfer, node_transfer, natural, coef, lifted):
    leaves, rank, points = basis.shape
    samples = direction.shape[1]
    rows = lax.broadcasted_iota(jnp.int32, (points, points), 0)
    node = jnp.zeros((samples, rank), F32)
    for g in range(leaves):
        place = jnp.where(rows == order[g : g + 1, :], 1.0, 0.0).astype(BF)
        own = nt(basis[g], place).astype(BF)
        natural[g] = own
        weights = nt(direction[g], own).astype(BF)
        coef[g] = weights
        node = node + nt(weights, leaf_transfer[g])
    lifted[...] = nt(node.astype(BF), node_transfer[0])


def features(offsets):
    x, y, z = (offsets[i : i + 1, :] for i in range(3))
    square = thirds(KAPPA * (x * x + y * y + z * z))
    row = lax.broadcasted_iota(jnp.int32, (8, x.shape[1]), 0)
    packed = jnp.zeros((8, x.shape[1]), F32)
    for i, value in enumerate((x, y, z, jnp.ones_like(x)) + square):
        packed = jnp.where(row == i, value, packed)
    return packed.astype(BF)


def spread_features(offsets):
    lane = lax.broadcasted_iota(jnp.int32, (8, 128), 1)
    source = jnp.where(
        lane < 9,
        lane // 3,
        jnp.where(lane < 12, lane - 5, jnp.where(lane < 16, 7, jnp.where(lane < 64, 3, 0))),
    )
    source = jnp.where(lane < 112, source, 7)
    row = lax.broadcasted_iota(jnp.int32, (8, 128), 0)
    pick = jnp.where((row == source) & (row < 7), 1.0, 0.0).astype(BF)
    return lax.dot_general(
        features(offsets), pick, (((0,), (0,)), ((), ())), preferred_element_type=F32
    ).astype(BF)


def tile_kernel(start, near, prev, own, after, tiles, spread_x):
    count = tiles.shape[0]
    entries = near.shape[1]
    points = own.shape[2]
    leaves = own.shape[0]
    total = leaves * lax.axis_size("blk") * lax.axis_size("leaf")
    device = lax.axis_index("blk") * lax.axis_size("leaf") + lax.axis_index("leaf")
    anchor = (device - 1) * leaves
    for side, ref in enumerate((prev, own, after)):
        for j in range(leaves):
            spread_x[side * leaves + j] = spread_features(ref[j].astype(F32))
    row = lax.broadcasted_iota(jnp.int32, (16, points), 0)
    lane = lax.broadcasted_iota(jnp.int32, (1, 128), 1)

    def leaf(i, carry):
        g = lax.axis_index("sample") * (leaves // 2) + start + i
        offsets = own[g].astype(F32)
        x, y, z = (offsets[k : k + 1, :] for k in range(3))
        first = jnp.where((row >= 9) & (row < 12), 1.0, jnp.zeros((16, points), F32))
        at = 0
        for value in (x, y, z):
            for part in thirds(value * (-2.0 * KAPPA)):
                first = jnp.where(row == at, part, first)
                at += 1
        slots = []
        gap = jnp.zeros((16, points), F32)
        for e in range(entries):
            slot = lax.rem(near[g, e] - anchor + 2 * total, total)
            slots.append(slot)
            gap = jnp.where(row == e, (leaves + g - slot).astype(F32) * SPREAD, gap)
        moved = x + gap
        fixed = thirds(KAPPA * (moved * moved + y * y + z * z))
        gaps = thirds(gap * (-2.0 * KAPPA))
        weights = jnp.concatenate(
            [part.astype(BF) for part in (first,) + fixed + gaps + (jnp.zeros_like(first),)],
            axis=0,
        )
        for e in range(entries):
            keep = jnp.where((lane < 16) | (lane % 16 == e), 1.0, 0.0).astype(BF)
            square = jnp.maximum(nn(spread_x[slots[e]] * keep, weights), 1e-30)
            scaled = square * lax.rsqrt(square)
            value = (1.0 + scaled) * jnp.exp2(scaled * (-LOG2E))
            tiles[i, e * points : (e + 1) * points, :] = value.astype(BF)
        return carry

    lax.fori_loop(0, count, leaf, 0)


def down_kernel(
    top_list,
    coupling_list,
    tops,
    top_coupling,
    node_transfer,
    leaf_transfer,
    before,
    after,
    coupling,
    natural,
    direction,
    base,
    window,
):
    leaves, samples, points = direction.shape
    rank = natural.shape[1]
    clusters = lax.axis_size("blk")
    here = lax.axis_index("blk")
    total = leaves * clusters * lax.axis_size("leaf")
    anchor = (here * lax.axis_size("leaf") + lax.axis_index("leaf") - 1) * leaves
    window[:leaves] = before[...]
    window[leaves:] = after[...]
    incoming = jnp.zeros((samples, rank), F32)
    for e in range(top_list.shape[1]):
        place = lax.rem(here - top_list[0, e] + clusters, clusters)
        incoming = incoming + nt(tops[place], top_coupling[0, e])
    down = nn(incoming.astype(BF), node_transfer[0]).astype(BF)
    for g in range(leaves):
        inward = nn(down, leaf_transfer[g])
        for c in range(coupling_list.shape[1]):
            slot = lax.rem(coupling_list[g, c] - anchor + 2 * total, total)
            slot = jnp.where(slot >= 2 * leaves, slot - leaves, slot)
            slot = jnp.minimum(slot, 2 * leaves - 1)
            inward = inward + nt(window[slot], coupling[g, c])
        far = nn(inward.astype(BF), natural[g])
        base[g] = NUGGET * direction[g].astype(F32) + far


def near_kernel(near, *refs):
    pieces, tiles, (kept, given, window, sems) = refs[:6], refs[6:-4], refs[-4:]
    leaves = window.shape[0] // 3
    samples = kept.shape[1]
    total = leaves * lax.axis_size("blk") * lax.axis_size("leaf")
    device = lax.axis_index("blk") * lax.axis_size("leaf") + lax.axis_index("leaf")
    anchor = (device - 1) * leaves
    copies = []
    for i, piece in enumerate(pieces):
        side, columns = i // 2, i % 2
        copies.append(
            pltpu.make_async_copy(
                piece,
                window.at[
                    side * leaves : (side + 1) * leaves,
                    columns * samples : (columns + 1) * samples,
                ],
                sems.at[i],
            )
        )
    for copy in copies:
        copy.start()
    for copy in copies:
        copy.wait()
    at = 0
    for part in tiles:

        def leaf(i, carry, part=part, at=at):
            g = lax.axis_index("sample") * kept.shape[0] + at + i
            values = []
            for e in range(near.shape[1]):
                values.append(window[lax.rem(near[g, e] - anchor + 2 * total, total)])
            field = nn(jnp.concatenate(values, axis=1), part[i]) * AMPLITUDE
            kept[at + i] = field[:samples]
            given[at + i] = field[samples:].astype(BF)
            return carry

        lax.fori_loop(0, part.shape[0], leaf, 0)
        at += part.shape[0]


def residual_kernel(step, base, kept, received, residual, updated, norms):
    half = kept.shape[0]
    core = lax.axis_index("sample")
    steps = column(step[...])
    totals = [jnp.zeros((step.shape[1], 1), F32)] * 2
    for i in range(half):
        for theirs in range(2):
            g = (core ^ theirs) * half + i
            near = received[i].astype(F32) if theirs else kept[i]
            old = residual[g]
            new = old - steps * (base[g] + near)
            updated[g] = new
            for k, value in enumerate((old, new)):
                totals[k] = totals[k] + jnp.sum(value * value, axis=1, keepdims=True)
    samples = steps.shape[0]
    lane = lax.broadcasted_iota(jnp.int32, (samples, 128), 1)
    sub = lax.broadcasted_iota(jnp.int32, (samples, 128), 0)
    rows = [jnp.sum(jnp.where(lane == sub, part, 0.0), axis=0, keepdims=True) for part in totals]
    row = lax.broadcasted_iota(jnp.int32, norms.shape[1:], 0)
    packed = jnp.where(row == 0, rows[0], jnp.where(row == 1, rows[1], 0.0))
    for i in range(norms.shape[0]):
        norms[i] = packed


def direction_kernel(norms, updated, direction, result, held, sems):
    leaves, samples, points = updated.shape
    sums = norms[0]
    for i in range(1, norms.shape[0]):
        sums = sums + norms[i]
    ratio = column((sums[1:2, :] / sums[0:1, :])[:, :samples])
    chunks = sems.shape[0]
    size = leaves // chunks
    copies = []
    for c in range(chunks):
        for g in range(c * size, (c + 1) * size):
            held[g] = (updated[g] + ratio * direction[g].astype(F32)).astype(BF)
        part = pl.ds(c * size, size)
        copies.append(pltpu.make_async_copy(held.at[part], result.at[part], sems.at[c]))
        copies[-1].start()
    for copy in copies:
        copy.wait()


def on_device(
    residual,
    direction,
    step,
    coords,
    order,
    basis,
    leaf_transfer,
    node_transfer,
    near_list,
    coupling_list,
    coupling,
    top_list,
    top_coupling,
):
    leaves, samples, points = direction.shape
    rank = basis.shape[1]
    entries = near_list.shape[1]
    half = leaves // 2
    blk_count = lax.axis_size("blk")
    leaf_count = lax.axis_size("leaf")
    shape = jax.ShapeDtypeStruct
    smem = pl.BlockSpec(memory_space=pltpu.SMEM)
    vmem = pl.BlockSpec(memory_space=pltpu.VMEM)
    anywhere = pl.BlockSpec(memory_space=pl.ANY)

    coords_prev = shifted(coords, RING, 1)
    coords_after = shifted(coords, RING, -1)
    direction_prev = shifted(direction, RING, 1)
    direction_after = shifted(direction, RING, -1)
    direction_other = partner(direction)

    natural, coef, lifted = call(
        up_kernel,
        (
            shape((leaves, rank, points), BF),
            shape((leaves, samples, rank), BF),
            shape((samples, rank), F32),
        ),
        4 * leaves * rank * points * points,
        6 * MIB,
        in_specs=[vmem] * 5,
        out_specs=(vmem,) * 3,
    )(order, basis, direction, leaf_transfer, node_transfer)

    coef_prev = shifted(coef, RING, 1)
    coef_after = shifted(coef, RING, -1)
    top = lifted
    for by in range(1, leaf_count):
        top = top + shifted(lifted, "leaf", by)
    top = top.astype(BF)
    if blk_count <= 8:
        tops = jnp.stack([top] + [shifted(top, "blk", by) for by in range(1, blk_count)])
    else:
        tops = lax.all_gather(top[None], "blk", axis=0, tiled=True)
        places = jnp.mod(lax.axis_index("blk") - jnp.arange(blk_count, dtype=jnp.int32), blk_count)
        tops = tops[places]

    def make_tiles(start, near):
        count = half // 2
        return call(
            functools.partial(tile_kernel, start),
            shape((count, entries * points, points), BF),
            40 * count * entries * points * points,
            count * entries * points * points * 2,
            in_specs=[smem] + [vmem] * 3,
            out_specs=vmem,
            scratch_shapes=[pltpu.VMEM((3 * leaves, points, 128), BF)],
            vmem=16,
        )(near, coords_prev, coords, coords_after)

    tiles_low = make_tiles(0, ordered(near_list, natural))
    tiles_high = make_tiles(half // 2, ordered(near_list, tiles_low, top))

    base = call(
        down_kernel,
        shape((leaves, samples, points), F32),
        2 * leaves * samples * rank * (points + 9 * rank),
        8 * MIB,
        in_specs=[smem] * 2 + [vmem] * 9,
        out_specs=vmem,
        scratch_shapes=[pltpu.VMEM((2 * leaves, samples, rank), BF)],
        vmem=16,
    )(
        ordered(top_list, tiles_high),
        coupling_list,
        tops,
        top_coupling,
        node_transfer,
        leaf_transfer,
        coef_prev,
        coef_after,
        coupling,
        natural,
        direction,
    )

    direction_prev = ordered(direction_prev, base)
    direction_after = ordered(direction_after, base)
    kept, given = call(
        near_kernel,
        (shape((half, samples, points), F32), shape((half, samples, points), BF)),
        4 * half * entries * samples * points * points,
        half * entries * points * points * 2,
        in_specs=[smem] + [anywhere] * 6 + [vmem] * 2,
        out_specs=(vmem, vmem),
        scratch_shapes=[
            pltpu.VMEM((3 * leaves, 2 * samples, points), BF),
            pltpu.SemaphoreType.DMA((6,)),
        ],
        vmem=16,
    )(
        near_list,
        direction_prev,
        partner(direction_prev),
        direction,
        direction_other,
        direction_after,
        partner(direction_after),
        tiles_low,
        tiles_high,
    )
    received = partner(given)

    devices = blk_count * leaf_count
    residual_next, norms = call(
        residual_kernel,
        (shape((leaves, samples, points), F32), shape((devices, 8, 128), F32)),
        4 * MIB,
        5 * MIB,
        in_specs=[vmem] * 5,
        out_specs=(vmem, vmem),
        vmem=16,
    )(step[None, :], base, kept, received, residual)
    norms = lax.all_to_all(norms, RING, 0, 0)
    direction_next = call(
        direction_kernel,
        shape((leaves, samples, points), BF),
        MIB,
        2 * MIB,
        in_specs=[vmem] * 3,
        out_specs=anywhere,
        scratch_shapes=[
            pltpu.VMEM((leaves, samples, points), BF),
            pltpu.SemaphoreType.DMA((4,)),
        ],
        vmem=16,
    )(norms, residual_next, direction)
    return (residual_next, direction_next)


def solution(mesh):
    in_specs = (
        P(("groups", "blk", "leaf"), "sample", None),
        P(("groups", "blk", "leaf"), "sample", None),
        P(("groups", "sample")),
        P(("groups", "blk", "leaf"), None, None),
        P(("groups", "blk", "leaf"), None),
        P(("groups", "blk", "leaf"), None, None),
        P(("groups", "blk", "leaf"), None, None),
        P(("groups", "blk", "leaf"), None, None),
        P(("groups", "blk", "leaf"), None),
        P(("groups", "blk", "leaf"), None),
        P(("groups", "blk", "leaf"), None, None, None),
        P(("groups", "blk"), None),
        P(("groups", "blk"), None, None, None),
    )
    out_specs = (
        P(("groups", "blk", "leaf"), "sample", None),
        P(("groups", "blk", "leaf"), "sample", None),
    )
    return jax.shard_map(
        on_device, mesh=mesh, in_specs=in_specs, out_specs=out_specs, check_vma=False
    )
```

```python
import functools
import math

import jax
import jax.numpy as jnp
from jax import lax
from jax.experimental import pallas as pl
from jax.experimental.pallas import tpu as pltpu
from jax.sharding import PartitionSpec as P

LEAF_DEV = 16

ROOT_THREE = math.sqrt(3.0)
LENGTH = 0.3
AMPLITUDE = 0.25
NUGGET = 0.5
SPREAD = 0.5 / LEAF_DEV
KAPPA = (ROOT_THREE / LENGTH) ** 2
LOG2E = 1.4426950408889634

RING = ("blk", "leaf")
BF = jnp.bfloat16
F32 = jnp.float32
MIB = 1 << 20


def shifted(array, axis, by):
    if isinstance(axis, tuple):
        count = math.prod(lax.axis_size(name) for name in axis)
    else:
        count = lax.axis_size(axis)
    return lax.ppermute(array, axis, [(i, (i + by) % count) for i in range(count)])


def partner(array):
    return lax.ppermute(array, "sample", [(0, 1), (1, 0)])


def ordered(array, *first):
    return lax.optimization_barrier((array,) + first)[0]


def column(row):
    size = row.shape[1]
    shape = (size, size)
    here = lax.broadcasted_iota(jnp.int32, shape, 0) == lax.broadcasted_iota(jnp.int32, shape, 1)
    return jnp.sum(jnp.where(here, row, 0.0), axis=1, keepdims=True)


def in_hbm(*arrays):
    return [pltpu.with_memory_space_constraint(array, pltpu.HBM) for array in arrays]


def thirds(value):
    high = value.astype(BF).astype(F32)
    rest = value - high
    middle = rest.astype(BF).astype(F32)
    return high, middle, rest - middle


def nt(left, right):
    return lax.dot_general(left, right, (((1,), (1,)), ((), ())), preferred_element_type=F32)


def nn(left, right):
    return jnp.dot(left, right, preferred_element_type=F32)


def call(kernel, outs, flops, moved, vmem=40, **kwargs):
    return pl.pallas_call(
        kernel,
        out_shape=outs,
        compiler_params=pltpu.CompilerParams(vmem_limit_bytes=vmem * MIB),
        cost_estimate=pl.CostEstimate(flops=flops, bytes_accessed=moved, transcendentals=0),
        **kwargs,
    )


def up_kernel(order_h, basis_h, direction_h, transfer_h, node_h, natural_h, coef, lifted, mark, *scratch):
    mark[...] = jnp.zeros_like(mark)
    order, basis, direction, leaf_transfer, node_transfer, natural, sems = scratch
    leaves, rank, points = basis.shape
    samples = direction.shape[1]
    chunks = sems.shape[1]
    size = leaves // chunks
    whole = [
        pltpu.make_async_copy(order_h, order, sems.at[3, 0]),
        pltpu.make_async_copy(node_h, node_transfer, sems.at[3, 1]),
    ]
    copies = []
    for c in range(chunks):
        part = pl.ds(c * size, size)
        copies.append(
            [
                pltpu.make_async_copy(source.at[part], target.at[part], sems.at[i, c])
                for i, (source, target) in enumerate(
                    ((basis_h, basis), (direction_h, direction), (transfer_h, leaf_transfer))
                )
            ]
        )
    for copy in whole + sum(copies, []):
        copy.start()
    for copy in whole:
        copy.wait()
    rows = lax.broadcasted_iota(jnp.int32, (points, points), 0)
    node = jnp.zeros((samples, rank), F32)
    leaving = []
    for g in range(leaves):
        if g % size == 0:
            for copy in copies[g // size]:
                copy.wait()
        place = jnp.where(rows == order[g : g + 1, :], 1.0, 0.0).astype(BF)
        own = nt(basis[g], place).astype(BF)
        natural[g] = own
        weights = nt(direction[g], own).astype(BF)
        coef[g] = weights
        node = node + nt(weights, leaf_transfer[g])
        if g % size == size - 1:
            part = pl.ds(g + 1 - size, size)
            copy = pltpu.make_async_copy(
                natural.at[part], natural_h.at[part], sems.at[4, g // size]
            )
            copy.start()
            leaving.append(copy)
    lifted[...] = nt(node.astype(BF), node_transfer[0])
    for copy in leaving:
        copy.wait()


def features(offsets):
    x, y, z = (offsets[i : i + 1, :] for i in range(3))
    square = thirds(KAPPA * (x * x + y * y + z * z))
    row = lax.broadcasted_iota(jnp.int32, (8, x.shape[1]), 0)
    packed = jnp.zeros((8, x.shape[1]), F32)
    for i, value in enumerate((x, y, z, jnp.ones_like(x)) + square):
        packed = jnp.where(row == i, value, packed)
    return packed.astype(BF)


def spread_features(offsets):
    lane = lax.broadcasted_iota(jnp.int32, (8, 128), 1)
    source = jnp.where(
        lane < 9,
        lane // 3,
        jnp.where(lane < 12, lane - 5, jnp.where(lane < 16, 7, jnp.where(lane < 64, 3, 0))),
    )
    source = jnp.where(lane < 112, source, 7)
    row = lax.broadcasted_iota(jnp.int32, (8, 128), 0)
    pick = jnp.where((row == source) & (row < 7), 1.0, 0.0).astype(BF)
    return lax.dot_general(
        features(offsets), pick, (((0,), (0,)), ((), ())), preferred_element_type=F32
    ).astype(BF)


def tile_kernel(start, near_h, prev, own, after, tiles, mark, spread_x, near, sem):
    listed = pltpu.make_async_copy(near_h, near, sem)
    listed.start()
    mark[...] = jnp.zeros_like(mark)
    count = tiles.shape[0]
    entries = near.shape[1]
    points = own.shape[2]
    leaves = own.shape[0]
    total = leaves * lax.axis_size("blk") * lax.axis_size("leaf")
    device = lax.axis_index("blk") * lax.axis_size("leaf") + lax.axis_index("leaf")
    anchor = (device - 1) * leaves
    for side, ref in enumerate((prev, own, after)):
        for j in range(leaves):
            spread_x[side * leaves + j] = spread_features(ref[j].astype(F32))
    listed.wait()
    row = lax.broadcasted_iota(jnp.int32, (16, points), 0)
    lane = lax.broadcasted_iota(jnp.int32, (1, 128), 1)

    def leaf(i, carry):
        g = lax.axis_index("sample") * (leaves // 2) + start + i
        offsets = own[g].astype(F32)
        x, y, z = (offsets[k : k + 1, :] for k in range(3))
        first = jnp.where((row >= 9) & (row < 12), 1.0, jnp.zeros((16, points), F32))
        at = 0
        for value in (x, y, z):
            for part in thirds(value * (-2.0 * KAPPA)):
                first = jnp.where(row == at, part, first)
                at += 1
        slots = []
        gap = jnp.zeros((16, points), F32)
        for e in range(entries):
            slot = lax.rem(near[g, e] - anchor + 2 * total, total)
            slots.append(slot)
            gap = jnp.where(row == e, (leaves + g - slot).astype(F32) * SPREAD, gap)
        moved = x + gap
        fixed = thirds(KAPPA * (moved * moved + y * y + z * z))
        gaps = thirds(gap * (-2.0 * KAPPA))
        weights = jnp.concatenate(
            [part.astype(BF) for part in (first,) + fixed + gaps + (jnp.zeros_like(first),)],
            axis=0,
        )
        for e in range(entries):
            keep = jnp.where((lane < 16) | (lane % 16 == e), 1.0, 0.0).astype(BF)
            square = jnp.maximum(nn(spread_x[slots[e]] * keep, weights), 1e-30)
            scaled = square * lax.rsqrt(square)
            value = (1.0 + scaled) * jnp.exp2(scaled * (-LOG2E))
            tiles[i, e * points : (e + 1) * points, :] = value.astype(BF)
        return carry

    lax.fori_loop(0, count, leaf, 0)


def down_kernel(*refs):
    tops, before, after = refs[:3]
    sources, base, targets, sems = refs[3:11], refs[11], refs[12:21], refs[21]
    window, targets = targets[0], targets[1:]
    top_list, coupling_list, top_coupling, node_transfer = targets[:4]
    leaf_transfer, coupling, natural, direction = targets[4:]
    leaves, samples, points = direction.shape
    rank = natural.shape[1]
    clusters = lax.axis_size("blk")
    here = lax.axis_index("blk")
    total = leaves * clusters * lax.axis_size("leaf")
    anchor = (here * lax.axis_size("leaf") + lax.axis_index("leaf") - 1) * leaves
    pairs = [(before, window.at[:leaves]), (after, window.at[leaves:])]
    pairs += list(zip(sources[:4], targets[:4]))
    whole = [
        pltpu.make_async_copy(source, target, sems.at[0, i])
        for i, (source, target) in enumerate(pairs)
    ]
    chunks = 4
    size = leaves // chunks
    parts = []
    for c in range(chunks):
        part = pl.ds(c * size, size)
        parts.append(
            [
                pltpu.make_async_copy(source.at[part], target.at[part], sems.at[1 + c, i])
                for i, (source, target) in enumerate(zip(sources[4:], targets[4:]))
            ]
        )
    for copy in whole + sum(parts, []):
        copy.start()
    for copy in whole:
        copy.wait()
    incoming = jnp.zeros((samples, rank), F32)
    for e in range(top_list.shape[1]):
        place = lax.rem(here - top_list[0, e] + clusters, clusters)
        incoming = incoming + nt(tops[place], top_coupling[0, e])
    down = nn(incoming.astype(BF), node_transfer[0]).astype(BF)
    for g in range(leaves):
        if g % size == 0:
            for copy in parts[g // size]:
                copy.wait()
        inward = nn(down, leaf_transfer[g])
        for c in range(coupling_list.shape[1]):
            slot = lax.rem(coupling_list[g, c] - anchor + 2 * total, total)
            slot = jnp.where(slot >= 2 * leaves, slot - leaves, slot)
            slot = jnp.minimum(slot, 2 * leaves - 1)
            inward = inward + nt(window[slot], coupling[g, c])
        far = nn(inward.astype(BF), natural[g])
        base[g] = NUGGET * direction[g].astype(F32) + far


def near_kernel(near_h, *refs):
    pieces, tiles, (kept, given, mark, window, near, sems) = refs[:6], refs[6:-6], refs[-6:]
    mark[...] = jnp.zeros_like(mark)
    leaves = window.shape[0] // 3
    samples = kept.shape[1]
    total = leaves * lax.axis_size("blk") * lax.axis_size("leaf")
    device = lax.axis_index("blk") * lax.axis_size("leaf") + lax.axis_index("leaf")
    anchor = (device - 1) * leaves
    copies = [pltpu.make_async_copy(near_h, near, sems.at[6])]
    for i, piece in enumerate(pieces):
        side, columns = i // 2, i % 2
        copies.append(
            pltpu.make_async_copy(
                piece,
                window.at[
                    side * leaves : (side + 1) * leaves,
                    columns * samples : (columns + 1) * samples,
                ],
                sems.at[i],
            )
        )
    for copy in copies:
        copy.start()
    for copy in copies:
        copy.wait()
    at = 0
    for part in tiles:

        def leaf(i, carry, part=part, at=at):
            g = lax.axis_index("sample") * kept.shape[0] + at + i
            values = []
            for e in range(near.shape[1]):
                values.append(window[lax.rem(near[g, e] - anchor + 2 * total, total)])
            field = nn(jnp.concatenate(values, axis=1), part[i]) * AMPLITUDE
            kept[at + i] = field[:samples]
            given[at + i] = field[samples:].astype(BF)
            return carry

        lax.fori_loop(0, part.shape[0], leaf, 0)
        at += part.shape[0]


def residual_kernel(step, base, kept, received, residual_h, updated_h, updated, norms, *scratch):
    residual, sems = scratch
    half = kept.shape[0]
    chunks = sems.shape[1]
    size = half // chunks
    arrivals, leaving = [], []
    for c in range(chunks):
        for k in range(2):
            part = pl.ds(k * half + c * size, size)
            arrivals.append(
                pltpu.make_async_copy(residual_h.at[part], residual.at[part], sems.at[k, c])
            )
            leaving.append(
                pltpu.make_async_copy(updated.at[part], updated_h.at[part], sems.at[2 + k, c])
            )
    for copy in arrivals:
        copy.start()
    core = lax.axis_index("sample")
    steps = column(step[...])
    totals = [jnp.zeros((step.shape[1], 1), F32)] * 2
    for i in range(half):
        if i % size == 0:
            for k in range(2):
                arrivals[2 * (i // size) + k].wait()
        for theirs in range(2):
            g = (core ^ theirs) * half + i
            near = received[i].astype(F32) if theirs else kept[i]
            old = residual[g]
            new = old - steps * (base[g] + near)
            updated[g] = new
            for k, value in enumerate((old, new)):
                totals[k] = totals[k] + jnp.sum(value * value, axis=1, keepdims=True)
        if i % size == size - 1:
            for k in range(2):
                leaving[2 * (i // size) + k].start()
    samples = steps.shape[0]
    lane = lax.broadcasted_iota(jnp.int32, (samples, 128), 1)
    sub = lax.broadcasted_iota(jnp.int32, (samples, 128), 0)
    rows = [jnp.sum(jnp.where(lane == sub, part, 0.0), axis=0, keepdims=True) for part in totals]
    row = lax.broadcasted_iota(jnp.int32, norms.shape[1:], 0)
    packed = jnp.where(row == 0, rows[0], jnp.where(row == 1, rows[1], 0.0))
    for i in range(norms.shape[0]):
        norms[i] = packed
    for copy in leaving:
        copy.wait()


def direction_kernel(norms, updated, direction, result, held, sems):
    leaves, samples, points = updated.shape
    sums = norms[0]
    for i in range(1, norms.shape[0]):
        sums = sums + norms[i]
    ratio = column((sums[1:2, :] / sums[0:1, :])[:, :samples])
    chunks = sems.shape[0]
    size = leaves // chunks
    copies = []
    for c in range(chunks):
        for g in range(c * size, (c + 1) * size):
            held[g] = (updated[g] + ratio * direction[g].astype(F32)).astype(BF)
        part = pl.ds(c * size, size)
        copies.append(pltpu.make_async_copy(held.at[part], result.at[part], sems.at[c]))
        copies[-1].start()
    for copy in copies:
        copy.wait()


def on_device(
    residual,
    direction,
    step,
    coords,
    order,
    basis,
    leaf_transfer,
    node_transfer,
    near_list,
    coupling_list,
    coupling,
    top_list,
    top_coupling,
):
    leaves, samples, points = direction.shape
    rank = basis.shape[1]
    entries = near_list.shape[1]
    half = leaves // 2
    blk_count = lax.axis_size("blk")
    leaf_count = lax.axis_size("leaf")
    shape = jax.ShapeDtypeStruct
    token = shape((8, 128), F32)
    vmem = pl.BlockSpec(memory_space=pltpu.VMEM)
    anywhere = pl.BlockSpec(memory_space=pl.ANY)
    hbm = pl.BlockSpec(memory_space=pltpu.HBM)

    coords_prev = shifted(coords, RING, 1)
    coords_after = shifted(coords, RING, -1)
    travelling, first = lax.optimization_barrier((direction, order, coords_prev, coords_after))[:2]
    direction_prev = shifted(travelling, RING, 1)
    direction_after = shifted(travelling, RING, -1)
    direction_other = partner(direction)

    natural, coef, lifted, up_mark = call(
        up_kernel,
        (
            pltpu.HBM((leaves, rank, points), BF),
            shape((leaves, samples, rank), BF),
            shape((samples, rank), F32),
            token,
        ),
        4 * leaves * rank * points * points,
        6 * MIB,
        in_specs=[hbm] * 5,
        out_specs=(hbm, vmem, vmem, vmem),
        scratch_shapes=[
            pltpu.VMEM(order.shape, jnp.int32),
            pltpu.VMEM(basis.shape, BF),
            pltpu.VMEM(direction.shape, BF),
            pltpu.VMEM(leaf_transfer.shape, BF),
            pltpu.VMEM(node_transfer.shape, BF),
            pltpu.VMEM(basis.shape, BF),
            pltpu.SemaphoreType.DMA((5, 4)),
        ],
        vmem=8,
    )(*in_hbm(first, basis, direction, leaf_transfer, node_transfer))

    def make_tiles(start, near):
        count = half // 2
        return call(
            functools.partial(tile_kernel, start),
            (shape((count, entries * points, points), BF), token),
            40 * count * entries * points * points,
            count * entries * points * points * 2,
            in_specs=[hbm] + [vmem] * 3,
            out_specs=(vmem, vmem),
            scratch_shapes=[
                pltpu.VMEM((3 * leaves, points, 128), BF),
                pltpu.SMEM(near_list.shape, jnp.int32),
                pltpu.SemaphoreType.DMA,
            ],
            vmem=8,
        )(*in_hbm(near), coords_prev, coords, coords_after)

    coef_prev = shifted(coef, RING, 1)
    coef_after = shifted(coef, RING, -1)
    terms = [shifted(lifted, "leaf", by) for by in range(1, leaf_count)]
    tiles_low, low_mark = make_tiles(0, ordered(near_list, up_mark))
    top = ordered(lifted, low_mark)
    for term in terms:
        top = top + term
    top = top.astype(BF)
    tiles_high, high_mark = make_tiles(
        half // 2, ordered(near_list, low_mark, top, coef_prev, coef_after)
    )
    if blk_count <= 8:
        others = [shifted(top, "blk", by) for by in range(1, blk_count)]
    else:
        others = lax.all_gather(top[None], "blk", axis=0, tiled=True)
        places = jnp.mod(lax.axis_index("blk") - jnp.arange(blk_count, dtype=jnp.int32), blk_count)
        others = list(others[places][1:])
    direction_prev = ordered(direction_prev, high_mark, *others)
    direction_after = ordered(direction_after, high_mark, *others)
    kept, given, near_mark = call(
        near_kernel,
        (shape((half, samples, points), F32), shape((half, samples, points), BF), token),
        4 * half * entries * samples * points * points,
        half * entries * points * points * 2,
        in_specs=[hbm] + [anywhere] * 6 + [vmem] * 2,
        out_specs=(vmem,) * 3,
        scratch_shapes=[
            pltpu.VMEM((3 * leaves, 2 * samples, points), BF),
            pltpu.SMEM(near_list.shape, jnp.int32),
            pltpu.SemaphoreType.DMA((7,)),
        ],
        vmem=8,
    )(
        *in_hbm(near_list),
        direction_prev,
        partner(direction_prev),
        *in_hbm(direction),
        direction_other,
        direction_after,
        partner(direction_after),
        tiles_low,
        tiles_high,
    )
    tops = jnp.stack([top] + [ordered(other, near_mark) for other in others])
    arrays = (
        ordered(top_list, near_mark),
        coupling_list,
        top_coupling,
        node_transfer,
        leaf_transfer,
        coupling,
        natural,
        direction,
    )
    spaces = (pltpu.SMEM,) * 2 + (pltpu.VMEM,) * 6
    base = call(
        down_kernel,
        shape((leaves, samples, points), F32),
        2 * leaves * samples * rank * (points + 9 * rank),
        8 * MIB,
        in_specs=[vmem] + [hbm] * 10,
        out_specs=vmem,
        scratch_shapes=[pltpu.VMEM((2 * leaves, samples, rank), BF)]
        + [space(array.shape, array.dtype) for space, array in zip(spaces, arrays)]
        + [pltpu.SemaphoreType.DMA((5, 6))],
        vmem=10,
    )(tops, *in_hbm(coef_prev, coef_after, *arrays))
    received = partner(given)

    devices = blk_count * leaf_count
    whole = shape((leaves, samples, points), F32)
    residual_next, updated, norms = call(
        residual_kernel,
        (whole, whole, shape((devices, 8, 128), F32)),
        4 * MIB,
        5 * MIB,
        in_specs=[vmem] * 4 + [hbm],
        out_specs=(hbm, vmem, vmem),
        scratch_shapes=[
            pltpu.VMEM((leaves, samples, points), F32),
            pltpu.SemaphoreType.DMA((4, 2)),
        ],
        vmem=8,
    )(step[None, :], base, kept, received, *in_hbm(residual))
    norms = lax.all_to_all(norms, RING, 0, 0)
    direction_next = call(
        direction_kernel,
        shape((leaves, samples, points), BF),
        MIB,
        2 * MIB,
        in_specs=[vmem] * 3,
        out_specs=anywhere,
        scratch_shapes=[
            pltpu.VMEM((leaves, samples, points), BF),
            pltpu.SemaphoreType.DMA((4,)),
        ],
        vmem=8,
    )(norms, updated, direction)
    return (residual_next, direction_next)


def solution(mesh):
    in_specs = (
        P(("groups", "blk", "leaf"), "sample", None),
        P(("groups", "blk", "leaf"), "sample", None),
        P(("groups", "sample")),
        P(("groups", "blk", "leaf"), None, None),
        P(("groups", "blk", "leaf"), None),
        P(("groups", "blk", "leaf"), None, None),
        P(("groups", "blk", "leaf"), None, None),
        P(("groups", "blk", "leaf"), None, None),
        P(("groups", "blk", "leaf"), None),
        P(("groups", "blk", "leaf"), None),
        P(("groups", "blk", "leaf"), None, None, None),
        P(("groups", "blk"), None),
        P(("groups", "blk"), None, None, None),
    )
    out_specs = (
        P(("groups", "blk", "leaf"), "sample", None),
        P(("groups", "blk", "leaf"), "sample", None),
    )
    return jax.shard_map(
        on_device, mesh=mesh, in_specs=in_specs, out_specs=out_specs, check_vma=False
    )
```

```python
import functools
import math

import jax
import jax.numpy as jnp
from jax import lax
from jax.experimental import pallas as pl
from jax.experimental.pallas import tpu as pltpu
from jax.sharding import PartitionSpec as P

LEAF_DEV = 16

ROOT_THREE = math.sqrt(3.0)
LENGTH = 0.3
AMPLITUDE = 0.25
NUGGET = 0.5
SPREAD = 0.5 / LEAF_DEV
KAPPA = (ROOT_THREE / LENGTH) ** 2
LOG2E = 1.4426950408889634

RING = ("blk", "leaf")
BF = jnp.bfloat16
F32 = jnp.float32
MIB = 1 << 20


def shifted(array, axis, by):
    if isinstance(axis, tuple):
        count = math.prod(lax.axis_size(name) for name in axis)
    else:
        count = lax.axis_size(axis)
    return lax.ppermute(array, axis, [(i, (i + by) % count) for i in range(count)])


def partner(array):
    return lax.ppermute(array, "sample", [(0, 1), (1, 0)])


def ordered(array, *first):
    return lax.optimization_barrier((array,) + first)[0]


def column(row):
    size = row.shape[1]
    shape = (size, size)
    here = lax.broadcasted_iota(jnp.int32, shape, 0) == lax.broadcasted_iota(jnp.int32, shape, 1)
    return jnp.sum(jnp.where(here, row, 0.0), axis=1, keepdims=True)


def in_hbm(*arrays):
    return [pltpu.with_memory_space_constraint(array, pltpu.HBM) for array in arrays]


def thirds(value):
    high = value.astype(BF).astype(F32)
    rest = value - high
    middle = rest.astype(BF).astype(F32)
    return high, middle, rest - middle


def nt(left, right):
    return lax.dot_general(left, right, (((1,), (1,)), ((), ())), preferred_element_type=F32)


def nn(left, right):
    return jnp.dot(left, right, preferred_element_type=F32)


def call(kernel, outs, flops, moved, vmem=40, **kwargs):
    return pl.pallas_call(
        kernel,
        out_shape=outs,
        compiler_params=pltpu.CompilerParams(vmem_limit_bytes=vmem * MIB),
        cost_estimate=pl.CostEstimate(flops=flops, bytes_accessed=moved, transcendentals=0),
        **kwargs,
    )


def up_kernel(order_h, basis_h, direction_h, transfer_h, node_h, natural_h, coef, mark, *scratch):
    mark[...] = jnp.zeros_like(mark)
    order, basis, direction, leaf_transfer, node_transfer, natural, sems = scratch
    leaves, rank, points = basis.shape
    samples = direction.shape[1]
    chunks = sems.shape[1]
    size = leaves // chunks
    whole = [
        pltpu.make_async_copy(order_h, order, sems.at[3, 0]),
        pltpu.make_async_copy(node_h, node_transfer, sems.at[3, 1]),
    ]
    copies = []
    for c in range(chunks):
        part = pl.ds(c * size, size)
        copies.append(
            [
                pltpu.make_async_copy(source.at[part], target.at[part], sems.at[i, c])
                for i, (source, target) in enumerate(
                    ((basis_h, basis), (direction_h, direction), (transfer_h, leaf_transfer))
                )
            ]
        )
    for copy in whole + sum(copies, []):
        copy.start()
    for copy in whole:
        copy.wait()
    rows = lax.broadcasted_iota(jnp.int32, (points, points), 0)
    node = jnp.zeros((samples, rank), F32)
    leaving = []
    for g in range(leaves):
        if g % size == 0:
            for copy in copies[g // size]:
                copy.wait()
        place = jnp.where(rows == order[g : g + 1, :], 1.0, 0.0).astype(BF)
        own = nt(basis[g], place).astype(BF)
        natural[g] = own
        weights = nt(direction[g], own).astype(BF)
        coef[g // 2, :, (g % 2) * rank : (g % 2 + 1) * rank] = weights
        node = node + nt(weights, leaf_transfer[g])
        if g % size == size - 1:
            part = pl.ds(g + 1 - size, size)
            copy = pltpu.make_async_copy(
                natural.at[part], natural_h.at[part], sems.at[4, g // size]
            )
            copy.start()
            leaving.append(copy)
    for i, part in enumerate(thirds(nt(node.astype(BF), node_transfer[0]))):
        at = leaves + i
        coef[at // 2, :, (at % 2) * rank : (at % 2 + 1) * rank] = part.astype(BF)
    for copy in leaving:
        copy.wait()


def features(offsets):
    x, y, z = (offsets[i : i + 1, :] for i in range(3))
    square = thirds(KAPPA * (x * x + y * y + z * z))
    row = lax.broadcasted_iota(jnp.int32, (8, x.shape[1]), 0)
    packed = jnp.zeros((8, x.shape[1]), F32)
    for i, value in enumerate((x, y, z, jnp.ones_like(x)) + square):
        packed = jnp.where(row == i, value, packed)
    return packed.astype(BF)


def spread_features(offsets):
    lane = lax.broadcasted_iota(jnp.int32, (8, 128), 1)
    source = jnp.where(
        lane < 9,
        lane // 3,
        jnp.where(lane < 12, lane - 5, jnp.where(lane < 16, 7, jnp.where(lane < 64, 3, 0))),
    )
    source = jnp.where(lane < 112, source, 7)
    row = lax.broadcasted_iota(jnp.int32, (8, 128), 0)
    pick = jnp.where((row == source) & (row < 7), 1.0, 0.0).astype(BF)
    return lax.dot_general(
        features(offsets), pick, (((0,), (0,)), ((), ())), preferred_element_type=F32
    ).astype(BF)


def tile_kernel(start, near_h, _, own, *refs):
    if start == 0:
        prev, after, tiles, mark, spread_x, near, sem = refs
    else:
        spread_x, tiles, mark, near, sem = refs
    listed = pltpu.make_async_copy(near_h, near, sem)
    listed.start()
    mark[...] = jnp.zeros_like(mark)
    count = tiles.shape[0]
    entries = near.shape[1]
    points = own.shape[2]
    leaves = own.shape[0]
    total = leaves * lax.axis_size("blk") * lax.axis_size("leaf")
    device = lax.axis_index("blk") * lax.axis_size("leaf") + lax.axis_index("leaf")
    anchor = (device - 1) * leaves
    if start == 0:
        for side, ref in enumerate((prev, own, after)):
            for j in range(leaves):
                spread_x[side * leaves + j] = spread_features(ref[j].astype(F32))
    listed.wait()
    row = lax.broadcasted_iota(jnp.int32, (16, points), 0)
    lane = lax.broadcasted_iota(jnp.int32, (1, 128), 1)

    def leaf(i, carry):
        g = lax.axis_index("sample") * (leaves // 2) + start + i
        offsets = own[g].astype(F32)
        x, y, z = (offsets[k : k + 1, :] for k in range(3))
        first = jnp.where((row >= 9) & (row < 12), 1.0, jnp.zeros((16, points), F32))
        at = 0
        for value in (x, y, z):
            for part in thirds(value * (-2.0 * KAPPA)):
                first = jnp.where(row == at, part, first)
                at += 1
        slots = []
        gap = jnp.zeros((16, points), F32)
        for e in range(entries):
            slot = lax.rem(near[g, e] - anchor + 2 * total, total)
            slots.append(slot)
            gap = jnp.where(row == e, (leaves + g - slot).astype(F32) * SPREAD, gap)
        moved = x + gap
        fixed = thirds(KAPPA * (moved * moved + y * y + z * z))
        gaps = thirds(gap * (-2.0 * KAPPA))
        weights = jnp.concatenate(
            [part.astype(BF) for part in (first,) + fixed + gaps + (jnp.zeros_like(first),)],
            axis=0,
        )
        for e in range(entries):
            keep = jnp.where((lane < 16) | (lane % 16 == e), 1.0, 0.0).astype(BF)
            square = jnp.maximum(nn(spread_x[slots[e]] * keep, weights), 1e-30)
            scaled = square * lax.rsqrt(square)
            value = (1.0 + scaled) * jnp.exp2(scaled * (-LOG2E))
            tiles[i, e * points : (e + 1) * points, :] = value.astype(BF)
        return carry

    lax.fori_loop(0, count, leaf, 0)


def top_kernel(own, *refs):
    sides, top = refs[:-2], refs[-1]
    samples, rank = top.shape
    at = own.shape[0] - 2

    def term(ref):
        first, second = ref[at].astype(F32), ref[at + 1].astype(F32)
        return first[:, :rank] + first[:, rank:] + second[:, :rank]

    total = term(own)
    if sides:
        low = lax.axis_index("leaf") == 0
        total = total + jnp.where(low, term(sides[1]), term(sides[0]))
    top[...] = total.astype(top.dtype)


def down_kernel(*refs):
    tops, before, after, residual_h = refs[:4]
    sources, (base, residual), targets, sems = refs[4:12], refs[13:15], refs[15:24], refs[24]
    window, targets = targets[0], targets[1:]
    top_list, coupling_list, top_coupling, node_transfer = targets[:4]
    leaf_transfer, coupling, natural, direction = targets[4:]
    leaves, samples, points = direction.shape
    rank = natural.shape[1]
    clusters = lax.axis_size("blk")
    here = lax.axis_index("blk")
    total = leaves * clusters * lax.axis_size("leaf")
    anchor = (here * lax.axis_size("leaf") + lax.axis_index("leaf") - 1) * leaves
    pairs = list(zip(sources[:4], targets[:4]))
    whole = [
        pltpu.make_async_copy(source, target, sems.at[0, i])
        for i, (source, target) in enumerate(pairs)
    ]
    chunks = 4
    size = leaves // chunks
    parts = []
    for c in range(chunks):
        part = pl.ds(c * size, size)
        parts.append(
            [
                pltpu.make_async_copy(source.at[part], target.at[part], sems.at[1 + c, i])
                for i, (source, target) in enumerate(zip(sources[4:], targets[4:]))
            ]
        )
    ahead = pltpu.make_async_copy(residual_h, residual, sems.at[0, 6])
    for copy in whole + sum(parts, []) + [ahead]:
        copy.start()
    for side, packed in enumerate((before, after)):
        for g in range(leaves):
            part = packed[g // 2, :, (g % 2) * rank : (g % 2 + 1) * rank]
            window[side * leaves + g] = part
    for copy in whole:
        copy.wait()
    incoming = jnp.zeros((samples, rank), F32)
    for e in range(top_list.shape[1]):
        place = lax.rem(here - top_list[0, e] + clusters, clusters)
        incoming = incoming + nt(tops[place], top_coupling[0, e])
    down = nn(incoming.astype(BF), node_transfer[0]).astype(BF)
    for g in range(leaves):
        if g % size == 0:
            for copy in parts[g // size]:
                copy.wait()
        inward = nn(down, leaf_transfer[g])
        rows = []
        for c in range(coupling_list.shape[1]):
            slot = lax.rem(coupling_list[g, c] - anchor + 2 * total, total)
            slot = jnp.where(slot >= 2 * leaves, slot - leaves, slot)
            slot = jnp.minimum(slot, 2 * leaves - 1)
            rows.append(window[slot])
        columns = [coupling[g, c] for c in range(coupling_list.shape[1])]
        inward = inward + nt(jnp.concatenate(rows, axis=1), jnp.concatenate(columns, axis=1))
        far = nn(inward.astype(BF), natural[g])
        base[g] = NUGGET * direction[g].astype(F32) + far
    ahead.wait()


def near_kernel(near_h, *refs):
    pieces, tiles, (kept, given, mark, window, near, sems) = refs[:6], refs[6:8], refs[-6:]
    mark[...] = jnp.zeros_like(mark)
    leaves = window.shape[0] // 3
    samples = kept.shape[1]
    total = leaves * lax.axis_size("blk") * lax.axis_size("leaf")
    device = lax.axis_index("blk") * lax.axis_size("leaf") + lax.axis_index("leaf")
    anchor = (device - 1) * leaves
    copies = [pltpu.make_async_copy(near_h, near, sems.at[6])]
    for i, piece in enumerate(pieces):
        side, columns = i // 2, i % 2
        copies.append(
            pltpu.make_async_copy(
                piece,
                window.at[
                    side * leaves : (side + 1) * leaves,
                    columns * samples : (columns + 1) * samples,
                ],
                sems.at[i],
            )
        )
    for copy in copies:
        copy.start()
    for copy in copies:
        copy.wait()
    at = 0
    for part in tiles:

        def leaf(i, carry, part=part, at=at):
            g = lax.axis_index("sample") * kept.shape[0] + at + i
            values = []
            for e in range(near.shape[1]):
                values.append(window[lax.rem(near[g, e] - anchor + 2 * total, total)])
            field = nn(jnp.concatenate(values, axis=1), part[i]) * AMPLITUDE
            kept[at + i] = field[:samples]
            given[at + i] = field[samples:].astype(BF)
            return carry

        lax.fori_loop(0, part.shape[0], leaf, 0)
        at += part.shape[0]


def residual_kernel(step, base, kept, received, residual, updated_h, updated, norms, sems):
    half = kept.shape[0]
    chunks = sems.shape[1]
    size = half // chunks
    leaving = []
    for c in range(chunks):
        for k in range(2):
            part = pl.ds(k * half + c * size, size)
            leaving.append(
                pltpu.make_async_copy(updated.at[part], updated_h.at[part], sems.at[k, c])
            )
    core = lax.axis_index("sample")
    steps = column(step[...])
    totals = [jnp.zeros((step.shape[1], 1), F32)] * 2
    for i in range(half):
        for theirs in range(2):
            g = (core ^ theirs) * half + i
            near = received[i].astype(F32) if theirs else kept[i]
            old = residual[g]
            new = old - steps * (base[g] + near)
            updated[g] = new
            for k, value in enumerate((old, new)):
                totals[k] = totals[k] + jnp.sum(value * value, axis=1, keepdims=True)
        if i % size == size - 1:
            for k in range(2):
                leaving[2 * (i // size) + k].start()
    samples = steps.shape[0]
    lane = lax.broadcasted_iota(jnp.int32, (samples, 128), 1)
    sub = lax.broadcasted_iota(jnp.int32, (samples, 128), 0)
    rows = [jnp.sum(jnp.where(lane == sub, part, 0.0), axis=0, keepdims=True) for part in totals]
    row = lax.broadcasted_iota(jnp.int32, norms.shape[1:], 0)
    packed = jnp.where(row == 0, rows[0], jnp.where(row == 1, rows[1], 0.0))
    for i in range(norms.shape[0]):
        norms[i] = packed
    for copy in leaving:
        copy.wait()


def direction_kernel(norms, updated, direction, result, held, sems):
    leaves, samples, points = updated.shape
    sums = norms[0]
    for i in range(1, norms.shape[0]):
        sums = sums + norms[i]
    ratio = column((sums[1:2, :] / sums[0:1, :])[:, :samples])
    chunks = sems.shape[0]
    size = leaves // chunks
    copies = []
    for c in range(chunks):
        for g in range(c * size, (c + 1) * size):
            held[g] = (updated[g] + ratio * direction[g].astype(F32)).astype(BF)
        part = pl.ds(c * size, size)
        copies.append(pltpu.make_async_copy(held.at[part], result.at[part], sems.at[c]))
        copies[-1].start()
    for copy in copies:
        copy.wait()


def on_device(
    residual,
    direction,
    step,
    coords,
    order,
    basis,
    leaf_transfer,
    node_transfer,
    near_list,
    coupling_list,
    coupling,
    top_list,
    top_coupling,
):
    leaves, samples, points = direction.shape
    rank = basis.shape[1]
    entries = near_list.shape[1]
    half = leaves // 2
    blk_count = lax.axis_size("blk")
    leaf_count = lax.axis_size("leaf")
    shape = jax.ShapeDtypeStruct
    token = shape((8, 128), F32)
    vmem = pl.BlockSpec(memory_space=pltpu.VMEM)
    anywhere = pl.BlockSpec(memory_space=pl.ANY)
    hbm = pl.BlockSpec(memory_space=pltpu.HBM)

    coords_prev = shifted(coords, RING, 1)
    coords_after = shifted(coords, RING, -1)
    travelling, first = lax.optimization_barrier((direction, order, coords_prev, coords_after))[:2]
    direction_prev = shifted(travelling, RING, 1)
    direction_after = shifted(travelling, RING, -1)
    direction_other = partner(direction)

    natural, coef, up_mark = call(
        up_kernel,
        (
            pltpu.HBM((leaves, rank, points), BF),
            shape((leaves // 2 + 2, samples, 2 * rank), BF),
            token,
        ),
        4 * leaves * rank * points * points,
        6 * MIB,
        in_specs=[hbm] * 5,
        out_specs=(hbm, vmem, vmem),
        scratch_shapes=[
            pltpu.VMEM(order.shape, jnp.int32),
            pltpu.VMEM(basis.shape, BF),
            pltpu.VMEM(direction.shape, BF),
            pltpu.VMEM(leaf_transfer.shape, BF),
            pltpu.VMEM(node_transfer.shape, BF),
            pltpu.VMEM(basis.shape, BF),
            pltpu.SemaphoreType.DMA((5, 4)),
        ],
        vmem=8,
    )(*in_hbm(first, basis, direction, leaf_transfer, node_transfer))

    def make_tiles(start, done, *operands):
        count = half // 2
        outs = (pltpu.VMEM((count, entries * points, points), BF), token)
        if start == 0:
            outs += (shape((3 * leaves, points, 128), BF),)
        return call(
            functools.partial(tile_kernel, start),
            outs,
            40 * count * entries * points * points,
            count * entries * points * points * 2,
            in_specs=[hbm, anywhere] + [vmem] * len(operands),
            out_specs=(vmem,) * len(outs),
            scratch_shapes=[
                pltpu.SMEM(near_list.shape, jnp.int32),
                pltpu.SemaphoreType.DMA,
            ],
            vmem=8,
        )(*in_hbm(near_list), done, *operands)

    coef_prev = shifted(coef, RING, 1)
    coef_after = shifted(coef, RING, -1)
    tiles_low, low_mark, spread_x = make_tiles(
        0, up_mark, coords, coords_prev, coords_after
    )
    tiles_high, high_mark = make_tiles(half // 2, low_mark, coords, spread_x)
    direction_prev = ordered(direction_prev, high_mark)
    direction_after = ordered(direction_after, high_mark)
    kept, given, near_mark = call(
        near_kernel,
        (shape((half, samples, points), F32), shape((half, samples, points), BF), token),
        4 * half * entries * samples * points * points,
        half * entries * points * points * 2,
        in_specs=[hbm] + [anywhere] * 6 + [vmem] * 2,
        out_specs=(vmem,) * 3,
        scratch_shapes=[
            pltpu.VMEM((3 * leaves, 2 * samples, points), BF),
            pltpu.SMEM(near_list.shape, jnp.int32),
            pltpu.SemaphoreType.DMA((7,)),
        ],
        vmem=8,
    )(
        *in_hbm(near_list),
        direction_prev,
        partner(direction_prev),
        *in_hbm(direction),
        direction_other,
        direction_after,
        partner(direction_after),
        tiles_low,
        tiles_high,
    )

    paired = leaf_count == 2
    top = call(
        top_kernel,
        shape((samples, rank), BF if paired else F32),
        MIB,
        MIB,
        in_specs=[vmem] * (3 if paired else 1) + [anywhere],
        out_specs=vmem,
        vmem=4,
    )(coef, *((coef_prev, coef_after) if paired else ()), near_mark)
    if not paired:
        terms = [shifted(top, "leaf", by) for by in range(1, leaf_count)]
        top = sum(terms, top).astype(BF)
    if blk_count <= 8:
        others = [shifted(top, "blk", by) for by in range(1, blk_count)]
    else:
        others = lax.all_gather(top[None], "blk", axis=0, tiled=True)
        places = jnp.mod(lax.axis_index("blk") - jnp.arange(blk_count, dtype=jnp.int32), blk_count)
        others = list(others[places][1:])
    tops = jnp.stack([top] + others)
    arrays = (
        top_list,
        coupling_list,
        top_coupling,
        node_transfer,
        leaf_transfer,
        coupling,
        natural,
        direction,
    )
    spaces = (pltpu.SMEM,) * 2 + (pltpu.VMEM,) * 6
    whole = shape((leaves, samples, points), F32)
    base, residual_here = call(
        down_kernel,
        (whole, whole),
        2 * leaves * samples * rank * (points + 9 * rank),
        8 * MIB,
        in_specs=[vmem] * 3 + [hbm] * 9 + [anywhere],
        out_specs=(vmem, vmem),
        scratch_shapes=[pltpu.VMEM((2 * leaves, samples, rank), BF)]
        + [space(array.shape, array.dtype) for space, array in zip(spaces, arrays)]
        + [pltpu.SemaphoreType.DMA((5, 7))],
        vmem=10,
    )(tops, coef_prev, coef_after, *in_hbm(residual, *arrays), near_mark)
    received = partner(given)

    devices = blk_count * leaf_count
    residual_next, updated, norms = call(
        residual_kernel,
        (whole, whole, shape((devices, 8, 128), F32)),
        4 * MIB,
        5 * MIB,
        in_specs=[vmem] * 5,
        out_specs=(hbm, vmem, vmem),
        scratch_shapes=[pltpu.SemaphoreType.DMA((2, 4))],
        vmem=8,
    )(step[None, :], base, kept, received, residual_here)
    norms = lax.all_to_all(norms, RING, 0, 0)
    direction_next = call(
        direction_kernel,
        shape((leaves, samples, points), BF),
        MIB,
        2 * MIB,
        in_specs=[vmem] * 3,
        out_specs=anywhere,
        scratch_shapes=[
            pltpu.VMEM((leaves, samples, points), BF),
            pltpu.SemaphoreType.DMA((4,)),
        ],
        vmem=8,
    )(norms, updated, direction)
    return (residual_next, direction_next)


def solution(mesh):
    in_specs = (
        P(("groups", "blk", "leaf"), "sample", None),
        P(("groups", "blk", "leaf"), "sample", None),
        P(("groups", "sample")),
        P(("groups", "blk", "leaf"), None, None),
        P(("groups", "blk", "leaf"), None),
        P(("groups", "blk", "leaf"), None, None),
        P(("groups", "blk", "leaf"), None, None),
        P(("groups", "blk", "leaf"), None, None),
        P(("groups", "blk", "leaf"), None),
        P(("groups", "blk", "leaf"), None),
        P(("groups", "blk", "leaf"), None, None, None),
        P(("groups", "blk"), None),
        P(("groups", "blk"), None, None, None),
    )
    out_specs = (
        P(("groups", "blk", "leaf"), "sample", None),
        P(("groups", "blk", "leaf"), "sample", None),
    )
    return jax.shard_map(
        on_device, mesh=mesh, in_specs=in_specs, out_specs=out_specs, check_vma=False
    )
```

```python
import functools
import math

import jax
import jax.numpy as jnp
from jax import lax
from jax.experimental import pallas as pl
from jax.experimental.pallas import tpu as pltpu
from jax.sharding import PartitionSpec as P

LEAF_DEV = 16

ROOT_THREE = math.sqrt(3.0)
LENGTH = 0.3
AMPLITUDE = 0.25
NUGGET = 0.5
SPREAD = 0.5 / LEAF_DEV
KAPPA = (ROOT_THREE / LENGTH) ** 2
LOG2E = 1.4426950408889634

RING = ("blk", "leaf")
BF = jnp.bfloat16
F32 = jnp.float32
MIB = 1 << 20


def shifted(array, axis, by):
    if isinstance(axis, tuple):
        count = math.prod(lax.axis_size(name) for name in axis)
    else:
        count = lax.axis_size(axis)
    return lax.ppermute(array, axis, [(i, (i + by) % count) for i in range(count)])


def partner(array):
    return lax.ppermute(array, "sample", [(0, 1), (1, 0)])


def ordered(array, *first):
    return lax.optimization_barrier((array,) + first)[0]


def column(row):
    size = row.shape[1]
    shape = (size, size)
    here = lax.broadcasted_iota(jnp.int32, shape, 0) == lax.broadcasted_iota(jnp.int32, shape, 1)
    return jnp.sum(jnp.where(here, row, 0.0), axis=1, keepdims=True)


def in_hbm(*arrays):
    return [pltpu.with_memory_space_constraint(array, pltpu.HBM) for array in arrays]


def thirds(value):
    high = value.astype(BF).astype(F32)
    rest = value - high
    middle = rest.astype(BF).astype(F32)
    return high, middle, rest - middle


def nt(left, right):
    return lax.dot_general(left, right, (((1,), (1,)), ((), ())), preferred_element_type=F32)


def nn(left, right):
    return jnp.dot(left, right, preferred_element_type=F32)


def call(kernel, outs, flops, moved, vmem=40, **kwargs):
    return pl.pallas_call(
        kernel,
        out_shape=outs,
        compiler_params=pltpu.CompilerParams(vmem_limit_bytes=vmem * MIB),
        cost_estimate=pl.CostEstimate(flops=flops, bytes_accessed=moved, transcendentals=0),
        **kwargs,
    )


def up_kernel(order_h, basis_h, direction_h, transfer_h, node_h, natural_h, coef, mark, *scratch):
    mark[...] = jnp.zeros_like(mark)
    order, basis, direction, leaf_transfer, node_transfer, natural, sems = scratch
    leaves, rank, points = basis.shape
    samples = direction.shape[1]
    chunks = sems.shape[1]
    size = leaves // chunks
    whole = [
        pltpu.make_async_copy(order_h, order, sems.at[3, 0]),
        pltpu.make_async_copy(node_h, node_transfer, sems.at[3, 1]),
    ]
    copies = []
    for c in range(chunks):
        part = pl.ds(c * size, size)
        copies.append(
            [
                pltpu.make_async_copy(source.at[part], target.at[part], sems.at[i, c])
                for i, (source, target) in enumerate(
                    ((basis_h, basis), (direction_h, direction), (transfer_h, leaf_transfer))
                )
            ]
        )
    for copy in whole + sum(copies, []):
        copy.start()
    for copy in whole:
        copy.wait()
    rows = lax.broadcasted_iota(jnp.int32, (points, points), 0)
    node = jnp.zeros((samples, rank), F32)
    leaving = []
    for g in range(leaves):
        if g % size == 0:
            for copy in copies[g // size]:
                copy.wait()
        place = jnp.where(rows == order[g : g + 1, :], 1.0, 0.0).astype(BF)
        own = nt(basis[g], place).astype(BF)
        natural[g] = own
        weights = nt(direction[g], own).astype(BF)
        coef[g // 2, :, (g % 2) * rank : (g % 2 + 1) * rank] = weights
        node = node + nt(weights, leaf_transfer[g])
        if g % size == size - 1:
            part = pl.ds(g + 1 - size, size)
            copy = pltpu.make_async_copy(
                natural.at[part], natural_h.at[part], sems.at[4, g // size]
            )
            copy.start()
            leaving.append(copy)
    for i, part in enumerate(thirds(nt(node.astype(BF), node_transfer[0]))):
        at = leaves + i
        coef[at // 2, :, (at % 2) * rank : (at % 2 + 1) * rank] = part.astype(BF)
    for copy in leaving:
        copy.wait()


def features(offsets):
    x, y, z = (offsets[i : i + 1] for i in range(3))
    square = thirds(KAPPA * (x * x + y * y + z * z))
    row = lax.broadcasted_iota(jnp.int32, (8, x.shape[1]), 0)
    packed = jnp.zeros((8, x.shape[1]), F32)
    for i, value in enumerate((x, y, z, jnp.ones_like(x)) + square):
        packed = jnp.where(row == i, value, packed)
    return packed.astype(BF)


def spread_features(offsets):
    lane = lax.broadcasted_iota(jnp.int32, (8, 128), 1)
    source = jnp.where(
        lane < 9,
        lane // 3,
        jnp.where(lane < 12, lane - 5, jnp.where(lane < 16, 7, jnp.where(lane < 64, 3, 0))),
    )
    source = jnp.where(lane < 112, source, 7)
    row = lax.broadcasted_iota(jnp.int32, (8, 128), 0)
    pick = jnp.where((row == source) & (row < 7), 1.0, 0.0).astype(BF)
    return lax.dot_general(
        features(offsets), pick, (((0,), (0,)), ((), ())), preferred_element_type=F32
    ).astype(BF)


def tile_kernel(start, near_h, _, *refs):
    if start == 0:
        own, prev, after, tiles, mark, spread_x, plain, near, sem = refs
    else:
        plain, spread_x, tiles, mark, near, sem = refs
        own = plain
    listed = pltpu.make_async_copy(near_h, near, sem)
    listed.start()
    mark[...] = jnp.zeros_like(mark)
    count = tiles.shape[0]
    entries = near.shape[1]
    points = own.shape[2]
    leaves = own.shape[1]
    total = leaves * lax.axis_size("blk") * lax.axis_size("leaf")
    device = lax.axis_index("blk") * lax.axis_size("leaf") + lax.axis_index("leaf")
    anchor = (device - 1) * leaves
    if start == 0:
        for side, ref in enumerate((prev, own, after)):
            offsets = ref[...].astype(F32)
            for j in range(leaves):
                spread_x[side * leaves + j] = spread_features(offsets[:, j])
            if side == 1:
                plain[...] = offsets
    listed.wait()
    row = lax.broadcasted_iota(jnp.int32, (16, points), 0)
    lane = lax.broadcasted_iota(jnp.int32, (1, 128), 1)

    def leaf(i, carry):
        g = lax.axis_index("sample") * (leaves // 2) + start + i
        x, y, z = (plain[k, pl.ds(g, 1), :] for k in range(3))
        first = jnp.where((row >= 9) & (row < 12), 1.0, jnp.zeros((16, points), F32))
        at = 0
        for value in (x, y, z):
            for part in thirds(value * (-2.0 * KAPPA)):
                first = jnp.where(row == at, part, first)
                at += 1
        slots = []
        gap = jnp.zeros((16, points), F32)
        for e in range(entries):
            slot = lax.rem(near[g, e] - anchor + 2 * total, total)
            slots.append(slot)
            gap = jnp.where(row == e, (leaves + g - slot).astype(F32) * SPREAD, gap)
        moved = x + gap
        fixed = thirds(KAPPA * (moved * moved + y * y + z * z))
        gaps = thirds(gap * (-2.0 * KAPPA))
        weights = jnp.concatenate(
            [part.astype(BF) for part in (first,) + fixed + gaps + (jnp.zeros_like(first),)],
            axis=0,
        )
        for e in range(entries):
            keep = jnp.where((lane < 16) | (lane % 16 == e), 1.0, 0.0).astype(BF)
            square = jnp.maximum(nn(spread_x[slots[e]] * keep, weights), 1e-30)
            scaled = square * lax.rsqrt(square)
            value = (1.0 + scaled) * jnp.exp2(scaled * (-LOG2E))
            tiles[i, e * points : (e + 1) * points, :] = value.astype(BF)
        return carry

    lax.fori_loop(0, count, leaf, 0)


def top_kernel(own, *refs):
    sides, top = refs[:-2], refs[-1]
    samples, rank = top.shape
    at = own.shape[0] - 2

    def term(ref):
        first, second = ref[at].astype(F32), ref[at + 1].astype(F32)
        return first[:, :rank] + first[:, rank:] + second[:, :rank]

    total = term(own)
    if sides:
        low = lax.axis_index("leaf") == 0
        total = total + jnp.where(low, term(sides[1]), term(sides[0]))
    top[...] = total.astype(top.dtype)


def down_kernel(*refs):
    tops, before, after, residual_h = refs[:4]
    sources, (base, residual), targets, sems = refs[4:12], refs[13:15], refs[15:24], refs[24]
    window, targets = targets[0], targets[1:]
    top_list, coupling_list, top_coupling, node_transfer = targets[:4]
    leaf_transfer, coupling, natural, direction = targets[4:]
    leaves, samples, points = direction.shape
    rank = natural.shape[1]
    clusters = lax.axis_size("blk")
    here = lax.axis_index("blk")
    total = leaves * clusters * lax.axis_size("leaf")
    anchor = (here * lax.axis_size("leaf") + lax.axis_index("leaf") - 1) * leaves
    pairs = list(zip(sources[:4], targets[:4]))
    whole = [
        pltpu.make_async_copy(source, target, sems.at[0, i])
        for i, (source, target) in enumerate(pairs)
    ]
    chunks = 4
    size = leaves // chunks
    parts = []
    for c in range(chunks):
        part = pl.ds(c * size, size)
        parts.append(
            [
                pltpu.make_async_copy(source.at[part], target.at[part], sems.at[1 + c, i])
                for i, (source, target) in enumerate(zip(sources[4:], targets[4:]))
            ]
        )
    ahead = pltpu.make_async_copy(residual_h, residual, sems.at[0, 6])
    for copy in whole + sum(parts, []) + [ahead]:
        copy.start()
    for side, packed in enumerate((before, after)):
        for g in range(leaves):
            part = packed[g // 2, :, (g % 2) * rank : (g % 2 + 1) * rank]
            window[side * leaves + g] = part
    for copy in whole:
        copy.wait()
    incoming = jnp.zeros((samples, rank), F32)
    for e in range(top_list.shape[1]):
        place = lax.rem(here - top_list[0, e] + clusters, clusters)
        incoming = incoming + nt(tops[place], top_coupling[0, e])
    down = nn(incoming.astype(BF), node_transfer[0]).astype(BF)
    for g in range(leaves):
        if g % size == 0:
            for copy in parts[g // size]:
                copy.wait()
        inward = nn(down, leaf_transfer[g])
        rows = []
        for c in range(coupling_list.shape[0]):
            slot = lax.rem(coupling_list[c, g] - anchor + 2 * total, total)
            slot = jnp.where(slot >= 2 * leaves, slot - leaves, slot)
            slot = jnp.minimum(slot, 2 * leaves - 1)
            rows.append(window[slot])
        columns = [coupling[g, c] for c in range(coupling_list.shape[0])]
        inward = inward + nt(jnp.concatenate(rows, axis=1), jnp.concatenate(columns, axis=1))
        far = nn(inward.astype(BF), natural[g])
        base[g] = NUGGET * direction[g].astype(F32) + far
    ahead.wait()


def near_kernel(near_h, *refs):
    pieces, tiles, (kept, given, mark, window, near, sems) = refs[:6], refs[6:8], refs[-6:]
    mark[...] = jnp.zeros_like(mark)
    leaves = window.shape[0] // 3
    samples = kept.shape[1]
    total = leaves * lax.axis_size("blk") * lax.axis_size("leaf")
    device = lax.axis_index("blk") * lax.axis_size("leaf") + lax.axis_index("leaf")
    anchor = (device - 1) * leaves
    copies = [pltpu.make_async_copy(near_h, near, sems.at[6])]
    for i, piece in enumerate(pieces):
        side, columns = i // 2, i % 2
        copies.append(
            pltpu.make_async_copy(
                piece,
                window.at[
                    side * leaves : (side + 1) * leaves,
                    columns * samples : (columns + 1) * samples,
                ],
                sems.at[i],
            )
        )
    for copy in copies:
        copy.start()
    for copy in copies:
        copy.wait()
    at = 0
    for part in tiles:

        def leaf(i, carry, part=part, at=at):
            g = lax.axis_index("sample") * kept.shape[0] + at + i
            values = []
            for e in range(near.shape[1]):
                values.append(window[lax.rem(near[g, e] - anchor + 2 * total, total)])
            field = nn(jnp.concatenate(values, axis=1), part[i]) * AMPLITUDE
            kept[at + i] = field[:samples]
            given[at + i] = field[samples:].astype(BF)
            return carry

        lax.fori_loop(0, part.shape[0], leaf, 0)
        at += part.shape[0]


def residual_kernel(step, base, kept, received, residual, updated_h, updated, norms, sems):
    half = kept.shape[0]
    chunks = sems.shape[1]
    size = half // chunks
    leaving = []
    for c in range(chunks):
        for k in range(2):
            part = pl.ds(k * half + c * size, size)
            leaving.append(
                pltpu.make_async_copy(updated.at[part], updated_h.at[part], sems.at[k, c])
            )
    core = lax.axis_index("sample")
    steps = column(step[...])
    totals = [jnp.zeros((step.shape[1], 1), F32)] * 2
    for i in range(half):
        for theirs in range(2):
            g = (core ^ theirs) * half + i
            near = received[i].astype(F32) if theirs else kept[i]
            old = residual[g]
            new = old - steps * (base[g] + near)
            updated[g] = new
            for k, value in enumerate((old, new)):
                totals[k] = totals[k] + jnp.sum(value * value, axis=1, keepdims=True)
        if i % size == size - 1:
            for k in range(2):
                leaving[2 * (i // size) + k].start()
    samples = steps.shape[0]
    lane = lax.broadcasted_iota(jnp.int32, (samples, 128), 1)
    sub = lax.broadcasted_iota(jnp.int32, (samples, 128), 0)
    rows = [jnp.sum(jnp.where(lane == sub, part, 0.0), axis=0, keepdims=True) for part in totals]
    row = lax.broadcasted_iota(jnp.int32, norms.shape[1:], 0)
    packed = jnp.where(row == 0, rows[0], jnp.where(row == 1, rows[1], 0.0))
    for i in range(norms.shape[0]):
        norms[i] = packed
    for copy in leaving:
        copy.wait()


def direction_kernel(norms, updated, direction, result, held, sems):
    leaves, samples, points = updated.shape
    sums = norms[0]
    for i in range(1, norms.shape[0]):
        sums = sums + norms[i]
    ratio = column((sums[1:2, :] / sums[0:1, :])[:, :samples])
    chunks = sems.shape[0]
    size = leaves // chunks
    copies = []
    for c in range(chunks):
        for g in range(c * size, (c + 1) * size):
            held[g] = (updated[g] + ratio * direction[g].astype(F32)).astype(BF)
        part = pl.ds(c * size, size)
        copies.append(pltpu.make_async_copy(held.at[part], result.at[part], sems.at[c]))
        copies[-1].start()
    for copy in copies:
        copy.wait()


def on_device(
    residual,
    direction,
    step,
    coords,
    order,
    basis,
    leaf_transfer,
    node_transfer,
    near_list,
    coupling_list,
    coupling,
    top_list,
    top_coupling,
):
    leaves, samples, points = direction.shape
    rank = basis.shape[1]
    entries = near_list.shape[1]
    half = leaves // 2
    blk_count = lax.axis_size("blk")
    leaf_count = lax.axis_size("leaf")
    shape = jax.ShapeDtypeStruct
    token = shape((8, 128), F32)
    vmem = pl.BlockSpec(memory_space=pltpu.VMEM)
    anywhere = pl.BlockSpec(memory_space=pl.ANY)
    hbm = pl.BlockSpec(memory_space=pltpu.HBM)

    coords = jnp.transpose(coords, (1, 0, 2))
    coords_prev = shifted(coords, RING, 1)
    coords_after = shifted(coords, RING, -1)
    travelling, first = lax.optimization_barrier((direction, order, coords_prev, coords_after))[:2]
    direction_prev = shifted(travelling, RING, 1)
    direction_after = shifted(travelling, RING, -1)
    direction_other = partner(direction)

    natural, coef, up_mark = call(
        up_kernel,
        (
            pltpu.HBM((leaves, rank, points), BF),
            shape((leaves // 2 + 2, samples, 2 * rank), BF),
            token,
        ),
        4 * leaves * rank * points * points,
        6 * MIB,
        in_specs=[hbm] * 5,
        out_specs=(hbm, vmem, vmem),
        scratch_shapes=[
            pltpu.VMEM(order.shape, jnp.int32),
            pltpu.VMEM(basis.shape, BF),
            pltpu.VMEM(direction.shape, BF),
            pltpu.VMEM(leaf_transfer.shape, BF),
            pltpu.VMEM(node_transfer.shape, BF),
            pltpu.VMEM(basis.shape, BF),
            pltpu.SemaphoreType.DMA((5, 4)),
        ],
        vmem=8,
    )(*in_hbm(first, basis, direction, leaf_transfer, node_transfer))

    def make_tiles(start, done, *operands):
        count = half // 2
        outs = (pltpu.VMEM((count, entries * points, points), BF), token)
        if start == 0:
            outs += (shape((3 * leaves, points, 128), BF), shape(coords.shape, F32))
        return call(
            functools.partial(tile_kernel, start),
            outs,
            40 * count * entries * points * points,
            count * entries * points * points * 2,
            in_specs=[hbm, anywhere] + [vmem] * len(operands),
            out_specs=(vmem,) * len(outs),
            scratch_shapes=[
                pltpu.SMEM(near_list.shape, jnp.int32),
                pltpu.SemaphoreType.DMA,
            ],
            vmem=8,
        )(*in_hbm(near_list), done, *operands)

    coef_prev = shifted(coef, RING, 1)
    coef_after = shifted(coef, RING, -1)
    tiles_low, low_mark, spread_x, plain = make_tiles(
        0, up_mark, coords, coords_prev, coords_after
    )
    tiles_high, high_mark = make_tiles(half // 2, low_mark, plain, spread_x)
    direction_prev = ordered(direction_prev, high_mark, coef_prev, coef_after)
    direction_after = ordered(direction_after, high_mark, coef_prev, coef_after)
    paired = leaf_count == 2
    top = call(
        top_kernel,
        shape((samples, rank), BF if paired else F32),
        MIB,
        MIB,
        in_specs=[vmem] * (3 if paired else 1) + [anywhere],
        out_specs=vmem,
        vmem=4,
    )(coef, *((coef_prev, coef_after) if paired else ()), high_mark)
    if not paired:
        terms = [shifted(top, "leaf", by) for by in range(1, leaf_count)]
        top = sum(terms, top).astype(BF)
    if blk_count <= 8:
        others = [shifted(top, "blk", by) for by in range(1, blk_count)]
    else:
        others = lax.all_gather(top[None], "blk", axis=0, tiled=True)
        places = jnp.mod(lax.axis_index("blk") - jnp.arange(blk_count, dtype=jnp.int32), blk_count)
        others = list(others[places][1:])
    kept, given, near_mark = call(
        near_kernel,
        (shape((half, samples, points), F32), shape((half, samples, points), BF), token),
        4 * half * entries * samples * points * points,
        half * entries * points * points * 2,
        in_specs=[hbm] + [anywhere] * 6 + [vmem] * 2 + [anywhere] * len(others),
        out_specs=(vmem,) * 3,
        scratch_shapes=[
            pltpu.VMEM((3 * leaves, 2 * samples, points), BF),
            pltpu.SMEM(near_list.shape, jnp.int32),
            pltpu.SemaphoreType.DMA((7,)),
        ],
        vmem=8,
    )(
        *in_hbm(near_list),
        direction_prev,
        partner(direction_prev),
        *in_hbm(direction),
        direction_other,
        direction_after,
        partner(direction_after),
        tiles_low,
        tiles_high,
        *others,
    )

    tops = jnp.stack([top] + others)
    arrays = (
        top_list,
        coupling_list.T,
        top_coupling,
        node_transfer,
        leaf_transfer,
        coupling,
        natural,
        direction,
    )
    spaces = (pltpu.SMEM,) * 2 + (pltpu.VMEM,) * 6
    whole = shape((leaves, samples, points), F32)
    base, residual_here = call(
        down_kernel,
        (whole, whole),
        2 * leaves * samples * rank * (points + 9 * rank),
        8 * MIB,
        in_specs=[vmem] * 3 + [hbm] * 9 + [anywhere],
        out_specs=(vmem, vmem),
        scratch_shapes=[pltpu.VMEM((2 * leaves, samples, rank), BF)]
        + [space(array.shape, array.dtype) for space, array in zip(spaces, arrays)]
        + [pltpu.SemaphoreType.DMA((5, 7))],
        vmem=10,
    )(tops, coef_prev, coef_after, *in_hbm(residual, *arrays), near_mark)
    received = partner(given)

    devices = blk_count * leaf_count
    residual_next, updated, norms = call(
        residual_kernel,
        (whole, whole, shape((devices, 8, 128), F32)),
        4 * MIB,
        5 * MIB,
        in_specs=[vmem] * 5,
        out_specs=(hbm, vmem, vmem),
        scratch_shapes=[pltpu.SemaphoreType.DMA((2, 4))],
        vmem=8,
    )(step[None, :], base, kept, received, residual_here)
    norms = lax.all_to_all(norms, RING, 0, 0)
    direction_next = call(
        direction_kernel,
        shape((leaves, samples, points), BF),
        MIB,
        2 * MIB,
        in_specs=[vmem] * 3,
        out_specs=anywhere,
        scratch_shapes=[
            pltpu.VMEM((leaves, samples, points), BF),
            pltpu.SemaphoreType.DMA((4,)),
        ],
        vmem=8,
    )(norms, updated, direction)
    return (residual_next, direction_next)


def solution(mesh):
    in_specs = (
        P(("groups", "blk", "leaf"), "sample", None),
        P(("groups", "blk", "leaf"), "sample", None),
        P(("groups", "sample")),
        P(("groups", "blk", "leaf"), None, None),
        P(("groups", "blk", "leaf"), None),
        P(("groups", "blk", "leaf"), None, None),
        P(("groups", "blk", "leaf"), None, None),
        P(("groups", "blk", "leaf"), None, None),
        P(("groups", "blk", "leaf"), None),
        P(("groups", "blk", "leaf"), None),
        P(("groups", "blk", "leaf"), None, None, None),
        P(("groups", "blk"), None),
        P(("groups", "blk"), None, None, None),
    )
    out_specs = (
        P(("groups", "blk", "leaf"), "sample", None),
        P(("groups", "blk", "leaf"), "sample", None),
    )
    return jax.shard_map(
        on_device, mesh=mesh, in_specs=in_specs, out_specs=out_specs, check_vma=False
    )
```

```python
import functools
import math

import jax
import jax.numpy as jnp
from jax import lax
from jax.experimental import pallas as pl
from jax.experimental.pallas import tpu as pltpu
from jax.sharding import PartitionSpec as P

LEAF_DEV = 16

ROOT_THREE = math.sqrt(3.0)
LENGTH = 0.3
AMPLITUDE = 0.25
NUGGET = 0.5
SPREAD = 0.5 / LEAF_DEV
KAPPA = (ROOT_THREE / LENGTH) ** 2
LOG2E = 1.4426950408889634

RING = ("blk", "leaf")
BF = jnp.bfloat16
F32 = jnp.float32
MIB = 1 << 20


def shifted(array, axis, by):
    if isinstance(axis, tuple):
        count = math.prod(lax.axis_size(name) for name in axis)
    else:
        count = lax.axis_size(axis)
    return lax.ppermute(array, axis, [(i, (i + by) % count) for i in range(count)])


def partner(array):
    return lax.ppermute(array, "sample", [(0, 1), (1, 0)])


def passed_on(array):
    count = lax.axis_size("blk") * 2
    pairs = [(i, (i + 2 - 4 * (i % 2)) % count) for i in range(count)]
    return lax.ppermute(array, RING, pairs)


def place(slot, leaves, flip):
    if not flip:
        return slot
    moved = jnp.where(slot >= 2 * leaves, slot - 2 * leaves, slot)
    moved = jnp.where(slot < leaves, slot + 2 * leaves, moved)
    return jnp.where(lax.axis_index("leaf") == 0, moved, slot)


def ordered(array, *first):
    return lax.optimization_barrier((array,) + first)[0]


def column(row):
    size = row.shape[1]
    shape = (size, size)
    here = lax.broadcasted_iota(jnp.int32, shape, 0) == lax.broadcasted_iota(jnp.int32, shape, 1)
    return jnp.sum(jnp.where(here, row, 0.0), axis=1, keepdims=True)


def in_hbm(*arrays):
    return [pltpu.with_memory_space_constraint(array, pltpu.HBM) for array in arrays]


def thirds(value):
    high = value.astype(BF).astype(F32)
    rest = value - high
    middle = rest.astype(BF).astype(F32)
    return high, middle, rest - middle


def nt(left, right):
    return lax.dot_general(left, right, (((1,), (1,)), ((), ())), preferred_element_type=F32)


def nn(left, right):
    return jnp.dot(left, right, preferred_element_type=F32)


def call(kernel, outs, flops, moved, vmem=40, **kwargs):
    return pl.pallas_call(
        kernel,
        out_shape=outs,
        compiler_params=pltpu.CompilerParams(vmem_limit_bytes=vmem * MIB),
        cost_estimate=pl.CostEstimate(flops=flops, bytes_accessed=moved, transcendentals=0),
        **kwargs,
    )


def up_kernel(order_h, basis_h, direction_h, transfer_h, node_h, natural_h, coef, mark, *scratch):
    mark[...] = jnp.zeros_like(mark)
    order, basis, direction, leaf_transfer, node_transfer, natural, sems = scratch
    leaves, rank, points = basis.shape
    samples = direction.shape[1]
    chunks = sems.shape[1]
    size = leaves // chunks
    whole = [
        pltpu.make_async_copy(order_h, order, sems.at[3, 0]),
        pltpu.make_async_copy(node_h, node_transfer, sems.at[3, 1]),
    ]
    copies = []
    for c in range(chunks):
        part = pl.ds(c * size, size)
        copies.append(
            [
                pltpu.make_async_copy(source.at[part], target.at[part], sems.at[i, c])
                for i, (source, target) in enumerate(
                    ((basis_h, basis), (direction_h, direction), (transfer_h, leaf_transfer))
                )
            ]
        )
    for copy in whole + sum(copies, []):
        copy.start()
    for copy in whole:
        copy.wait()
    rows = lax.broadcasted_iota(jnp.int32, (points, points), 0)
    node = jnp.zeros((samples, rank), F32)
    leaving = []
    for g in range(leaves):
        if g % size == 0:
            for copy in copies[g // size]:
                copy.wait()
        spot = jnp.where(rows == order[g : g + 1, :], 1.0, 0.0).astype(BF)
        own = nt(basis[g], spot).astype(BF)
        natural[g] = own
        weights = nt(direction[g], own).astype(BF)
        coef[g // 2, :, (g % 2) * rank : (g % 2 + 1) * rank] = weights
        node = node + nt(weights, leaf_transfer[g])
        if g % size == size - 1:
            part = pl.ds(g + 1 - size, size)
            copy = pltpu.make_async_copy(
                natural.at[part], natural_h.at[part], sems.at[4, g // size]
            )
            copy.start()
            leaving.append(copy)
    for i, part in enumerate(thirds(nt(node.astype(BF), node_transfer[0]))):
        at = leaves + i
        coef[at // 2, :, (at % 2) * rank : (at % 2 + 1) * rank] = part.astype(BF)
    for copy in leaving:
        copy.wait()


def features(offsets):
    x, y, z = (offsets[i : i + 1] for i in range(3))
    square = thirds(KAPPA * (x * x + y * y + z * z))
    row = lax.broadcasted_iota(jnp.int32, (8, x.shape[1]), 0)
    packed = jnp.zeros((8, x.shape[1]), F32)
    for i, value in enumerate((x, y, z, jnp.ones_like(x)) + square):
        packed = jnp.where(row == i, value, packed)
    return packed.astype(BF)


def spread_features(offsets):
    lane = lax.broadcasted_iota(jnp.int32, (8, 128), 1)
    source = jnp.where(
        lane < 9,
        lane // 3,
        jnp.where(lane < 12, lane - 5, jnp.where(lane < 16, 7, jnp.where(lane < 64, 3, 0))),
    )
    source = jnp.where(lane < 112, source, 7)
    row = lax.broadcasted_iota(jnp.int32, (8, 128), 0)
    pick = jnp.where((row == source) & (row < 7), 1.0, 0.0).astype(BF)
    return lax.dot_general(
        features(offsets), pick, (((0,), (0,)), ((), ())), preferred_element_type=F32
    ).astype(BF)


def tile_kernel(start, waits, near_h, *refs):
    refs = refs[waits:]
    if start == 0:
        own, prev, after, tiles, mark, spread_x, plain, near, sem = refs
    else:
        plain, spread_x, tiles, mark, near, sem = refs
        own = plain
    listed = pltpu.make_async_copy(near_h, near, sem)
    listed.start()
    mark[...] = jnp.zeros_like(mark)
    count = tiles.shape[0]
    entries = near.shape[1]
    points = own.shape[2]
    leaves = own.shape[1]
    total = leaves * lax.axis_size("blk") * lax.axis_size("leaf")
    device = lax.axis_index("blk") * lax.axis_size("leaf") + lax.axis_index("leaf")
    anchor = (device - 1) * leaves
    if start == 0:
        for side, ref in enumerate((prev, own, after)):
            offsets = ref[...].astype(F32)
            for j in range(leaves):
                spread_x[side * leaves + j] = spread_features(offsets[:, j])
            if side == 1:
                plain[...] = offsets
    listed.wait()
    row = lax.broadcasted_iota(jnp.int32, (16, points), 0)
    lane = lax.broadcasted_iota(jnp.int32, (1, 128), 1)

    def leaf(i, carry):
        g = lax.axis_index("sample") * (leaves // 2) + start + i
        x, y, z = (plain[k, pl.ds(g, 1), :] for k in range(3))
        first = jnp.where((row >= 9) & (row < 12), 1.0, jnp.zeros((16, points), F32))
        at = 0
        for value in (x, y, z):
            for part in thirds(value * (-2.0 * KAPPA)):
                first = jnp.where(row == at, part, first)
                at += 1
        slots = []
        gap = jnp.zeros((16, points), F32)
        for e in range(entries):
            slot = lax.rem(near[g, e] - anchor + 2 * total, total)
            slots.append(slot)
            gap = jnp.where(row == e, (leaves + g - slot).astype(F32) * SPREAD, gap)
        moved = x + gap
        fixed = thirds(KAPPA * (moved * moved + y * y + z * z))
        gaps = thirds(gap * (-2.0 * KAPPA))
        weights = jnp.concatenate(
            [part.astype(BF) for part in (first,) + fixed + gaps + (jnp.zeros_like(first),)],
            axis=0,
        )
        for e in range(entries):
            keep = jnp.where((lane < 16) | (lane % 16 == e), 1.0, 0.0).astype(BF)
            square = jnp.maximum(nn(spread_x[slots[e]] * keep, weights), 1e-30)
            scaled = square * lax.rsqrt(square)
            value = (1.0 + scaled) * jnp.exp2(scaled * (-LOG2E))
            tiles[i, e * points : (e + 1) * points, :] = value.astype(BF)
        return carry

    lax.fori_loop(0, count, leaf, 0)


def top_kernel(own, *refs):
    sides, top = refs[:-2], refs[-1]
    samples, rank = top.shape
    at = own.shape[0] - 2

    def term(ref):
        first, second = ref[at].astype(F32), ref[at + 1].astype(F32)
        return first[:, :rank] + first[:, rank:] + second[:, :rank]

    total = term(own)
    if sides:
        total = total + term(sides[0])
    top[...] = total.astype(top.dtype)


def down_kernel(flip, *refs):
    tops, before, after, residual_h = refs[:4]
    sources, (base, residual), targets, sems = refs[4:12], refs[13:15], refs[15:24], refs[24]
    window, targets = targets[0], targets[1:]
    top_list, coupling_list, top_coupling, node_transfer = targets[:4]
    leaf_transfer, coupling, natural, direction = targets[4:]
    leaves, samples, points = direction.shape
    rank = natural.shape[1]
    clusters = lax.axis_size("blk")
    here = lax.axis_index("blk")
    total = leaves * clusters * lax.axis_size("leaf")
    anchor = (here * lax.axis_size("leaf") + lax.axis_index("leaf") - 1) * leaves
    pairs = list(zip(sources[:4], targets[:4]))
    whole = [
        pltpu.make_async_copy(source, target, sems.at[0, i])
        for i, (source, target) in enumerate(pairs)
    ]
    chunks = 4
    size = leaves // chunks
    parts = []
    for c in range(chunks):
        part = pl.ds(c * size, size)
        parts.append(
            [
                pltpu.make_async_copy(source.at[part], target.at[part], sems.at[1 + c, i])
                for i, (source, target) in enumerate(zip(sources[4:], targets[4:]))
            ]
        )
    ahead = pltpu.make_async_copy(residual_h, residual, sems.at[0, 6])
    for copy in whole + sum(parts, []) + [ahead]:
        copy.start()
    for side, packed in enumerate((before, after)):
        for g in range(leaves):
            part = packed[g // 2, :, (g % 2) * rank : (g % 2 + 1) * rank]
            window[side * leaves + g] = part
    for copy in whole:
        copy.wait()
    incoming = jnp.zeros((samples, rank), F32)
    for e in range(top_list.shape[1]):
        index = lax.rem(here - top_list[0, e] + clusters, clusters)
        incoming = incoming + nt(tops[index], top_coupling[0, e])
    down = nn(incoming.astype(BF), node_transfer[0]).astype(BF)
    for g in range(leaves):
        if g % size == 0:
            for copy in parts[g // size]:
                copy.wait()
        inward = nn(down, leaf_transfer[g])
        rows = []
        for c in range(coupling_list.shape[0]):
            slot = lax.rem(coupling_list[c, g] - anchor + 2 * total, total)
            slot = place(slot, leaves, flip)
            slot = jnp.where(slot >= 2 * leaves, slot - leaves, slot)
            slot = jnp.minimum(slot, 2 * leaves - 1)
            rows.append(window[slot])
        columns = [coupling[g, c] for c in range(coupling_list.shape[0])]
        inward = inward + nt(jnp.concatenate(rows, axis=1), jnp.concatenate(columns, axis=1))
        far = nn(inward.astype(BF), natural[g])
        base[g] = NUGGET * direction[g].astype(F32) + far
    ahead.wait()


def near_kernel(count, flip, near_h, *refs):
    pieces, tiles = refs[:count], refs[count : count + 2]
    kept, given, mark, window, near, sems = refs[-6:]
    mark[...] = jnp.zeros_like(mark)
    leaves = window.shape[0] // 3
    samples = kept.shape[1]
    total = leaves * lax.axis_size("blk") * lax.axis_size("leaf")
    device = lax.axis_index("blk") * lax.axis_size("leaf") + lax.axis_index("leaf")
    anchor = (device - 1) * leaves
    copies = [pltpu.make_async_copy(near_h, near, sems.at[count])]
    at = 0
    for i, piece in enumerate(pieces):
        columns = i % 2
        target = window.at[
            at : at + piece.shape[0], columns * samples : (columns + 1) * samples
        ]
        copies.append(pltpu.make_async_copy(piece, target, sems.at[i]))
        at += piece.shape[0] * columns
    for copy in copies:
        copy.start()
    for copy in copies:
        copy.wait()
    at = 0
    for part in tiles:

        def leaf(i, carry, part=part, at=at):
            g = lax.axis_index("sample") * kept.shape[0] + at + i
            values = []
            for e in range(near.shape[1]):
                slot = lax.rem(near[g, e] - anchor + 2 * total, total)
                values.append(window[place(slot, leaves, flip)])
            field = nn(jnp.concatenate(values, axis=1), part[i]) * AMPLITUDE
            kept[at + i] = field[:samples]
            given[at + i] = field[samples:].astype(BF)
            return carry

        lax.fori_loop(0, part.shape[0], leaf, 0)
        at += part.shape[0]


def residual_kernel(step, base, kept, received, residual, updated_h, updated, norms, sems):
    half = kept.shape[0]
    chunks = sems.shape[1]
    size = half // chunks
    leaving = []
    for c in range(chunks):
        for k in range(2):
            part = pl.ds(k * half + c * size, size)
            leaving.append(
                pltpu.make_async_copy(updated.at[part], updated_h.at[part], sems.at[k, c])
            )
    core = lax.axis_index("sample")
    steps = column(step[...])
    totals = [jnp.zeros((step.shape[1], 1), F32)] * 2
    for i in range(half):
        for theirs in range(2):
            g = (core ^ theirs) * half + i
            near = received[i].astype(F32) if theirs else kept[i]
            old = residual[g]
            new = old - steps * (base[g] + near)
            updated[g] = new
            for k, value in enumerate((old, new)):
                totals[k] = totals[k] + jnp.sum(value * value, axis=1, keepdims=True)
        if i % size == size - 1:
            for k in range(2):
                leaving[2 * (i // size) + k].start()
    samples = steps.shape[0]
    lane = lax.broadcasted_iota(jnp.int32, (samples, 128), 1)
    sub = lax.broadcasted_iota(jnp.int32, (samples, 128), 0)
    rows = [jnp.sum(jnp.where(lane == sub, part, 0.0), axis=0, keepdims=True) for part in totals]
    row = lax.broadcasted_iota(jnp.int32, norms.shape[1:], 0)
    packed = jnp.where(row == 0, rows[0], jnp.where(row == 1, rows[1], 0.0))
    for i in range(norms.shape[0]):
        norms[i] = packed
    for copy in leaving:
        copy.wait()


def direction_kernel(norms, updated, direction, result, held, sems):
    leaves, samples, points = updated.shape
    sums = norms[0]
    for i in range(1, norms.shape[0]):
        sums = sums + norms[i]
    ratio = column((sums[1:2, :] / sums[0:1, :])[:, :samples])
    chunks = sems.shape[0]
    size = leaves // chunks
    copies = []
    for c in range(chunks):
        for g in range(c * size, (c + 1) * size):
            held[g] = (updated[g] + ratio * direction[g].astype(F32)).astype(BF)
        part = pl.ds(c * size, size)
        copies.append(pltpu.make_async_copy(held.at[part], result.at[part], sems.at[c]))
        copies[-1].start()
    for copy in copies:
        copy.wait()


def on_device(
    residual,
    direction,
    step,
    coords,
    order,
    basis,
    leaf_transfer,
    node_transfer,
    near_list,
    coupling_list,
    coupling,
    top_list,
    top_coupling,
):
    leaves, samples, points = direction.shape
    rank = basis.shape[1]
    entries = near_list.shape[1]
    half = leaves // 2
    blk_count = lax.axis_size("blk")
    leaf_count = lax.axis_size("leaf")
    shape = jax.ShapeDtypeStruct
    token = shape((8, 128), F32)
    vmem = pl.BlockSpec(memory_space=pltpu.VMEM)
    anywhere = pl.BlockSpec(memory_space=pl.ANY)
    hbm = pl.BlockSpec(memory_space=pltpu.HBM)

    coords = jnp.transpose(coords, (1, 0, 2))
    coords_prev = shifted(coords, RING, 1)
    coords_after = shifted(coords, RING, -1)
    flip = leaf_count == 2
    travelling, first = lax.optimization_barrier((direction, order, coords_prev, coords_after))[:2]
    if flip:
        near_side = [shifted(travelling[i : i + half], "leaf", 1) for i in (0, half)]
    else:
        near_side = [shifted(travelling, RING, 1)]
        far_side = [shifted(travelling, RING, -1)]

    natural, coef, up_mark = call(
        up_kernel,
        (
            pltpu.HBM((leaves, rank, points), BF),
            shape((leaves // 2 + 2, samples, 2 * rank), BF),
            token,
        ),
        4 * leaves * rank * points * points,
        6 * MIB,
        in_specs=[hbm] * 5,
        out_specs=(hbm, vmem, vmem),
        scratch_shapes=[
            pltpu.VMEM(order.shape, jnp.int32),
            pltpu.VMEM(basis.shape, BF),
            pltpu.VMEM(direction.shape, BF),
            pltpu.VMEM(leaf_transfer.shape, BF),
            pltpu.VMEM(node_transfer.shape, BF),
            pltpu.VMEM(basis.shape, BF),
            pltpu.SemaphoreType.DMA((5, 4)),
        ],
        vmem=8,
    )(*in_hbm(first, basis, direction, leaf_transfer, node_transfer))

    def make_tiles(start, done, *operands):
        count = half // 2
        outs = (pltpu.VMEM((count, entries * points, points), BF), token)
        if start == 0:
            outs += (shape((3 * leaves, points, 128), BF), shape(coords.shape, F32))
        return call(
            functools.partial(tile_kernel, start, len(done)),
            outs,
            40 * count * entries * points * points,
            count * entries * points * points * 2,
            in_specs=[hbm] + [anywhere] * len(done) + [vmem] * len(operands),
            out_specs=(vmem,) * len(outs),
            scratch_shapes=[
                pltpu.SMEM(near_list.shape, jnp.int32),
                pltpu.SemaphoreType.DMA,
            ],
            vmem=8,
        )(*in_hbm(near_list), *done, *operands)

    if flip:
        coef_near = shifted(coef, "leaf", 1)
        coef_far = passed_on(coef_near)
    else:
        coef_near = shifted(coef, RING, 1)
        coef_far = shifted(coef, RING, -1)
    tiles_low, low_mark, spread_x, plain = make_tiles(
        0, [up_mark] + near_side[:1] * flip, coords, coords_prev, coords_after
    )
    if flip:
        marks = (up_mark, low_mark)
        far_side = [passed_on(ordered(part, mark)) for part, mark in zip(near_side, marks)]
    tiles_high, high_mark = make_tiles(
        half // 2, [low_mark] + (near_side[1:] + far_side[:1]) * flip, plain, spread_x
    )
    near_side = [ordered(part, high_mark) for part in near_side]
    far_side = [ordered(part, high_mark) for part in far_side]
    top = call(
        top_kernel,
        shape((samples, rank), BF if flip else F32),
        MIB,
        MIB,
        in_specs=[vmem] * (2 if flip else 1) + [anywhere],
        out_specs=vmem,
        vmem=4,
    )(coef, *([coef_near] if flip else []), high_mark)
    if not flip:
        terms = [shifted(top, "leaf", by) for by in range(1, leaf_count)]
        top = sum(terms, top).astype(BF)
    if blk_count <= 8:
        others = [shifted(top, "blk", by) for by in range(1, blk_count)]
    else:
        others = lax.all_gather(top[None], "blk", axis=0, tiled=True)
        places = jnp.mod(lax.axis_index("blk") - jnp.arange(blk_count, dtype=jnp.int32), blk_count)
        others = list(others[places][1:])
    pieces = []
    for part in near_side + in_hbm(direction) + far_side:
        pieces += [part, partner(part)]
    kept, given, near_mark = call(
        functools.partial(near_kernel, len(pieces), flip),
        (shape((half, samples, points), F32), shape((half, samples, points), BF), token),
        4 * half * entries * samples * points * points,
        half * entries * points * points * 2,
        in_specs=[hbm] + [anywhere] * len(pieces) + [vmem] * 2 + [anywhere] * (len(others) + 1),
        out_specs=(vmem,) * 3,
        scratch_shapes=[
            pltpu.VMEM((3 * leaves, 2 * samples, points), BF),
            pltpu.SMEM(near_list.shape, jnp.int32),
            pltpu.SemaphoreType.DMA((len(pieces) + 1,)),
        ],
        vmem=8,
    )(*in_hbm(near_list), *pieces, tiles_low, tiles_high, *others, coef_far)
    tops = jnp.stack([top] + others)
    arrays = (
        top_list,
        coupling_list.T,
        top_coupling,
        node_transfer,
        leaf_transfer,
        coupling,
        natural,
        direction,
    )
    spaces = (pltpu.SMEM,) * 2 + (pltpu.VMEM,) * 6
    whole = shape((leaves, samples, points), F32)
    base, residual_here = call(
        functools.partial(down_kernel, flip),
        (whole, whole),
        2 * leaves * samples * rank * (points + 9 * rank),
        8 * MIB,
        in_specs=[vmem] * 3 + [hbm] * 9 + [anywhere],
        out_specs=(vmem, vmem),
        scratch_shapes=[pltpu.VMEM((2 * leaves, samples, rank), BF)]
        + [space(array.shape, array.dtype) for space, array in zip(spaces, arrays)]
        + [pltpu.SemaphoreType.DMA((5, 7))],
        vmem=10,
    )(tops, coef_near, coef_far, *in_hbm(residual, *arrays), near_mark)
    received = partner(given)

    devices = blk_count * leaf_count
    residual_next, updated, norms = call(
        residual_kernel,
        (whole, whole, shape((devices, 8, 128), F32)),
        4 * MIB,
        5 * MIB,
        in_specs=[vmem] * 5,
        out_specs=(hbm, vmem, vmem),
        scratch_shapes=[pltpu.SemaphoreType.DMA((2, 4))],
        vmem=8,
    )(step[None, :], base, kept, received, residual_here)
    norms = lax.all_to_all(norms, RING, 0, 0)
    direction_next = call(
        direction_kernel,
        shape((leaves, samples, points), BF),
        MIB,
        2 * MIB,
        in_specs=[vmem] * 3,
        out_specs=anywhere,
        scratch_shapes=[
            pltpu.VMEM((leaves, samples, points), BF),
            pltpu.SemaphoreType.DMA((4,)),
        ],
        vmem=8,
    )(norms, updated, direction)
    return (residual_next, direction_next)


def solution(mesh):
    in_specs = (
        P(("groups", "blk", "leaf"), "sample", None),
        P(("groups", "blk", "leaf"), "sample", None),
        P(("groups", "sample")),
        P(("groups", "blk", "leaf"), None, None),
        P(("groups", "blk", "leaf"), None),
        P(("groups", "blk", "leaf"), None, None),
        P(("groups", "blk", "leaf"), None, None),
        P(("groups", "blk", "leaf"), None, None),
        P(("groups", "blk", "leaf"), None),
        P(("groups", "blk", "leaf"), None),
        P(("groups", "blk", "leaf"), None, None, None),
        P(("groups", "blk"), None),
        P(("groups", "blk"), None, None, None),
    )
    out_specs = (
        P(("groups", "blk", "leaf"), "sample", None),
        P(("groups", "blk", "leaf"), "sample", None),
    )
    return jax.shard_map(
        on_device, mesh=mesh, in_specs=in_specs, out_specs=out_specs, check_vma=False
    )
```

```python
import functools
import math

import jax
import jax.numpy as jnp
from jax import lax
from jax.experimental import pallas as pl
from jax.experimental.pallas import tpu as pltpu
from jax.sharding import PartitionSpec as P

LEAF_DEV = 16

ROOT_THREE = math.sqrt(3.0)
LENGTH = 0.3
AMPLITUDE = 0.25
NUGGET = 0.5
SPREAD = 0.5 / LEAF_DEV
KAPPA = (ROOT_THREE / LENGTH) ** 2
LOG2E = 1.4426950408889634

RING = ("blk", "leaf")
BF = jnp.bfloat16
F32 = jnp.float32
MIB = 1 << 20


def shifted(array, axis, by):
    if isinstance(axis, tuple):
        count = math.prod(lax.axis_size(name) for name in axis)
    else:
        count = lax.axis_size(axis)
    return lax.ppermute(array, axis, [(i, (i + by) % count) for i in range(count)])


def partner(array):
    return lax.ppermute(array, "sample", [(0, 1), (1, 0)])


def ordered(array, *first):
    return lax.optimization_barrier((array,) + first)[0]


def column(row):
    size = row.shape[1]
    shape = (size, size)
    here = lax.broadcasted_iota(jnp.int32, shape, 0) == lax.broadcasted_iota(jnp.int32, shape, 1)
    return jnp.sum(jnp.where(here, row, 0.0), axis=1, keepdims=True)


def in_hbm(*arrays):
    return [pltpu.with_memory_space_constraint(array, pltpu.HBM) for array in arrays]


def thirds(value):
    high = value.astype(BF).astype(F32)
    rest = value - high
    middle = rest.astype(BF).astype(F32)
    return high, middle, rest - middle


def nt(left, right):
    return lax.dot_general(left, right, (((1,), (1,)), ((), ())), preferred_element_type=F32)


def nn(left, right):
    return jnp.dot(left, right, preferred_element_type=F32)


def call(kernel, outs, flops, moved, vmem=40, **kwargs):
    return pl.pallas_call(
        kernel,
        out_shape=outs,
        compiler_params=pltpu.CompilerParams(vmem_limit_bytes=vmem * MIB),
        cost_estimate=pl.CostEstimate(flops=flops, bytes_accessed=moved, transcendentals=0),
        **kwargs,
    )


def up_kernel(order_h, basis_h, direction_h, transfer_h, node_h, natural_h, coef, mark, *scratch):
    mark[...] = jnp.zeros_like(mark)
    order, basis, direction, leaf_transfer, node_transfer, natural, sems = scratch
    leaves, rank, points = basis.shape
    samples = direction.shape[1]
    chunks = sems.shape[1]
    size = leaves // chunks
    whole = [
        pltpu.make_async_copy(order_h, order, sems.at[3, 0]),
        pltpu.make_async_copy(node_h, node_transfer, sems.at[3, 1]),
    ]
    copies = []
    for c in range(chunks):
        part = pl.ds(c * size, size)
        copies.append(
            [
                pltpu.make_async_copy(source.at[part], target.at[part], sems.at[i, c])
                for i, (source, target) in enumerate(
                    ((basis_h, basis), (direction_h, direction), (transfer_h, leaf_transfer))
                )
            ]
        )
    for copy in whole + sum(copies, []):
        copy.start()
    for copy in whole:
        copy.wait()
    rows = lax.broadcasted_iota(jnp.int32, (points, points), 0)
    node = jnp.zeros((samples, rank), F32)
    leaving = []
    for g in range(leaves):
        if g % size == 0:
            for copy in copies[g // size]:
                copy.wait()
        place = jnp.where(rows == order[g : g + 1, :], 1.0, 0.0).astype(BF)
        own = nt(basis[g], place).astype(BF)
        natural[g] = own
        weights = nt(direction[g], own).astype(BF)
        coef[g // 2, :, (g % 2) * rank : (g % 2 + 1) * rank] = weights
        node = node + nt(weights, leaf_transfer[g])
        if g % size == size - 1:
            part = pl.ds(g + 1 - size, size)
            copy = pltpu.make_async_copy(
                natural.at[part], natural_h.at[part], sems.at[4, g // size]
            )
            copy.start()
            leaving.append(copy)
    for i, part in enumerate(thirds(nt(node.astype(BF), node_transfer[0]))):
        at = leaves + i
        coef[at // 2, :, (at % 2) * rank : (at % 2 + 1) * rank] = part.astype(BF)
    for copy in leaving:
        copy.wait()


def features(offsets):
    x, y, z = (offsets[i : i + 1] for i in range(3))
    square = thirds(KAPPA * (x * x + y * y + z * z))
    row = lax.broadcasted_iota(jnp.int32, (8, x.shape[1]), 0)
    packed = jnp.zeros((8, x.shape[1]), F32)
    for i, value in enumerate((x, y, z, jnp.ones_like(x)) + square):
        packed = jnp.where(row == i, value, packed)
    return packed.astype(BF)


def spread_features(offsets):
    lane = lax.broadcasted_iota(jnp.int32, (8, 128), 1)
    source = jnp.where(
        lane < 9,
        lane // 3,
        jnp.where(lane < 12, lane - 5, jnp.where(lane < 16, 7, jnp.where(lane < 64, 3, 0))),
    )
    source = jnp.where(lane < 112, source, 7)
    row = lax.broadcasted_iota(jnp.int32, (8, 128), 0)
    pick = jnp.where((row == source) & (row < 7), 1.0, 0.0).astype(BF)
    return lax.dot_general(
        features(offsets), pick, (((0,), (0,)), ((), ())), preferred_element_type=F32
    ).astype(BF)


def tile_kernel(start, near_h, _, *refs):
    if start == 0:
        own_h, prev, after, tiles, mark, spread_x, plain, own, near, sem = refs
        offered = pltpu.make_async_copy(own_h, own, sem.at[1])
        offered.start()
    else:
        plain, spread_x, tiles, mark, near, sem = refs
        own = plain
    listed = pltpu.make_async_copy(near_h, near, sem.at[0])
    listed.start()
    mark[...] = jnp.zeros_like(mark)
    count = tiles.shape[0]
    entries = near.shape[1]
    points = own.shape[2]
    leaves = own.shape[1]
    total = leaves * lax.axis_size("blk") * lax.axis_size("leaf")
    device = lax.axis_index("blk") * lax.axis_size("leaf") + lax.axis_index("leaf")
    anchor = (device - 1) * leaves
    if start == 0:
        offered.wait()
        for side, ref in enumerate((prev, own, after)):
            offsets = ref[...].astype(F32)
            for j in range(leaves):
                spread_x[side * leaves + j] = spread_features(offsets[:, j])
            if side == 1:
                plain[...] = offsets
    listed.wait()
    row = lax.broadcasted_iota(jnp.int32, (16, points), 0)
    lane = lax.broadcasted_iota(jnp.int32, (1, 128), 1)

    def leaf(i, carry):
        g = lax.axis_index("sample") * (leaves // 2) + start + i
        x, y, z = (plain[k, pl.ds(g, 1), :] for k in range(3))
        first = jnp.where((row >= 9) & (row < 12), 1.0, jnp.zeros((16, points), F32))
        at = 0
        for value in (x, y, z):
            for part in thirds(value * (-2.0 * KAPPA)):
                first = jnp.where(row == at, part, first)
                at += 1
        slots = []
        gap = jnp.zeros((16, points), F32)
        for e in range(entries):
            slot = lax.rem(near[g, e] - anchor + 2 * total, total)
            slots.append(slot)
            gap = jnp.where(row == e, (leaves + g - slot).astype(F32) * SPREAD, gap)
        moved = x + gap
        fixed = thirds(KAPPA * (moved * moved + y * y + z * z))
        gaps = thirds(gap * (-2.0 * KAPPA))
        weights = jnp.concatenate(
            [part.astype(BF) for part in (first,) + fixed + gaps + (jnp.zeros_like(first),)],
            axis=0,
        )
        for e in range(entries):
            keep = jnp.where((lane < 16) | (lane % 16 == e), 1.0, 0.0).astype(BF)
            square = jnp.maximum(nn(spread_x[slots[e]] * keep, weights), 1e-30)
            scaled = square * lax.rsqrt(square)
            value = (1.0 + scaled) * jnp.exp2(scaled * (-LOG2E))
            tiles[i, e * points : (e + 1) * points, :] = value.astype(BF)
        return carry

    lax.fori_loop(0, count, leaf, 0)


def top_kernel(own, *refs):
    sides, top = refs[:-2], refs[-1]
    samples, rank = top.shape
    at = own.shape[0] - 2

    def term(ref):
        first, second = ref[at].astype(F32), ref[at + 1].astype(F32)
        return first[:, :rank] + first[:, rank:] + second[:, :rank]

    total = term(own)
    if sides:
        low = lax.axis_index("leaf") == 0
        total = total + jnp.where(low, term(sides[1]), term(sides[0]))
    top[...] = total.astype(top.dtype)


def down_kernel(*refs):
    tops, before, after, leaf_transfer, coupling, natural, direction = refs[:7]
    sources, base, window, targets, sems = refs[7:11], refs[12], refs[13], refs[14:18], refs[18]
    top_list, coupling_list, top_coupling, node_transfer = targets
    leaves, samples, points = direction.shape
    rank = natural.shape[1]
    clusters = lax.axis_size("blk")
    here = lax.axis_index("blk")
    total = leaves * clusters * lax.axis_size("leaf")
    anchor = (here * lax.axis_size("leaf") + lax.axis_index("leaf") - 1) * leaves
    copies = [
        pltpu.make_async_copy(source, target, sems.at[i])
        for i, (source, target) in enumerate(zip(sources, targets))
    ]
    for copy in copies:
        copy.start()
    for side, packed in enumerate((before, after)):
        for g in range(leaves):
            part = packed[g // 2, :, (g % 2) * rank : (g % 2 + 1) * rank]
            window[side * leaves + g] = part
    for copy in copies:
        copy.wait()
    incoming = jnp.zeros((samples, rank), F32)
    for e in range(top_list.shape[1]):
        place = lax.rem(here - top_list[0, e] + clusters, clusters)
        incoming = incoming + nt(tops[place], top_coupling[0, e])
    down = nn(incoming.astype(BF), node_transfer[0]).astype(BF)
    for g in range(leaves):
        inward = nn(down, leaf_transfer[g])
        rows = []
        for c in range(coupling_list.shape[0]):
            slot = lax.rem(coupling_list[c, g] - anchor + 2 * total, total)
            slot = jnp.where(slot >= 2 * leaves, slot - leaves, slot)
            slot = jnp.minimum(slot, 2 * leaves - 1)
            rows.append(window[slot])
        columns = [coupling[g, c] for c in range(coupling_list.shape[0])]
        inward = inward + nt(jnp.concatenate(rows, axis=1), jnp.concatenate(columns, axis=1))
        far = nn(inward.astype(BF), natural[g])
        base[g] = NUGGET * direction[g].astype(F32) + far


def near_kernel(near_h, *refs):
    pieces, tiles, (kept, given, mark, window, near, sems) = refs[:6], refs[6:8], refs[-6:]
    mark[...] = jnp.zeros_like(mark)
    leaves = window.shape[0] // 3
    samples = kept.shape[1]
    total = leaves * lax.axis_size("blk") * lax.axis_size("leaf")
    device = lax.axis_index("blk") * lax.axis_size("leaf") + lax.axis_index("leaf")
    anchor = (device - 1) * leaves
    copies = [pltpu.make_async_copy(near_h, near, sems.at[6])]
    for i, piece in enumerate(pieces):
        side, columns = i // 2, i % 2
        copies.append(
            pltpu.make_async_copy(
                piece,
                window.at[
                    side * leaves : (side + 1) * leaves,
                    columns * samples : (columns + 1) * samples,
                ],
                sems.at[i],
            )
        )
    for copy in copies:
        copy.start()
    for copy in copies:
        copy.wait()
    at = 0
    for part in tiles:

        def leaf(i, carry, part=part, at=at):
            g = lax.axis_index("sample") * kept.shape[0] + at + i
            values = []
            for e in range(near.shape[1]):
                values.append(window[lax.rem(near[g, e] - anchor + 2 * total, total)])
            field = nn(jnp.concatenate(values, axis=1), part[i]) * AMPLITUDE
            kept[at + i] = field[:samples]
            given[at + i] = field[samples:].astype(BF)
            return carry

        lax.fori_loop(0, part.shape[0], leaf, 0)
        at += part.shape[0]


def residual_kernel(step, base, kept, received, residual, updated_h, updated, norms, sems):
    half = kept.shape[0]
    chunks = sems.shape[1]
    size = half // chunks
    leaving = []
    for c in range(chunks):
        for k in range(2):
            part = pl.ds(k * half + c * size, size)
            leaving.append(
                pltpu.make_async_copy(updated.at[part], updated_h.at[part], sems.at[k, c])
            )
    core = lax.axis_index("sample")
    steps = column(step[...])
    totals = [jnp.zeros((step.shape[1], 1), F32)] * 2
    for i in range(half):
        for theirs in range(2):
            g = (core ^ theirs) * half + i
            near = received[i].astype(F32) if theirs else kept[i]
            old = residual[g]
            new = old - steps * (base[g] + near)
            updated[g] = new
            for k, value in enumerate((old, new)):
                totals[k] = totals[k] + jnp.sum(value * value, axis=1, keepdims=True)
        if i % size == size - 1:
            for k in range(2):
                leaving[2 * (i // size) + k].start()
    samples = steps.shape[0]
    lane = lax.broadcasted_iota(jnp.int32, (samples, 128), 1)
    sub = lax.broadcasted_iota(jnp.int32, (samples, 128), 0)
    rows = [jnp.sum(jnp.where(lane == sub, part, 0.0), axis=0, keepdims=True) for part in totals]
    row = lax.broadcasted_iota(jnp.int32, norms.shape[1:], 0)
    packed = jnp.where(row == 0, rows[0], jnp.where(row == 1, rows[1], 0.0))
    for i in range(norms.shape[0]):
        norms[i] = packed
    for copy in leaving:
        copy.wait()


def direction_kernel(norms, updated, direction, result, held, sems):
    leaves, samples, points = updated.shape
    sums = norms[0]
    for i in range(1, norms.shape[0]):
        sums = sums + norms[i]
    ratio = column((sums[1:2, :] / sums[0:1, :])[:, :samples])
    chunks = sems.shape[0]
    size = leaves // chunks
    copies = []
    for c in range(chunks):
        for g in range(c * size, (c + 1) * size):
            held[g] = (updated[g] + ratio * direction[g].astype(F32)).astype(BF)
        part = pl.ds(c * size, size)
        copies.append(pltpu.make_async_copy(held.at[part], result.at[part], sems.at[c]))
        copies[-1].start()
    for copy in copies:
        copy.wait()


def on_device(
    residual,
    direction,
    step,
    coords,
    order,
    basis,
    leaf_transfer,
    node_transfer,
    near_list,
    coupling_list,
    coupling,
    top_list,
    top_coupling,
):
    leaves, samples, points = direction.shape
    rank = basis.shape[1]
    entries = near_list.shape[1]
    half = leaves // 2
    blk_count = lax.axis_size("blk")
    leaf_count = lax.axis_size("leaf")
    shape = jax.ShapeDtypeStruct
    token = shape((8, 128), F32)
    vmem = pl.BlockSpec(memory_space=pltpu.VMEM)
    anywhere = pl.BlockSpec(memory_space=pl.ANY)
    hbm = pl.BlockSpec(memory_space=pltpu.HBM)

    coords = jnp.transpose(coords, (1, 0, 2))
    coords_prev = shifted(coords, RING, 1)
    coords_after = shifted(coords, RING, -1)
    travelling, first = lax.optimization_barrier((direction, order, coords_prev, coords_after))[:2]
    direction_prev = shifted(travelling, RING, 1)
    direction_after = shifted(travelling, RING, -1)
    direction_other = partner(direction)

    natural, coef, up_mark = call(
        up_kernel,
        (
            pltpu.HBM((leaves, rank, points), BF),
            shape((leaves // 2 + 2, samples, 2 * rank), BF),
            token,
        ),
        4 * leaves * rank * points * points,
        6 * MIB,
        in_specs=[hbm] * 5,
        out_specs=(hbm, vmem, vmem),
        scratch_shapes=[
            pltpu.VMEM(order.shape, jnp.int32),
            pltpu.VMEM(basis.shape, BF),
            pltpu.VMEM(direction.shape, BF),
            pltpu.VMEM(leaf_transfer.shape, BF),
            pltpu.VMEM(node_transfer.shape, BF),
            pltpu.VMEM(basis.shape, BF),
            pltpu.SemaphoreType.DMA((5, 4)),
        ],
        vmem=8,
    )(*in_hbm(first, basis, direction, leaf_transfer, node_transfer))

    def make_tiles(start, done, *operands):
        count = half // 2
        outs = (pltpu.VMEM((count, entries * points, points), BF), token)
        if start == 0:
            outs += (shape((3 * leaves, points, 128), BF), shape(coords.shape, F32))
        return call(
            functools.partial(tile_kernel, start),
            outs,
            40 * count * entries * points * points,
            count * entries * points * points * (16 if start == 0 else 1),
            in_specs=[hbm, anywhere, hbm if start == 0 else vmem] + [vmem] * (len(operands) - 1),
            out_specs=(vmem,) * len(outs),
            scratch_shapes=[pltpu.VMEM(coords.shape, BF)] * (start == 0)
            + [pltpu.SMEM(near_list.shape, jnp.int32), pltpu.SemaphoreType.DMA((2,))],
            vmem=8,
        )(*in_hbm(near_list), done, *operands)

    coef_prev = shifted(coef, RING, 1)
    coef_after = shifted(coef, RING, -1)
    tiles_low, low_mark, spread_x, plain = make_tiles(
        0, up_mark, *in_hbm(coords), coords_prev, coords_after
    )
    tiles_high, high_mark = make_tiles(half // 2, low_mark, plain, spread_x)
    direction_prev = ordered(direction_prev, high_mark)
    direction_after = ordered(direction_after, high_mark)
    kept, given, near_mark = call(
        near_kernel,
        (shape((half, samples, points), F32), shape((half, samples, points), BF), token),
        MIB,
        MIB,
        in_specs=[hbm] + [anywhere] * 6 + [vmem] * 2,
        out_specs=(vmem,) * 3,
        scratch_shapes=[
            pltpu.VMEM((3 * leaves, 2 * samples, points), BF),
            pltpu.SMEM(near_list.shape, jnp.int32),
            pltpu.SemaphoreType.DMA((7,)),
        ],
        vmem=8,
    )(
        *in_hbm(near_list),
        direction_prev,
        partner(direction_prev),
        *in_hbm(direction),
        direction_other,
        direction_after,
        partner(direction_after),
        tiles_low,
        tiles_high,
    )

    paired = leaf_count == 2
    top = call(
        top_kernel,
        shape((samples, rank), BF if paired else F32),
        MIB,
        MIB,
        in_specs=[vmem] * (3 if paired else 1) + [anywhere],
        out_specs=vmem,
        vmem=4,
    )(coef, *((coef_prev, coef_after) if paired else ()), near_mark)
    if not paired:
        terms = [shifted(top, "leaf", by) for by in range(1, leaf_count)]
        top = sum(terms, top).astype(BF)
    if blk_count <= 8:
        others = [shifted(top, "blk", by) for by in range(1, blk_count)]
    else:
        others = lax.all_gather(top[None], "blk", axis=0, tiled=True)
        places = jnp.mod(lax.axis_index("blk") - jnp.arange(blk_count, dtype=jnp.int32), blk_count)
        others = list(others[places][1:])
    tops = jnp.stack([top] + others)
    arrays = (top_list, coupling_list.T, top_coupling, node_transfer)
    spaces = (pltpu.SMEM,) * 2 + (pltpu.VMEM,) * 2
    whole = shape((leaves, samples, points), F32)
    base = call(
        down_kernel,
        whole,
        2 * leaves * samples * rank * (points + 9 * rank),
        8 * MIB,
        in_specs=[vmem] * 7 + [hbm] * 4 + [anywhere],
        out_specs=vmem,
        scratch_shapes=[pltpu.VMEM((2 * leaves, samples, rank), BF)]
        + [space(array.shape, array.dtype) for space, array in zip(spaces, arrays)]
        + [pltpu.SemaphoreType.DMA((4,))],
        vmem=10,
    )(
        tops,
        coef_prev,
        coef_after,
        leaf_transfer,
        coupling,
        natural,
        direction,
        *in_hbm(*arrays),
        near_mark,
    )
    received = partner(given)

    devices = blk_count * leaf_count
    residual_next, updated, norms = call(
        residual_kernel,
        (whole, whole, shape((devices, 8, 128), F32)),
        4 * MIB,
        5 * MIB,
        in_specs=[vmem] * 5,
        out_specs=(hbm, vmem, vmem),
        scratch_shapes=[pltpu.SemaphoreType.DMA((2, 4))],
        vmem=8,
    )(step[None, :], base, kept, received, residual)
    norms = lax.all_to_all(norms, RING, 0, 0)
    direction_next = call(
        direction_kernel,
        shape((leaves, samples, points), BF),
        MIB,
        2 * MIB,
        in_specs=[vmem] * 3,
        out_specs=anywhere,
        scratch_shapes=[
            pltpu.VMEM((leaves, samples, points), BF),
            pltpu.SemaphoreType.DMA((4,)),
        ],
        vmem=8,
    )(norms, updated, direction)
    return (residual_next, direction_next)


def solution(mesh):
    in_specs = (
        P(("groups", "blk", "leaf"), "sample", None),
        P(("groups", "blk", "leaf"), "sample", None),
        P(("groups", "sample")),
        P(("groups", "blk", "leaf"), None, None),
        P(("groups", "blk", "leaf"), None),
        P(("groups", "blk", "leaf"), None, None),
        P(("groups", "blk", "leaf"), None, None),
        P(("groups", "blk", "leaf"), None, None),
        P(("groups", "blk", "leaf"), None),
        P(("groups", "blk", "leaf"), None),
        P(("groups", "blk", "leaf"), None, None, None),
        P(("groups", "blk"), None),
        P(("groups", "blk"), None, None, None),
    )
    out_specs = (
        P(("groups", "blk", "leaf"), "sample", None),
        P(("groups", "blk", "leaf"), "sample", None),
    )
    return jax.shard_map(
        on_device, mesh=mesh, in_specs=in_specs, out_specs=out_specs, check_vma=False
    )
```

```python
import functools
import math

import jax
import jax.numpy as jnp
from jax import lax
from jax.experimental import pallas as pl
from jax.experimental.pallas import tpu as pltpu
from jax.sharding import PartitionSpec as P

LEAF_DEV = 16

ROOT_THREE = math.sqrt(3.0)
LENGTH = 0.3
AMPLITUDE = 0.25
NUGGET = 0.5
SPREAD = 0.5 / LEAF_DEV
KAPPA = (ROOT_THREE / LENGTH) ** 2
LOG2E = 1.4426950408889634

RING = ("blk", "leaf")
BF = jnp.bfloat16
F32 = jnp.float32
MIB = 1 << 20


def shifted(array, axis, by):
    if isinstance(axis, tuple):
        count = math.prod(lax.axis_size(name) for name in axis)
    else:
        count = lax.axis_size(axis)
    return lax.ppermute(array, axis, [(i, (i + by) % count) for i in range(count)])


def partner(array):
    return lax.ppermute(array, "sample", [(0, 1), (1, 0)])


def ordered(array, *first):
    return lax.optimization_barrier((array,) + first)[0]


def column(row):
    size = row.shape[1]
    shape = (size, size)
    here = lax.broadcasted_iota(jnp.int32, shape, 0) == lax.broadcasted_iota(jnp.int32, shape, 1)
    return jnp.sum(jnp.where(here, row, 0.0), axis=1, keepdims=True)


def in_hbm(*arrays):
    return [pltpu.with_memory_space_constraint(array, pltpu.HBM) for array in arrays]


def thirds(value):
    high = value.astype(BF).astype(F32)
    rest = value - high
    middle = rest.astype(BF).astype(F32)
    return high, middle, rest - middle


def nt(left, right):
    return lax.dot_general(left, right, (((1,), (1,)), ((), ())), preferred_element_type=F32)


def nn(left, right):
    return jnp.dot(left, right, preferred_element_type=F32)


def call(kernel, outs, flops, moved, vmem=40, **kwargs):
    return pl.pallas_call(
        kernel,
        out_shape=outs,
        compiler_params=pltpu.CompilerParams(vmem_limit_bytes=vmem * MIB),
        cost_estimate=pl.CostEstimate(flops=flops, bytes_accessed=moved, transcendentals=0),
        **kwargs,
    )


def up_kernel(order_h, basis_h, direction_h, transfer_h, node_h, natural_h, coef, lifted, mark, *scratch):
    mark[...] = jnp.zeros_like(mark)
    order, basis, direction, leaf_transfer, node_transfer, natural, sems = scratch
    leaves, rank, points = basis.shape
    samples = direction.shape[1]
    chunks = sems.shape[1]
    size = leaves // chunks
    whole = [
        pltpu.make_async_copy(order_h, order, sems.at[3, 0]),
        pltpu.make_async_copy(node_h, node_transfer, sems.at[3, 1]),
    ]
    copies = []
    for c in range(chunks):
        part = pl.ds(c * size, size)
        copies.append(
            [
                pltpu.make_async_copy(source.at[part], target.at[part], sems.at[i, c])
                for i, (source, target) in enumerate(
                    ((basis_h, basis), (direction_h, direction), (transfer_h, leaf_transfer))
                )
            ]
        )
    for copy in whole + sum(copies, []):
        copy.start()
    for copy in whole:
        copy.wait()
    rows = lax.broadcasted_iota(jnp.int32, (points, points), 0)
    node = jnp.zeros((samples, rank), F32)
    leaving = []
    for g in range(leaves):
        if g % size == 0:
            for copy in copies[g // size]:
                copy.wait()
        place = jnp.where(rows == order[g : g + 1, :], 1.0, 0.0).astype(BF)
        own = nt(basis[g], place).astype(BF)
        natural[g] = own
        weights = nt(direction[g], own).astype(BF)
        coef[g // 2, :, (g % 2) * rank : (g % 2 + 1) * rank] = weights
        node = node + nt(weights, leaf_transfer[g])
        if g % size == size - 1:
            part = pl.ds(g + 1 - size, size)
            copy = pltpu.make_async_copy(
                natural.at[part], natural_h.at[part], sems.at[4, g // size]
            )
            copy.start()
            leaving.append(copy)
    lifted[...] = nt(node.astype(BF), node_transfer[0])
    for copy in leaving:
        copy.wait()


def features(offsets):
    x, y, z = (offsets[i : i + 1] for i in range(3))
    square = thirds(KAPPA * (x * x + y * y + z * z))
    row = lax.broadcasted_iota(jnp.int32, (8, x.shape[1]), 0)
    packed = jnp.zeros((8, x.shape[1]), F32)
    for i, value in enumerate((x, y, z, jnp.ones_like(x)) + square):
        packed = jnp.where(row == i, value, packed)
    return packed.astype(BF)


def spread_features(offsets):
    lane = lax.broadcasted_iota(jnp.int32, (8, 128), 1)
    source = jnp.where(
        lane < 9,
        lane // 3,
        jnp.where(lane < 12, lane - 5, jnp.where(lane < 16, 7, jnp.where(lane < 64, 3, 0))),
    )
    source = jnp.where(lane < 112, source, 7)
    row = lax.broadcasted_iota(jnp.int32, (8, 128), 0)
    pick = jnp.where((row == source) & (row < 7), 1.0, 0.0).astype(BF)
    return lax.dot_general(
        features(offsets), pick, (((0,), (0,)), ((), ())), preferred_element_type=F32
    ).astype(BF)


def tile_kernel(start, near_h, _, *refs):
    if start == 0:
        own_h, prev, after, tiles, mark, spread_x, plain, own, near, sem = refs
        offered = pltpu.make_async_copy(own_h, own, sem.at[1])
        offered.start()
    else:
        plain, spread_x, tiles, mark, near, sem = refs
        own = plain
    listed = pltpu.make_async_copy(near_h, near, sem.at[0])
    listed.start()
    mark[...] = jnp.zeros_like(mark)
    count = tiles.shape[0]
    entries = near.shape[1]
    points = own.shape[2]
    leaves = own.shape[1]
    total = leaves * lax.axis_size("blk") * lax.axis_size("leaf")
    device = lax.axis_index("blk") * lax.axis_size("leaf") + lax.axis_index("leaf")
    anchor = (device - 1) * leaves
    if start == 0:
        offered.wait()
        for side, ref in enumerate((prev, own, after)):
            offsets = ref[...].astype(F32)
            for j in range(leaves):
                spread_x[side * leaves + j] = spread_features(offsets[:, j])
            if side == 1:
                plain[...] = offsets
    listed.wait()
    row = lax.broadcasted_iota(jnp.int32, (16, points), 0)
    lane = lax.broadcasted_iota(jnp.int32, (1, 128), 1)

    def leaf(i, carry):
        g = lax.axis_index("sample") * (leaves // 2) + start + i
        x, y, z = (plain[k, pl.ds(g, 1), :] for k in range(3))
        first = jnp.where((row >= 9) & (row < 12), 1.0, jnp.zeros((16, points), F32))
        at = 0
        for value in (x, y, z):
            for part in thirds(value * (-2.0 * KAPPA)):
                first = jnp.where(row == at, part, first)
                at += 1
        slots = []
        gap = jnp.zeros((16, points), F32)
        for e in range(entries):
            slot = lax.rem(near[g, e] - anchor + 2 * total, total)
            slots.append(slot)
            gap = jnp.where(row == e, (leaves + g - slot).astype(F32) * SPREAD, gap)
        moved = x + gap
        fixed = thirds(KAPPA * (moved * moved + y * y + z * z))
        gaps = thirds(gap * (-2.0 * KAPPA))
        weights = jnp.concatenate(
            [part.astype(BF) for part in (first,) + fixed + gaps + (jnp.zeros_like(first),)],
            axis=0,
        )
        for e in range(entries):
            keep = jnp.where((lane < 16) | (lane % 16 == e), 1.0, 0.0).astype(BF)
            square = jnp.maximum(nn(spread_x[slots[e]] * keep, weights), 1e-30)
            scaled = square * lax.rsqrt(square)
            value = (1.0 + scaled) * jnp.exp2(scaled * (-LOG2E))
            tiles[i, e * points : (e + 1) * points, :] = value.astype(BF)
        return carry

    lax.fori_loop(0, count, leaf, 0)


def top_kernel(_, *refs):
    terms, top = refs[:-1], refs[-1]
    total = terms[0][...]
    for term in terms[1:]:
        total = total + term[...]
    top[...] = total.astype(top.dtype)


def window_kernel(given, before, after, window, sent):
    sent[...] = given[...]
    rows, _, lanes = before.shape
    rank = lanes // 2
    for side, packed in enumerate((before, after)):
        for g in range(2 * rows):
            part = packed[g // 2, :, (g % 2) * rank : (g % 2 + 1) * rank]
            window[side * 2 * rows + g] = part


def down_kernel(*refs):
    clusters = lax.axis_size("blk")
    each, refs = refs[:clusters], refs[clusters:]
    window, leaf_transfer, coupling, natural, direction = refs[:5]
    sources, base, targets, tops, sems = refs[5:9], refs[9], refs[10:14], refs[14], refs[15]
    for i, top in enumerate(each):
        tops[i] = top[...]
    top_list, coupling_list, top_coupling, node_transfer = targets
    leaves, samples, points = direction.shape
    rank = natural.shape[1]
    here = lax.axis_index("blk")
    total = leaves * clusters * lax.axis_size("leaf")
    anchor = (here * lax.axis_size("leaf") + lax.axis_index("leaf") - 1) * leaves
    copies = [
        pltpu.make_async_copy(source, target, sems.at[i])
        for i, (source, target) in enumerate(zip(sources, targets))
    ]
    for copy in copies:
        copy.start()
    for copy in copies:
        copy.wait()
    incoming = jnp.zeros((samples, rank), F32)
    for e in range(top_list.shape[1]):
        place = lax.rem(here - top_list[0, e] + clusters, clusters)
        incoming = incoming + nt(tops[place], top_coupling[0, e])
    down = nn(incoming.astype(BF), node_transfer[0]).astype(BF)
    for g in range(leaves):
        inward = nn(down, leaf_transfer[g])
        rows = []
        for c in range(coupling_list.shape[0]):
            slot = lax.rem(coupling_list[c, g] - anchor + 2 * total, total)
            slot = jnp.where(slot >= 2 * leaves, slot - leaves, slot)
            slot = jnp.minimum(slot, 2 * leaves - 1)
            rows.append(window[slot])
        columns = [coupling[g, c] for c in range(coupling_list.shape[0])]
        inward = inward + nt(jnp.concatenate(rows, axis=1), jnp.concatenate(columns, axis=1))
        far = nn(inward.astype(BF), natural[g])
        base[g] = NUGGET * direction[g].astype(F32) + far


def near_kernel(near_h, *refs):
    pieces, tiles, (kept, given, mark, window, near, sems) = refs[:6], refs[6:8], refs[-6:]
    mark[...] = jnp.zeros_like(mark)
    leaves = window.shape[0] // 3
    samples = kept.shape[1]
    total = leaves * lax.axis_size("blk") * lax.axis_size("leaf")
    device = lax.axis_index("blk") * lax.axis_size("leaf") + lax.axis_index("leaf")
    anchor = (device - 1) * leaves
    copies = [pltpu.make_async_copy(near_h, near, sems.at[6])]
    for i, piece in enumerate(pieces):
        side, columns = i // 2, i % 2
        copies.append(
            pltpu.make_async_copy(
                piece,
                window.at[
                    side * leaves : (side + 1) * leaves,
                    columns * samples : (columns + 1) * samples,
                ],
                sems.at[i],
            )
        )
    for copy in copies:
        copy.start()
    for copy in copies:
        copy.wait()
    at = 0
    for part in tiles:

        def leaf(i, carry, part=part, at=at):
            g = lax.axis_index("sample") * kept.shape[0] + at + i
            values = []
            for e in range(near.shape[1]):
                values.append(window[lax.rem(near[g, e] - anchor + 2 * total, total)])
            field = nn(jnp.concatenate(values, axis=1), part[i]) * AMPLITUDE
            kept[at + i] = field[:samples]
            given[at + i] = field[samples:].astype(BF)
            return carry

        lax.fori_loop(0, part.shape[0], leaf, 0)
        at += part.shape[0]


def residual_kernel(step, base, kept, received, residual, updated_h, updated, norms, sems):
    half = kept.shape[0]
    chunks = sems.shape[1]
    size = half // chunks
    leaving = []
    for c in range(chunks):
        for k in range(2):
            part = pl.ds(k * half + c * size, size)
            leaving.append(
                pltpu.make_async_copy(updated.at[part], updated_h.at[part], sems.at[k, c])
            )
    core = lax.axis_index("sample")
    steps = column(step[...])
    totals = [jnp.zeros((step.shape[1], 1), F32)] * 2
    for i in range(half):
        for theirs in range(2):
            g = (core ^ theirs) * half + i
            near = received[i].astype(F32) if theirs else kept[i]
            old = residual[g]
            new = old - steps * (base[g] + near)
            updated[g] = new
            for k, value in enumerate((old, new)):
                totals[k] = totals[k] + jnp.sum(value * value, axis=1, keepdims=True)
        if i % size == size - 1:
            for k in range(2):
                leaving[2 * (i // size) + k].start()
    samples = steps.shape[0]
    lane = lax.broadcasted_iota(jnp.int32, (samples, 128), 1)
    sub = lax.broadcasted_iota(jnp.int32, (samples, 128), 0)
    rows = [jnp.sum(jnp.where(lane == sub, part, 0.0), axis=0, keepdims=True) for part in totals]
    row = lax.broadcasted_iota(jnp.int32, norms.shape[1:], 0)
    packed = jnp.where(row == 0, rows[0], jnp.where(row == 1, rows[1], 0.0))
    for i in range(norms.shape[0]):
        norms[i] = packed
    for copy in leaving:
        copy.wait()


def direction_kernel(norms, updated, direction, result, held, sems):
    leaves, samples, points = updated.shape
    sums = norms[0]
    for i in range(1, norms.shape[0]):
        sums = sums + norms[i]
    ratio = column((sums[1:2, :] / sums[0:1, :])[:, :samples])
    chunks = sems.shape[0]
    size = leaves // chunks
    copies = []
    for c in range(chunks):
        for g in range(c * size, (c + 1) * size):
            held[g] = (updated[g] + ratio * direction[g].astype(F32)).astype(BF)
        part = pl.ds(c * size, size)
        copies.append(pltpu.make_async_copy(held.at[part], result.at[part], sems.at[c]))
        copies[-1].start()
    for copy in copies:
        copy.wait()


def on_device(
    residual,
    direction,
    step,
    coords,
    order,
    basis,
    leaf_transfer,
    node_transfer,
    near_list,
    coupling_list,
    coupling,
    top_list,
    top_coupling,
):
    leaves, samples, points = direction.shape
    rank = basis.shape[1]
    entries = near_list.shape[1]
    half = leaves // 2
    blk_count = lax.axis_size("blk")
    leaf_count = lax.axis_size("leaf")
    shape = jax.ShapeDtypeStruct
    token = shape((8, 128), F32)
    vmem = pl.BlockSpec(memory_space=pltpu.VMEM)
    anywhere = pl.BlockSpec(memory_space=pl.ANY)
    hbm = pl.BlockSpec(memory_space=pltpu.HBM)

    coords = jnp.transpose(coords, (1, 0, 2))
    coords_prev = shifted(coords, RING, 1)
    coords_after = shifted(coords, RING, -1)
    natural, coef, lifted, up_mark = call(
        up_kernel,
        (
            pltpu.HBM((leaves, rank, points), BF),
            shape((leaves // 2, samples, 2 * rank), BF),
            shape((samples, rank), F32),
            token,
        ),
        4 * leaves * rank * points * points,
        6 * MIB,
        in_specs=[hbm] * 5,
        out_specs=(hbm, vmem, vmem, vmem),
        scratch_shapes=[
            pltpu.VMEM(order.shape, jnp.int32),
            pltpu.VMEM(basis.shape, BF),
            pltpu.VMEM(direction.shape, BF),
            pltpu.VMEM(leaf_transfer.shape, BF),
            pltpu.VMEM(node_transfer.shape, BF),
            pltpu.VMEM(basis.shape, BF),
            pltpu.SemaphoreType.DMA((5, 4)),
        ],
        vmem=8,
    )(*in_hbm(order, basis, direction, leaf_transfer, node_transfer))

    def make_tiles(start, done, *operands):
        count = half // 2
        outs = (pltpu.VMEM((count, entries * points, points), BF), token)
        if start == 0:
            outs += (shape((3 * leaves, points, 128), BF), shape(coords.shape, F32))
        return call(
            functools.partial(tile_kernel, start),
            outs,
            40 * count * entries * points * points,
            count * entries * points * points * (16 if start == 0 else 1),
            in_specs=[hbm, anywhere, hbm if start == 0 else vmem] + [vmem] * (len(operands) - 1),
            out_specs=(vmem,) * len(outs),
            scratch_shapes=[pltpu.VMEM(coords.shape, BF)] * (start == 0)
            + [pltpu.SMEM(near_list.shape, jnp.int32), pltpu.SemaphoreType.DMA((2,))],
            vmem=8,
        )(*in_hbm(near_list), done, *operands)

    terms = [shifted(lifted, "leaf", by) for by in range(1, leaf_count)]
    travelling = ordered(direction, coords_prev, coords_after, *terms)
    direction_prev = shifted(travelling, RING, 1)
    direction_after = shifted(travelling, RING, -1)
    direction_other = partner(direction)
    coef_prev = shifted(coef, RING, 1)
    coef_after = shifted(coef, RING, -1)
    tiles_low, low_mark, spread_x, plain = make_tiles(
        0, up_mark, *in_hbm(coords), coords_prev, coords_after
    )
    top = call(
        top_kernel,
        shape((samples, rank), BF),
        MIB,
        MIB,
        in_specs=[anywhere] + [vmem] * leaf_count,
        out_specs=vmem,
        vmem=4,
    )(low_mark, lifted, *terms)
    if blk_count <= 8:
        others = [shifted(top, "blk", by) for by in range(1, blk_count)]
    else:
        others = lax.all_gather(top[None], "blk", axis=0, tiled=True)
        places = jnp.mod(lax.axis_index("blk") - jnp.arange(blk_count, dtype=jnp.int32), blk_count)
        others = list(others[places][1:])
    tiles_high, high_mark = make_tiles(half // 2, low_mark, plain, spread_x)
    direction_prev = ordered(direction_prev, high_mark, *others)
    direction_after = ordered(direction_after, high_mark, *others)
    kept, given, near_mark = call(
        near_kernel,
        (shape((half, samples, points), F32), shape((half, samples, points), BF), token),
        MIB,
        MIB,
        in_specs=[hbm] + [anywhere] * 6 + [vmem] * 2,
        out_specs=(vmem,) * 3,
        scratch_shapes=[
            pltpu.VMEM((3 * leaves, 2 * samples, points), BF),
            pltpu.SMEM(near_list.shape, jnp.int32),
            pltpu.SemaphoreType.DMA((7,)),
        ],
        vmem=8,
    )(
        *in_hbm(near_list),
        direction_prev,
        partner(direction_prev),
        *in_hbm(direction),
        direction_other,
        direction_after,
        partner(direction_after),
        tiles_low,
        tiles_high,
    )

    coef_window, given = call(
        window_kernel,
        (shape((2 * leaves, samples, rank), BF), shape((half, samples, points), BF)),
        MIB,
        MIB,
        in_specs=[vmem] * 3,
        out_specs=(vmem, vmem),
        vmem=4,
    )(given, coef_prev, coef_after)
    arrays = (top_list, coupling_list.T, top_coupling, node_transfer)
    spaces = (pltpu.SMEM,) * 2 + (pltpu.VMEM,) * 2
    whole = shape((leaves, samples, points), F32)
    base = call(
        down_kernel,
        whole,
        2 * leaves * samples * rank * (points + 9 * rank),
        8 * MIB,
        in_specs=[vmem] * (5 + blk_count) + [hbm] * 4,
        out_specs=vmem,
        scratch_shapes=[space(array.shape, array.dtype) for space, array in zip(spaces, arrays)]
        + [pltpu.VMEM((blk_count, samples, rank), BF), pltpu.SemaphoreType.DMA((4,))],
        vmem=10,
    )(
        top,
        *others,
        coef_window,
        leaf_transfer,
        coupling,
        natural,
        direction,
        *in_hbm(*arrays),
    )
    received = partner(given)

    devices = blk_count * leaf_count
    residual_next, updated, norms = call(
        residual_kernel,
        (whole, whole, shape((devices, 8, 128), F32)),
        4 * MIB,
        5 * MIB,
        in_specs=[vmem] * 5,
        out_specs=(hbm, vmem, vmem),
        scratch_shapes=[pltpu.SemaphoreType.DMA((2, 4))],
        vmem=8,
    )(step[None, :], base, kept, received, residual)
    norms = lax.all_to_all(norms, RING, 0, 0)
    direction_next = call(
        direction_kernel,
        shape((leaves, samples, points), BF),
        MIB,
        2 * MIB,
        in_specs=[vmem] * 3,
        out_specs=anywhere,
        scratch_shapes=[
            pltpu.VMEM((leaves, samples, points), BF),
            pltpu.SemaphoreType.DMA((4,)),
        ],
        vmem=8,
    )(norms, updated, direction)
    return (residual_next, direction_next)


def solution(mesh):
    in_specs = (
        P(("groups", "blk", "leaf"), "sample", None),
        P(("groups", "blk", "leaf"), "sample", None),
        P(("groups", "sample")),
        P(("groups", "blk", "leaf"), None, None),
        P(("groups", "blk", "leaf"), None),
        P(("groups", "blk", "leaf"), None, None),
        P(("groups", "blk", "leaf"), None, None),
        P(("groups", "blk", "leaf"), None, None),
        P(("groups", "blk", "leaf"), None),
        P(("groups", "blk", "leaf"), None),
        P(("groups", "blk", "leaf"), None, None, None),
        P(("groups", "blk"), None),
        P(("groups", "blk"), None, None, None),
    )
    out_specs = (
        P(("groups", "blk", "leaf"), "sample", None),
        P(("groups", "blk", "leaf"), "sample", None),
    )
    return jax.shard_map(
        on_device, mesh=mesh, in_specs=in_specs, out_specs=out_specs, check_vma=False
    )
```

```python
import functools
import math

import jax
import jax.numpy as jnp
from jax import lax
from jax.experimental import pallas as pl
from jax.experimental.pallas import tpu as pltpu
from jax.sharding import PartitionSpec as P

LEAF_DEV = 16

ROOT_THREE = math.sqrt(3.0)
LENGTH = 0.3
AMPLITUDE = 0.25
NUGGET = 0.5
SPREAD = 0.5 / LEAF_DEV
KAPPA = (ROOT_THREE / LENGTH) ** 2
LOG2E = 1.4426950408889634

RING = ("blk", "leaf")
BF = jnp.bfloat16
F32 = jnp.float32
MIB = 1 << 20


def shifted(array, axis, by):
    if isinstance(axis, tuple):
        count = math.prod(lax.axis_size(name) for name in axis)
    else:
        count = lax.axis_size(axis)
    return lax.ppermute(array, axis, [(i, (i + by) % count) for i in range(count)])


def partner(array):
    return lax.ppermute(array, "sample", [(0, 1), (1, 0)])


def ordered(array, *first):
    return lax.optimization_barrier((array,) + first)[0]


def column(row):
    size = row.shape[1]
    shape = (size, size)
    here = lax.broadcasted_iota(jnp.int32, shape, 0) == lax.broadcasted_iota(jnp.int32, shape, 1)
    return jnp.sum(jnp.where(here, row, 0.0), axis=1, keepdims=True)


def in_hbm(*arrays):
    return [pltpu.with_memory_space_constraint(array, pltpu.HBM) for array in arrays]


def thirds(value):
    high = value.astype(BF).astype(F32)
    rest = value - high
    middle = rest.astype(BF).astype(F32)
    return high, middle, rest - middle


def nt(left, right):
    return lax.dot_general(left, right, (((1,), (1,)), ((), ())), preferred_element_type=F32)


def nn(left, right):
    return jnp.dot(left, right, preferred_element_type=F32)


def call(kernel, outs, flops, moved, vmem=40, **kwargs):
    return pl.pallas_call(
        kernel,
        out_shape=outs,
        compiler_params=pltpu.CompilerParams(vmem_limit_bytes=vmem * MIB),
        cost_estimate=pl.CostEstimate(flops=flops, bytes_accessed=moved, transcendentals=0),
        **kwargs,
    )


def up_kernel(order_h, basis_h, direction_h, transfer_h, node_h, natural_h, coef, lifted, mark, *scratch):
    mark[...] = jnp.zeros_like(mark)
    order, basis, direction, leaf_transfer, node_transfer, natural, sems = scratch
    leaves, rank, points = basis.shape
    samples = direction.shape[1]
    chunks = sems.shape[1]
    size = leaves // chunks
    whole = [
        pltpu.make_async_copy(order_h, order, sems.at[3, 0]),
        pltpu.make_async_copy(node_h, node_transfer, sems.at[3, 1]),
    ]
    copies = []
    for c in range(chunks):
        part = pl.ds(c * size, size)
        copies.append(
            [
                pltpu.make_async_copy(source.at[part], target.at[part], sems.at[i, c])
                for i, (source, target) in enumerate(
                    ((basis_h, basis), (direction_h, direction), (transfer_h, leaf_transfer))
                )
            ]
        )
    for copy in whole + sum(copies, []):
        copy.start()
    for copy in whole:
        copy.wait()
    rows = lax.broadcasted_iota(jnp.int32, (points, points), 0)
    node = jnp.zeros((samples, rank), F32)
    leaving = []
    for g in range(leaves):
        if g % size == 0:
            for copy in copies[g // size]:
                copy.wait()
        place = jnp.where(rows == order[g : g + 1, :], 1.0, 0.0).astype(BF)
        own = nt(basis[g], place).astype(BF)
        natural[g] = own
        weights = nt(direction[g], own).astype(BF)
        coef[g // 2, :, (g % 2) * rank : (g % 2 + 1) * rank] = weights
        node = node + nt(weights, leaf_transfer[g])
        if g % size == size - 1:
            part = pl.ds(g + 1 - size, size)
            copy = pltpu.make_async_copy(
                natural.at[part], natural_h.at[part], sems.at[4, g // size]
            )
            copy.start()
            leaving.append(copy)
    lifted[...] = nt(node.astype(BF), node_transfer[0])
    for copy in leaving:
        copy.wait()


def features(offsets):
    x, y, z = (offsets[i : i + 1] for i in range(3))
    square = thirds(KAPPA * (x * x + y * y + z * z))
    row = lax.broadcasted_iota(jnp.int32, (8, x.shape[1]), 0)
    packed = jnp.zeros((8, x.shape[1]), F32)
    for i, value in enumerate((x, y, z, jnp.ones_like(x)) + square):
        packed = jnp.where(row == i, value, packed)
    return packed.astype(BF)


def spread_features(offsets):
    lane = lax.broadcasted_iota(jnp.int32, (8, 128), 1)
    source = jnp.where(
        lane < 9,
        lane // 3,
        jnp.where(lane < 12, lane - 5, jnp.where(lane < 16, 7, jnp.where(lane < 64, 3, 0))),
    )
    source = jnp.where(lane < 112, source, 7)
    row = lax.broadcasted_iota(jnp.int32, (8, 128), 0)
    pick = jnp.where((row == source) & (row < 7), 1.0, 0.0).astype(BF)
    return lax.dot_general(
        features(offsets), pick, (((0,), (0,)), ((), ())), preferred_element_type=F32
    ).astype(BF)


def tile_kernel(start, near_h, _, *refs):
    if start == 0:
        own_h, prev, after, tiles, mark, spread_x, plain, own, near, sem = refs
        offered = pltpu.make_async_copy(own_h, own, sem.at[1])
        offered.start()
    else:
        plain, spread_x, tiles, mark, near, sem = refs
        own = plain
    listed = pltpu.make_async_copy(near_h, near, sem.at[0])
    listed.start()
    mark[...] = jnp.zeros_like(mark)
    count = tiles.shape[0]
    entries = near.shape[1]
    points = own.shape[2]
    leaves = own.shape[1]
    total = leaves * lax.axis_size("blk") * lax.axis_size("leaf")
    device = lax.axis_index("blk") * lax.axis_size("leaf") + lax.axis_index("leaf")
    anchor = (device - 1) * leaves
    if start == 0:
        offered.wait()
        for side, ref in enumerate((prev, own, after)):
            offsets = ref[...].astype(F32)
            for j in range(leaves):
                spread_x[side * leaves + j] = spread_features(offsets[:, j])
            if side == 1:
                plain[...] = offsets
    listed.wait()
    row = lax.broadcasted_iota(jnp.int32, (16, points), 0)
    lane = lax.broadcasted_iota(jnp.int32, (1, 128), 1)

    def leaf(i, carry):
        g = lax.axis_index("sample") * (leaves // 2) + start + i
        x, y, z = (plain[k, pl.ds(g, 1), :] for k in range(3))
        first = jnp.where((row >= 9) & (row < 12), 1.0, jnp.zeros((16, points), F32))
        at = 0
        for value in (x, y, z):
            for part in thirds(value * (-2.0 * KAPPA)):
                first = jnp.where(row == at, part, first)
                at += 1
        slots = []
        gap = jnp.zeros((16, points), F32)
        for e in range(entries):
            slot = lax.rem(near[g, e] - anchor + 2 * total, total)
            slots.append(slot)
            gap = jnp.where(row == e, (leaves + g - slot).astype(F32) * SPREAD, gap)
        moved = x + gap
        fixed = thirds(KAPPA * (moved * moved + y * y + z * z))
        gaps = thirds(gap * (-2.0 * KAPPA))
        weights = jnp.concatenate(
            [part.astype(BF) for part in (first,) + fixed + gaps + (jnp.zeros_like(first),)],
            axis=0,
        )
        for e in range(entries):
            keep = jnp.where((lane < 16) | (lane % 16 == e), 1.0, 0.0).astype(BF)
            square = jnp.maximum(nn(spread_x[slots[e]] * keep, weights), 1e-30)
            scaled = square * lax.rsqrt(square)
            value = (1.0 + scaled) * jnp.exp2(scaled * (-LOG2E))
            tiles[i, e * points : (e + 1) * points, :] = value.astype(BF)
        return carry

    lax.fori_loop(0, count, leaf, 0)


def after_kernel(_, source, target):
    target[...] = source[...]


def collect_kernel(*refs):
    terms, together = refs[:-1], refs[-1]
    for i, term in enumerate(terms):
        together[i] = term[...]


def window_kernel(given, before, after, *refs):
    terms, (window, sent, tops) = refs[:-3], refs[-3:]
    total = terms[0][...]
    for term in terms[1:]:
        total = total + term[...]
    tops[...] = total.astype(tops.dtype)
    sent[...] = given[...]
    rows, _, lanes = before.shape
    rank = lanes // 2
    for side, packed in enumerate((before, after)):
        for g in range(2 * rows):
            part = packed[g // 2, :, (g % 2) * rank : (g % 2 + 1) * rank]
            window[side * 2 * rows + g] = part


def down_kernel(*refs):
    clusters = lax.axis_size("blk")
    tops, window, leaf_transfer, coupling, natural, direction = refs[:6]
    sources, base, targets, sems = refs[6:10], refs[10], refs[11:15], refs[15]
    top_list, coupling_list, top_coupling, node_transfer = targets
    leaves, samples, points = direction.shape
    rank = natural.shape[1]
    here = lax.axis_index("blk")
    total = leaves * clusters * lax.axis_size("leaf")
    anchor = (here * lax.axis_size("leaf") + lax.axis_index("leaf") - 1) * leaves
    copies = [
        pltpu.make_async_copy(source, target, sems.at[i])
        for i, (source, target) in enumerate(zip(sources, targets))
    ]
    for copy in copies:
        copy.start()
    for copy in copies:
        copy.wait()
    incoming = jnp.zeros((samples, rank), F32)
    for e in range(top_list.shape[1]):
        place = lax.rem(here - top_list[0, e] + clusters, clusters)
        incoming = incoming + nt(tops[place], top_coupling[0, e])
    down = nn(incoming.astype(BF), node_transfer[0]).astype(BF)
    for g in range(leaves):
        inward = nn(down, leaf_transfer[g])
        rows = []
        for c in range(coupling_list.shape[0]):
            slot = lax.rem(coupling_list[c, g] - anchor + 2 * total, total)
            slot = jnp.where(slot >= 2 * leaves, slot - leaves, slot)
            slot = jnp.minimum(slot, 2 * leaves - 1)
            rows.append(window[slot])
        columns = [coupling[g, c] for c in range(coupling_list.shape[0])]
        inward = inward + nt(jnp.concatenate(rows, axis=1), jnp.concatenate(columns, axis=1))
        far = nn(inward.astype(BF), natural[g])
        base[g] = NUGGET * direction[g].astype(F32) + far


def near_kernel(near_h, *refs):
    pieces, tiles, (kept, given, mark, window, near, sems) = refs[:6], refs[6:8], refs[-6:]
    mark[...] = jnp.zeros_like(mark)
    leaves = window.shape[0] // 3
    samples = kept.shape[1]
    total = leaves * lax.axis_size("blk") * lax.axis_size("leaf")
    device = lax.axis_index("blk") * lax.axis_size("leaf") + lax.axis_index("leaf")
    anchor = (device - 1) * leaves
    copies = [pltpu.make_async_copy(near_h, near, sems.at[6])]
    for i, piece in enumerate(pieces):
        side, columns = i // 2, i % 2
        copies.append(
            pltpu.make_async_copy(
                piece,
                window.at[
                    side * leaves : (side + 1) * leaves,
                    columns * samples : (columns + 1) * samples,
                ],
                sems.at[i],
            )
        )
    for copy in copies:
        copy.start()
    for copy in copies:
        copy.wait()
    at = 0
    for part in tiles:

        def leaf(i, carry, part=part, at=at):
            g = lax.axis_index("sample") * kept.shape[0] + at + i
            values = []
            for e in range(near.shape[1]):
                values.append(window[lax.rem(near[g, e] - anchor + 2 * total, total)])
            field = nn(jnp.concatenate(values, axis=1), part[i]) * AMPLITUDE
            kept[at + i] = field[:samples]
            given[at + i] = field[samples:].astype(BF)
            return carry

        lax.fori_loop(0, part.shape[0], leaf, 0)
        at += part.shape[0]


def residual_kernel(step, base, kept, received, residual, updated_h, updated, norms, sems):
    half = kept.shape[0]
    chunks = sems.shape[1]
    size = half // chunks
    leaving = []
    for c in range(chunks):
        for k in range(2):
            part = pl.ds(k * half + c * size, size)
            leaving.append(
                pltpu.make_async_copy(updated.at[part], updated_h.at[part], sems.at[k, c])
            )
    core = lax.axis_index("sample")
    steps = column(step[...])
    totals = [jnp.zeros((step.shape[1], 1), F32)] * 2
    for i in range(half):
        for theirs in range(2):
            g = (core ^ theirs) * half + i
            near = received[i].astype(F32) if theirs else kept[i]
            old = residual[g]
            new = old - steps * (base[g] + near)
            updated[g] = new
            for k, value in enumerate((old, new)):
                totals[k] = totals[k] + jnp.sum(value * value, axis=1, keepdims=True)
        if i % size == size - 1:
            for k in range(2):
                leaving[2 * (i // size) + k].start()
    samples = steps.shape[0]
    lane = lax.broadcasted_iota(jnp.int32, (samples, 128), 1)
    sub = lax.broadcasted_iota(jnp.int32, (samples, 128), 0)
    rows = [jnp.sum(jnp.where(lane == sub, part, 0.0), axis=0, keepdims=True) for part in totals]
    row = lax.broadcasted_iota(jnp.int32, norms.shape[1:], 0)
    packed = jnp.where(row == 0, rows[0], jnp.where(row == 1, rows[1], 0.0))
    for i in range(norms.shape[0]):
        norms[i] = packed
    for copy in leaving:
        copy.wait()


def direction_kernel(norms, updated, direction, result, held, sems):
    leaves, samples, points = updated.shape
    sums = norms[0]
    for i in range(1, norms.shape[0]):
        sums = sums + norms[i]
    ratio = column((sums[1:2, :] / sums[0:1, :])[:, :samples])
    chunks = sems.shape[0]
    size = leaves // chunks
    copies = []
    for c in range(chunks):
        for g in range(c * size, (c + 1) * size):
            held[g] = (updated[g] + ratio * direction[g].astype(F32)).astype(BF)
        part = pl.ds(c * size, size)
        copies.append(pltpu.make_async_copy(held.at[part], result.at[part], sems.at[c]))
        copies[-1].start()
    for copy in copies:
        copy.wait()


def on_device(
    residual,
    direction,
    step,
    coords,
    order,
    basis,
    leaf_transfer,
    node_transfer,
    near_list,
    coupling_list,
    coupling,
    top_list,
    top_coupling,
):
    leaves, samples, points = direction.shape
    rank = basis.shape[1]
    entries = near_list.shape[1]
    half = leaves // 2
    blk_count = lax.axis_size("blk")
    leaf_count = lax.axis_size("leaf")
    shape = jax.ShapeDtypeStruct
    token = shape((8, 128), F32)
    vmem = pl.BlockSpec(memory_space=pltpu.VMEM)
    anywhere = pl.BlockSpec(memory_space=pl.ANY)
    hbm = pl.BlockSpec(memory_space=pltpu.HBM)

    coords = jnp.transpose(coords, (1, 0, 2))
    coords_prev = shifted(coords, RING, 1)
    coords_after = shifted(coords, RING, -1)
    travelling, first = lax.optimization_barrier((direction, order, coords_prev, coords_after))[:2]
    direction_prev = shifted(travelling, RING, 1)
    direction_after = shifted(travelling, RING, -1)
    natural, coef, lifted, up_mark = call(
        up_kernel,
        (
            pltpu.HBM((leaves, rank, points), BF),
            shape((leaves // 2, samples, 2 * rank), BF),
            shape((samples, rank), F32),
            token,
        ),
        4 * leaves * rank * points * points,
        6 * MIB,
        in_specs=[hbm] * 5,
        out_specs=(hbm, vmem, vmem, vmem),
        scratch_shapes=[
            pltpu.VMEM(order.shape, jnp.int32),
            pltpu.VMEM(basis.shape, BF),
            pltpu.VMEM(direction.shape, BF),
            pltpu.VMEM(leaf_transfer.shape, BF),
            pltpu.VMEM(node_transfer.shape, BF),
            pltpu.VMEM(basis.shape, BF),
            pltpu.SemaphoreType.DMA((5, 4)),
        ],
        vmem=8,
    )(*in_hbm(first, basis, direction, leaf_transfer, node_transfer))

    def make_tiles(start, done, *operands):
        count = half // 2
        outs = (pltpu.VMEM((count, entries * points, points), BF), token)
        if start == 0:
            outs += (shape((3 * leaves, points, 128), BF), shape(coords.shape, F32))
        return call(
            functools.partial(tile_kernel, start),
            outs,
            40 * count * entries * points * points,
            count * entries * points * points * (16 if start == 0 else 1),
            in_specs=[hbm, anywhere, hbm if start == 0 else vmem] + [vmem] * (len(operands) - 1),
            out_specs=(vmem,) * len(outs),
            scratch_shapes=[pltpu.VMEM(coords.shape, BF)] * (start == 0)
            + [pltpu.SMEM(near_list.shape, jnp.int32), pltpu.SemaphoreType.DMA((2,))],
            vmem=8,
        )(*in_hbm(near_list), done, *operands)

    coef_prev = shifted(coef, RING, 1)
    coef_after = shifted(coef, RING, -1)
    tiles_low, low_mark, spread_x, plain = make_tiles(
        0, up_mark, *in_hbm(coords), coords_prev, coords_after
    )
    leaving = call(
        after_kernel,
        shape((samples, rank), F32),
        MIB,
        MIB,
        in_specs=[anywhere, vmem],
        out_specs=vmem,
        vmem=4,
    )(low_mark, lifted)
    if blk_count <= 8:
        others = [shifted(leaving, "blk", by) for by in range(1, blk_count)]
    else:
        others = lax.all_gather(leaving[None], "blk", axis=0, tiled=True)
        places = jnp.mod(lax.axis_index("blk") - jnp.arange(blk_count, dtype=jnp.int32), blk_count)
        others = list(others[places][1:])
    tiles_high, high_mark = make_tiles(half // 2, low_mark, plain, spread_x)
    direction_other = partner(ordered(direction, high_mark, *others))
    direction_prev = ordered(direction_prev, high_mark, *others)
    direction_after = ordered(direction_after, high_mark, *others)
    together = call(
        collect_kernel,
        shape((blk_count, samples, rank), F32),
        MIB,
        MIB,
        in_specs=[vmem] * blk_count,
        out_specs=vmem,
        vmem=4,
    )(lifted, *others)
    terms = [shifted(together, "leaf", by) for by in range(1, leaf_count)]
    kept, given, near_mark = call(
        near_kernel,
        (shape((half, samples, points), F32), shape((half, samples, points), BF), token),
        MIB,
        MIB,
        in_specs=[hbm] + [anywhere] * 6 + [vmem] * 2,
        out_specs=(vmem,) * 3,
        scratch_shapes=[
            pltpu.VMEM((3 * leaves, 2 * samples, points), BF),
            pltpu.SMEM(near_list.shape, jnp.int32),
            pltpu.SemaphoreType.DMA((7,)),
        ],
        vmem=8,
    )(
        *in_hbm(near_list),
        direction_prev,
        partner(direction_prev),
        *in_hbm(direction),
        direction_other,
        direction_after,
        partner(direction_after),
        tiles_low,
        tiles_high,
    )

    coef_window, given, tops = call(
        window_kernel,
        (
            shape((2 * leaves, samples, rank), BF),
            shape((half, samples, points), BF),
            shape((blk_count, samples, rank), BF),
        ),
        MIB,
        MIB,
        in_specs=[vmem] * (3 + leaf_count),
        out_specs=(vmem,) * 3,
        vmem=8,
    )(given, coef_prev, coef_after, together, *terms)
    arrays = (top_list, coupling_list.T, top_coupling, node_transfer)
    spaces = (pltpu.SMEM,) * 2 + (pltpu.VMEM,) * 2
    whole = shape((leaves, samples, points), F32)
    base = call(
        down_kernel,
        whole,
        2 * leaves * samples * rank * (points + 9 * rank),
        8 * MIB,
        in_specs=[vmem] * 6 + [hbm] * 4,
        out_specs=vmem,
        scratch_shapes=[space(array.shape, array.dtype) for space, array in zip(spaces, arrays)]
        + [pltpu.SemaphoreType.DMA((4,))],
        vmem=10,
    )(
        tops,
        coef_window,
        leaf_transfer,
        coupling,
        natural,
        direction,
        *in_hbm(*arrays),
    )
    received = partner(given)

    devices = blk_count * leaf_count
    residual_next, updated, norms = call(
        residual_kernel,
        (whole, whole, shape((devices, 8, 128), F32)),
        4 * MIB,
        5 * MIB,
        in_specs=[vmem] * 5,
        out_specs=(hbm, vmem, vmem),
        scratch_shapes=[pltpu.SemaphoreType.DMA((2, 4))],
        vmem=8,
    )(step[None, :], base, kept, received, residual)
    norms = lax.all_to_all(norms, RING, 0, 0)
    direction_next = call(
        direction_kernel,
        shape((leaves, samples, points), BF),
        MIB,
        2 * MIB,
        in_specs=[vmem] * 3,
        out_specs=anywhere,
        scratch_shapes=[
            pltpu.VMEM((leaves, samples, points), BF),
            pltpu.SemaphoreType.DMA((4,)),
        ],
        vmem=8,
    )(norms, updated, direction)
    return (residual_next, direction_next)


def solution(mesh):
    in_specs = (
        P(("groups", "blk", "leaf"), "sample", None),
        P(("groups", "blk", "leaf"), "sample", None),
        P(("groups", "sample")),
        P(("groups", "blk", "leaf"), None, None),
        P(("groups", "blk", "leaf"), None),
        P(("groups", "blk", "leaf"), None, None),
        P(("groups", "blk", "leaf"), None, None),
        P(("groups", "blk", "leaf"), None, None),
        P(("groups", "blk", "leaf"), None),
        P(("groups", "blk", "leaf"), None),
        P(("groups", "blk", "leaf"), None, None, None),
        P(("groups", "blk"), None),
        P(("groups", "blk"), None, None, None),
    )
    out_specs = (
        P(("groups", "blk", "leaf"), "sample", None),
        P(("groups", "blk", "leaf"), "sample", None),
    )
    return jax.shard_map(
        on_device, mesh=mesh, in_specs=in_specs, out_specs=out_specs, check_vma=False
    )
```

```python
import functools
import math

import jax
import jax.numpy as jnp
from jax import lax
from jax.experimental import pallas as pl
from jax.experimental.pallas import tpu as pltpu
from jax.sharding import PartitionSpec as P

LEAF_DEV = 16

ROOT_THREE = math.sqrt(3.0)
LENGTH = 0.3
AMPLITUDE = 0.25
NUGGET = 0.5
SPREAD = 0.5 / LEAF_DEV
KAPPA = (ROOT_THREE / LENGTH) ** 2
LOG2E = 1.4426950408889634

RING = ("blk", "leaf")
BF = jnp.bfloat16
F32 = jnp.float32
MIB = 1 << 20


def shifted(array, axis, by):
    if isinstance(axis, tuple):
        count = math.prod(lax.axis_size(name) for name in axis)
    else:
        count = lax.axis_size(axis)
    return lax.ppermute(array, axis, [(i, (i + by) % count) for i in range(count)])


def partner(array):
    return lax.ppermute(array, "sample", [(0, 1), (1, 0)])


def ordered(array, *first):
    return lax.optimization_barrier((array,) + first)[0]


def column(row):
    size = row.shape[1]
    shape = (size, size)
    here = lax.broadcasted_iota(jnp.int32, shape, 0) == lax.broadcasted_iota(jnp.int32, shape, 1)
    return jnp.sum(jnp.where(here, row, 0.0), axis=1, keepdims=True)


def in_hbm(*arrays):
    return [pltpu.with_memory_space_constraint(array, pltpu.HBM) for array in arrays]


def thirds(value):
    high = value.astype(BF).astype(F32)
    rest = value - high
    middle = rest.astype(BF).astype(F32)
    return high, middle, rest - middle


def nt(left, right):
    return lax.dot_general(left, right, (((1,), (1,)), ((), ())), preferred_element_type=F32)


def nn(left, right):
    return jnp.dot(left, right, preferred_element_type=F32)


def call(kernel, outs, flops, moved, vmem=40, **kwargs):
    return pl.pallas_call(
        kernel,
        out_shape=outs,
        compiler_params=pltpu.CompilerParams(vmem_limit_bytes=vmem * MIB),
        cost_estimate=pl.CostEstimate(flops=flops, bytes_accessed=moved, transcendentals=0),
        **kwargs,
    )


def up_kernel(order_h, basis_h, direction_h, transfer_h, node_h, natural_h, coef, lifted, mark, *scratch):
    mark[...] = jnp.zeros_like(mark)
    order, basis, direction, leaf_transfer, node_transfer, natural, sems = scratch
    leaves, rank, points = basis.shape
    samples = direction.shape[1]
    chunks = sems.shape[1]
    size = leaves // chunks
    whole = [
        pltpu.make_async_copy(order_h, order, sems.at[3, 0]),
        pltpu.make_async_copy(node_h, node_transfer, sems.at[3, 1]),
    ]
    copies = []
    for c in range(chunks):
        part = pl.ds(c * size, size)
        copies.append(
            [
                pltpu.make_async_copy(source.at[part], target.at[part], sems.at[i, c])
                for i, (source, target) in enumerate(
                    ((basis_h, basis), (direction_h, direction), (transfer_h, leaf_transfer))
                )
            ]
        )
    for copy in whole + sum(copies, []):
        copy.start()
    for copy in whole:
        copy.wait()
    rows = lax.broadcasted_iota(jnp.int32, (points, points), 0)
    node = jnp.zeros((samples, rank), F32)
    leaving = []
    for g in range(leaves):
        if g % size == 0:
            for copy in copies[g // size]:
                copy.wait()
        place = jnp.where(rows == order[g : g + 1, :], 1.0, 0.0).astype(BF)
        own = nt(basis[g], place).astype(BF)
        natural[g] = own
        weights = nt(direction[g], own).astype(BF)
        coef[g // 2, :, (g % 2) * rank : (g % 2 + 1) * rank] = weights
        node = node + nt(weights, leaf_transfer[g])
        if g % size == size - 1:
            part = pl.ds(g + 1 - size, size)
            copy = pltpu.make_async_copy(
                natural.at[part], natural_h.at[part], sems.at[4, g // size]
            )
            copy.start()
            leaving.append(copy)
    lifted[...] = nt(node.astype(BF), node_transfer[0])
    for copy in leaving:
        copy.wait()


def features(offsets):
    x, y, z = (offsets[i : i + 1] for i in range(3))
    square = thirds(KAPPA * (x * x + y * y + z * z))
    row = lax.broadcasted_iota(jnp.int32, (8, x.shape[1]), 0)
    packed = jnp.zeros((8, x.shape[1]), F32)
    for i, value in enumerate((x, y, z, jnp.ones_like(x)) + square):
        packed = jnp.where(row == i, value, packed)
    return packed.astype(BF)


def spread_features(offsets):
    lane = lax.broadcasted_iota(jnp.int32, (8, 128), 1)
    source = jnp.where(
        lane < 9,
        lane // 3,
        jnp.where(lane < 12, lane - 5, jnp.where(lane < 16, 7, jnp.where(lane < 64, 3, 0))),
    )
    source = jnp.where(lane < 112, source, 7)
    row = lax.broadcasted_iota(jnp.int32, (8, 128), 0)
    pick = jnp.where((row == source) & (row < 7), 1.0, 0.0).astype(BF)
    return lax.dot_general(
        features(offsets), pick, (((0,), (0,)), ((), ())), preferred_element_type=F32
    ).astype(BF)


def tile_kernel(start, near_h, _, *refs):
    if start == 0:
        own_h, prev, after, tiles, mark, spread_x, plain, own, near, sem = refs
        offered = pltpu.make_async_copy(own_h, own, sem.at[1])
        offered.start()
    else:
        plain, spread_x, tiles, mark, near, sem = refs
        own = plain
    listed = pltpu.make_async_copy(near_h, near, sem.at[0])
    listed.start()
    mark[...] = jnp.zeros_like(mark)
    count = tiles.shape[0]
    entries = near.shape[1]
    points = own.shape[2]
    leaves = own.shape[1]
    total = leaves * lax.axis_size("blk") * lax.axis_size("leaf")
    device = lax.axis_index("blk") * lax.axis_size("leaf") + lax.axis_index("leaf")
    anchor = (device - 1) * leaves
    if start == 0:
        offered.wait()
        for side, ref in enumerate((prev, own, after)):
            offsets = ref[...].astype(F32)
            for j in range(leaves):
                spread_x[side * leaves + j] = spread_features(offsets[:, j])
            if side == 1:
                plain[...] = offsets
    listed.wait()
    row = lax.broadcasted_iota(jnp.int32, (16, points), 0)
    lane = lax.broadcasted_iota(jnp.int32, (1, 128), 1)

    def leaf(i, carry):
        g = lax.axis_index("sample") * (leaves // 2) + start + i
        x, y, z = (plain[k, pl.ds(g, 1), :] for k in range(3))
        first = jnp.where((row >= 9) & (row < 12), 1.0, jnp.zeros((16, points), F32))
        at = 0
        for value in (x, y, z):
            for part in thirds(value * (-2.0 * KAPPA)):
                first = jnp.where(row == at, part, first)
                at += 1
        slots = []
        gap = jnp.zeros((16, points), F32)
        for e in range(entries):
            slot = lax.rem(near[g, e] - anchor + 2 * total, total)
            slots.append(slot)
            gap = jnp.where(row == e, (leaves + g - slot).astype(F32) * SPREAD, gap)
        moved = x + gap
        fixed = thirds(KAPPA * (moved * moved + y * y + z * z))
        gaps = thirds(gap * (-2.0 * KAPPA))
        weights = jnp.concatenate(
            [part.astype(BF) for part in (first,) + fixed + gaps + (jnp.zeros_like(first),)],
            axis=0,
        )
        for e in range(entries):
            keep = jnp.where((lane < 16) | (lane % 16 == e), 1.0, 0.0).astype(BF)
            square = jnp.maximum(nn(spread_x[slots[e]] * keep, weights), 1e-30)
            scaled = square * lax.rsqrt(square)
            value = (1.0 + scaled) * jnp.exp2(scaled * (-LOG2E))
            tiles[i, e * points : (e + 1) * points, :] = value.astype(BF)
        return carry

    lax.fori_loop(0, count, leaf, 0)


def after_kernel(_, source, target):
    rank = source.shape[1]
    for i, part in enumerate(thirds(source[...])[:2]):
        target[:, i * rank : (i + 1) * rank] = part.astype(target.dtype)


def collect_kernel(*refs):
    terms, together = refs[:-1], refs[-1]
    for i, term in enumerate(terms):
        together[i] = term[...]


def window_kernel(given, before, after, window, sent):
    sent[...] = given[...]
    rows, _, lanes = before.shape
    rank = lanes // 2
    for side, packed in enumerate((before, after)):
        for g in range(2 * rows):
            part = packed[g // 2, :, (g % 2) * rank : (g % 2 + 1) * rank]
            window[side * 2 * rows + g] = part


def couple_kernel(window, coupling, list_h, part, coupling_list, sem):
    copy = pltpu.make_async_copy(list_h, coupling_list, sem)
    copy.start()
    leaves, count = coupling.shape[:2]
    total = leaves * lax.axis_size("blk") * lax.axis_size("leaf")
    device = lax.axis_index("blk") * lax.axis_size("leaf") + lax.axis_index("leaf")
    anchor = (device - 1) * leaves
    copy.wait()
    for g in range(leaves):
        rows = []
        for c in range(count):
            slot = lax.rem(coupling_list[c, g] - anchor + 2 * total, total)
            slot = jnp.where(slot >= 2 * leaves, slot - leaves, slot)
            slot = jnp.minimum(slot, 2 * leaves - 1)
            rows.append(window[slot])
        columns = [coupling[g, c] for c in range(count)]
        part[g] = nt(jnp.concatenate(rows, axis=1), jnp.concatenate(columns, axis=1))


def down_kernel(*refs):
    terms, refs = refs[: lax.axis_size("leaf")], refs[lax.axis_size("leaf") :]
    part, leaf_transfer, natural, direction = refs[:4]
    sources, base, targets, (tops, sems) = refs[4:7], refs[7], refs[8:11], refs[11:]
    top_list, top_coupling, node_transfer = targets
    copies = [
        pltpu.make_async_copy(source, target, sems.at[i])
        for i, (source, target) in enumerate(zip(sources, targets))
    ]
    for copy in copies:
        copy.start()
    leaves, samples, points = direction.shape
    rank = natural.shape[1]
    clusters = lax.axis_size("blk")
    here = lax.axis_index("blk")
    together = terms[0][...].astype(F32)
    for term in terms[1:]:
        together = together + term[...].astype(F32)
    tops[...] = (together[:, :, :rank] + together[:, :, rank:]).astype(tops.dtype)
    for copy in copies:
        copy.wait()
    incoming = jnp.zeros((samples, rank), F32)
    for e in range(top_list.shape[1]):
        index = lax.rem(here - top_list[0, e] + clusters, clusters)
        incoming = incoming + nt(tops[index], top_coupling[0, e])
    down = nn(incoming.astype(BF), node_transfer[0]).astype(BF)
    for g in range(leaves):
        inward = nn(down, leaf_transfer[g]) + part[g]
        far = nn(inward.astype(BF), natural[g])
        base[g] = NUGGET * direction[g].astype(F32) + far


def near_kernel(near_h, *refs):
    pieces, tiles, (kept, given, mark, window, near, sems) = refs[:6], refs[6:8], refs[-6:]
    mark[...] = jnp.zeros_like(mark)
    leaves = window.shape[0] // 3
    samples = kept.shape[1]
    total = leaves * lax.axis_size("blk") * lax.axis_size("leaf")
    device = lax.axis_index("blk") * lax.axis_size("leaf") + lax.axis_index("leaf")
    anchor = (device - 1) * leaves
    copies = [pltpu.make_async_copy(near_h, near, sems.at[6])]
    for i, piece in enumerate(pieces):
        side, columns = i // 2, i % 2
        copies.append(
            pltpu.make_async_copy(
                piece,
                window.at[
                    side * leaves : (side + 1) * leaves,
                    columns * samples : (columns + 1) * samples,
                ],
                sems.at[i],
            )
        )
    for copy in copies:
        copy.start()
    for copy in copies:
        copy.wait()
    at = 0
    for part in tiles:

        def leaf(i, carry, part=part, at=at):
            g = lax.axis_index("sample") * kept.shape[0] + at + i
            values = []
            for e in range(near.shape[1]):
                values.append(window[lax.rem(near[g, e] - anchor + 2 * total, total)])
            field = nn(jnp.concatenate(values, axis=1), part[i]) * AMPLITUDE
            kept[at + i] = field[:samples]
            given[at + i] = field[samples:].astype(BF)
            return carry

        lax.fori_loop(0, part.shape[0], leaf, 0)
        at += part.shape[0]


def residual_kernel(step, base, kept, received, residual, updated_h, updated, norms, sems):
    half = kept.shape[0]
    chunks = sems.shape[1]
    size = half // chunks
    leaving = []
    for c in range(chunks):
        for k in range(2):
            part = pl.ds(k * half + c * size, size)
            leaving.append(
                pltpu.make_async_copy(updated.at[part], updated_h.at[part], sems.at[k, c])
            )
    core = lax.axis_index("sample")
    steps = column(step[...])
    totals = [jnp.zeros((step.shape[1], 1), F32)] * 2
    for i in range(half):
        for theirs in range(2):
            g = (core ^ theirs) * half + i
            near = received[i].astype(F32) if theirs else kept[i]
            old = residual[g]
            new = old - steps * (base[g] + near)
            updated[g] = new
            for k, value in enumerate((old, new)):
                totals[k] = totals[k] + jnp.sum(value * value, axis=1, keepdims=True)
        if i % size == size - 1:
            for k in range(2):
                leaving[2 * (i // size) + k].start()
    samples = steps.shape[0]
    lane = lax.broadcasted_iota(jnp.int32, (samples, 128), 1)
    sub = lax.broadcasted_iota(jnp.int32, (samples, 128), 0)
    rows = [jnp.sum(jnp.where(lane == sub, part, 0.0), axis=0, keepdims=True) for part in totals]
    row = lax.broadcasted_iota(jnp.int32, norms.shape[1:], 0)
    packed = jnp.where(row == 0, rows[0], jnp.where(row == 1, rows[1], 0.0))
    for i in range(norms.shape[0]):
        norms[i] = packed
    for copy in leaving:
        copy.wait()


def direction_kernel(norms, updated, direction, result, held, sems):
    leaves, samples, points = updated.shape
    sums = norms[0]
    for i in range(1, norms.shape[0]):
        sums = sums + norms[i]
    ratio = column((sums[1:2, :] / sums[0:1, :])[:, :samples])
    chunks = sems.shape[0]
    size = leaves // chunks
    copies = []
    for c in range(chunks):
        for g in range(c * size, (c + 1) * size):
            held[g] = (updated[g] + ratio * direction[g].astype(F32)).astype(BF)
        part = pl.ds(c * size, size)
        copies.append(pltpu.make_async_copy(held.at[part], result.at[part], sems.at[c]))
        copies[-1].start()
    for copy in copies:
        copy.wait()


def on_device(
    residual,
    direction,
    step,
    coords,
    order,
    basis,
    leaf_transfer,
    node_transfer,
    near_list,
    coupling_list,
    coupling,
    top_list,
    top_coupling,
):
    leaves, samples, points = direction.shape
    rank = basis.shape[1]
    entries = near_list.shape[1]
    half = leaves // 2
    blk_count = lax.axis_size("blk")
    leaf_count = lax.axis_size("leaf")
    shape = jax.ShapeDtypeStruct
    token = shape((8, 128), F32)
    vmem = pl.BlockSpec(memory_space=pltpu.VMEM)
    anywhere = pl.BlockSpec(memory_space=pl.ANY)
    hbm = pl.BlockSpec(memory_space=pltpu.HBM)

    coords = jnp.transpose(coords, (1, 0, 2))
    coords_prev = shifted(coords, RING, 1)
    coords_after = shifted(coords, RING, -1)
    travelling, first = lax.optimization_barrier((direction, order, coords_prev, coords_after))[:2]
    direction_prev = shifted(travelling, RING, 1)
    direction_after = shifted(travelling, RING, -1)
    natural, coef, lifted, up_mark = call(
        up_kernel,
        (
            pltpu.HBM((leaves, rank, points), BF),
            shape((leaves // 2, samples, 2 * rank), BF),
            shape((samples, rank), F32),
            token,
        ),
        4 * leaves * rank * points * points,
        6 * MIB,
        in_specs=[hbm] * 5,
        out_specs=(hbm, vmem, vmem, vmem),
        scratch_shapes=[
            pltpu.VMEM(order.shape, jnp.int32),
            pltpu.VMEM(basis.shape, BF),
            pltpu.VMEM(direction.shape, BF),
            pltpu.VMEM(leaf_transfer.shape, BF),
            pltpu.VMEM(node_transfer.shape, BF),
            pltpu.VMEM(basis.shape, BF),
            pltpu.SemaphoreType.DMA((5, 4)),
        ],
        vmem=8,
    )(*in_hbm(first, basis, direction, leaf_transfer, node_transfer))

    def make_tiles(start, done, *operands):
        count = half // 2
        outs = (pltpu.VMEM((count, entries * points, points), BF), token)
        if start == 0:
            outs += (shape((3 * leaves, points, 128), BF), shape(coords.shape, F32))
        return call(
            functools.partial(tile_kernel, start),
            outs,
            40 * count * entries * points * points,
            count * entries * points * points * (16 if start == 0 else 1),
            in_specs=[hbm, anywhere, hbm if start == 0 else vmem] + [vmem] * (len(operands) - 1),
            out_specs=(vmem,) * len(outs),
            scratch_shapes=[pltpu.VMEM(coords.shape, BF)] * (start == 0)
            + [pltpu.SMEM(near_list.shape, jnp.int32), pltpu.SemaphoreType.DMA((2,))],
            vmem=8,
        )(*in_hbm(near_list), done, *operands)

    coef_prev = shifted(coef, RING, 1)
    coef_after = shifted(coef, RING, -1)
    tiles_low, low_mark, spread_x, plain = make_tiles(
        0, up_mark, *in_hbm(coords), coords_prev, coords_after
    )
    leaving = call(
        after_kernel,
        shape((samples, 2 * rank), BF),
        MIB,
        MIB,
        in_specs=[anywhere, vmem],
        out_specs=vmem,
        vmem=4,
    )(low_mark, lifted)
    if blk_count <= 8:
        others = [shifted(leaving, "blk", by) for by in range(1, blk_count)]
    else:
        others = lax.all_gather(leaving[None], "blk", axis=0, tiled=True)
        places = jnp.mod(lax.axis_index("blk") - jnp.arange(blk_count, dtype=jnp.int32), blk_count)
        others = list(others[places][1:])
    tiles_high, high_mark = make_tiles(half // 2, low_mark, plain, spread_x)
    direction_other = partner(ordered(direction, high_mark, *others))
    direction_prev = ordered(direction_prev, high_mark, *others)
    direction_after = ordered(direction_after, high_mark, *others)
    together = call(
        collect_kernel,
        shape((blk_count, samples, 2 * rank), BF),
        MIB,
        MIB,
        in_specs=[vmem] * blk_count,
        out_specs=vmem,
        vmem=4,
    )(leaving, *others)
    terms = [shifted(together, "leaf", by) for by in range(1, leaf_count)]
    kept, given, near_mark = call(
        near_kernel,
        (shape((half, samples, points), F32), shape((half, samples, points), BF), token),
        MIB,
        MIB,
        in_specs=[hbm] + [anywhere] * 6 + [vmem] * 2,
        out_specs=(vmem,) * 3,
        scratch_shapes=[
            pltpu.VMEM((3 * leaves, 2 * samples, points), BF),
            pltpu.SMEM(near_list.shape, jnp.int32),
            pltpu.SemaphoreType.DMA((7,)),
        ],
        vmem=8,
    )(
        *in_hbm(near_list),
        direction_prev,
        partner(direction_prev),
        *in_hbm(direction),
        direction_other,
        direction_after,
        partner(direction_after),
        tiles_low,
        tiles_high,
    )

    coef_window, given = call(
        window_kernel,
        (shape((2 * leaves, samples, rank), BF), shape((half, samples, points), BF)),
        MIB,
        MIB,
        in_specs=[vmem] * 3,
        out_specs=(vmem, vmem),
        vmem=4,
    )(given, coef_prev, coef_after)
    part = call(
        couple_kernel,
        shape((leaves, samples, rank), F32),
        2 * leaves * samples * rank * rank * 8,
        4 * MIB,
        in_specs=[vmem] * 2 + [hbm],
        out_specs=vmem,
        scratch_shapes=[
            pltpu.SMEM(coupling_list.shape[::-1], jnp.int32),
            pltpu.SemaphoreType.DMA,
        ],
        vmem=8,
    )(coef_window, coupling, *in_hbm(coupling_list.T))
    arrays = (top_list, top_coupling, node_transfer)
    spaces = (pltpu.SMEM, pltpu.VMEM, pltpu.VMEM)
    base = call(
        down_kernel,
        shape((leaves, samples, points), F32),
        2 * leaves * samples * rank * (points + rank),
        4 * MIB,
        in_specs=[vmem] * (4 + leaf_count) + [hbm] * 3,
        out_specs=vmem,
        scratch_shapes=[space(array.shape, array.dtype) for space, array in zip(spaces, arrays)]
        + [pltpu.VMEM((blk_count, samples, rank), BF), pltpu.SemaphoreType.DMA((3,))],
        vmem=10,
    )(together, *terms, part, leaf_transfer, natural, direction, *in_hbm(*arrays))
    received = partner(given)

    devices = blk_count * leaf_count
    whole = shape((leaves, samples, points), F32)
    residual_next, updated, norms = call(
        residual_kernel,
        (whole, whole, shape((devices, 8, 128), F32)),
        4 * MIB,
        5 * MIB,
        in_specs=[vmem] * 5,
        out_specs=(hbm, vmem, vmem),
        scratch_shapes=[pltpu.SemaphoreType.DMA((2, 4))],
        vmem=8,
    )(step[None, :], base, kept, received, residual)
    norms = lax.all_to_all(norms, RING, 0, 0)
    direction_next = call(
        direction_kernel,
        shape((leaves, samples, points), BF),
        MIB,
        2 * MIB,
        in_specs=[vmem] * 3,
        out_specs=anywhere,
        scratch_shapes=[
            pltpu.VMEM((leaves, samples, points), BF),
            pltpu.SemaphoreType.DMA((4,)),
        ],
        vmem=8,
    )(norms, updated, direction)
    return (residual_next, direction_next)


def solution(mesh):
    in_specs = (
        P(("groups", "blk", "leaf"), "sample", None),
        P(("groups", "blk", "leaf"), "sample", None),
        P(("groups", "sample")),
        P(("groups", "blk", "leaf"), None, None),
        P(("groups", "blk", "leaf"), None),
        P(("groups", "blk", "leaf"), None, None),
        P(("groups", "blk", "leaf"), None, None),
        P(("groups", "blk", "leaf"), None, None),
        P(("groups", "blk", "leaf"), None),
        P(("groups", "blk", "leaf"), None),
        P(("groups", "blk", "leaf"), None, None, None),
        P(("groups", "blk"), None),
        P(("groups", "blk"), None, None, None),
    )
    out_specs = (
        P(("groups", "blk", "leaf"), "sample", None),
        P(("groups", "blk", "leaf"), "sample", None),
    )
    return jax.shard_map(
        on_device, mesh=mesh, in_specs=in_specs, out_specs=out_specs, check_vma=False
    )
```

```python
import functools
import math

import jax
import jax.numpy as jnp
from jax import lax
from jax.experimental import pallas as pl
from jax.experimental.pallas import tpu as pltpu
from jax.sharding import PartitionSpec as P

LEAF_DEV = 16

ROOT_THREE = math.sqrt(3.0)
LENGTH = 0.3
AMPLITUDE = 0.25
NUGGET = 0.5
SPREAD = 0.5 / LEAF_DEV
KAPPA = (ROOT_THREE / LENGTH) ** 2
LOG2E = 1.4426950408889634

RING = ("blk", "leaf")
BF = jnp.bfloat16
F32 = jnp.float32
MIB = 1 << 20


def shifted(array, axis, by):
    if isinstance(axis, tuple):
        count = math.prod(lax.axis_size(name) for name in axis)
    else:
        count = lax.axis_size(axis)
    return lax.ppermute(array, axis, [(i, (i + by) % count) for i in range(count)])


def partner(array):
    return lax.ppermute(array, "sample", [(0, 1), (1, 0)])


def ordered(array, *first):
    return lax.optimization_barrier((array,) + first)[0]


def column(row):
    size = row.shape[1]
    shape = (size, size)
    here = lax.broadcasted_iota(jnp.int32, shape, 0) == lax.broadcasted_iota(jnp.int32, shape, 1)
    return jnp.sum(jnp.where(here, row, 0.0), axis=1, keepdims=True)


def in_hbm(*arrays):
    return [pltpu.with_memory_space_constraint(array, pltpu.HBM) for array in arrays]


def thirds(value):
    high = value.astype(BF).astype(F32)
    rest = value - high
    middle = rest.astype(BF).astype(F32)
    return high, middle, rest - middle


def nt(left, right):
    return lax.dot_general(left, right, (((1,), (1,)), ((), ())), preferred_element_type=F32)


def nn(left, right):
    return jnp.dot(left, right, preferred_element_type=F32)


def call(kernel, outs, flops, moved, vmem=40, **kwargs):
    return pl.pallas_call(
        kernel,
        out_shape=outs,
        compiler_params=pltpu.CompilerParams(vmem_limit_bytes=vmem * MIB),
        cost_estimate=pl.CostEstimate(flops=flops, bytes_accessed=moved, transcendentals=0),
        **kwargs,
    )


def up_kernel(order_h, basis_h, direction_h, transfer_h, node_h, natural_h, coef, lifted, mark, *scratch):
    mark[...] = jnp.zeros_like(mark)
    order, basis, direction, leaf_transfer, node_transfer, natural, sems = scratch
    leaves, rank, points = basis.shape
    samples = direction.shape[1]
    chunks = sems.shape[1]
    size = leaves // chunks
    whole = [
        pltpu.make_async_copy(order_h, order, sems.at[3, 0]),
        pltpu.make_async_copy(node_h, node_transfer, sems.at[3, 1]),
    ]
    copies = []
    for c in range(chunks):
        part = pl.ds(c * size, size)
        copies.append(
            [
                pltpu.make_async_copy(source.at[part], target.at[part], sems.at[i, c])
                for i, (source, target) in enumerate(
                    ((basis_h, basis), (direction_h, direction), (transfer_h, leaf_transfer))
                )
            ]
        )
    for copy in whole + sum(copies, []):
        copy.start()
    for copy in whole:
        copy.wait()
    rows = lax.broadcasted_iota(jnp.int32, (points, points), 0)
    node = jnp.zeros((samples, rank), F32)
    leaving = []
    for g in range(leaves):
        if g % size == 0:
            for copy in copies[g // size]:
                copy.wait()
        place = jnp.where(rows == order[g : g + 1, :], 1.0, 0.0).astype(BF)
        own = nt(basis[g], place).astype(BF)
        natural[g] = own
        weights = nt(direction[g], own).astype(BF)
        coef[g // 2, :, (g % 2) * rank : (g % 2 + 1) * rank] = weights
        node = node + nt(weights, leaf_transfer[g])
        if g % size == size - 1:
            part = pl.ds(g + 1 - size, size)
            copy = pltpu.make_async_copy(
                natural.at[part], natural_h.at[part], sems.at[4, g // size]
            )
            copy.start()
            leaving.append(copy)
    lifted[...] = nt(node.astype(BF), node_transfer[0])
    for copy in leaving:
        copy.wait()


def features(offsets):
    x, y, z = (offsets[i : i + 1] for i in range(3))
    square = thirds(KAPPA * (x * x + y * y + z * z))
    row = lax.broadcasted_iota(jnp.int32, (8, x.shape[1]), 0)
    packed = jnp.zeros((8, x.shape[1]), F32)
    for i, value in enumerate((x, y, z, jnp.ones_like(x)) + square):
        packed = jnp.where(row == i, value, packed)
    return packed.astype(BF)


def spread_features(offsets):
    lane = lax.broadcasted_iota(jnp.int32, (8, 128), 1)
    source = jnp.where(
        lane < 9,
        lane // 3,
        jnp.where(lane < 12, lane - 5, jnp.where(lane < 16, 7, jnp.where(lane < 64, 3, 0))),
    )
    source = jnp.where(lane < 112, source, 7)
    row = lax.broadcasted_iota(jnp.int32, (8, 128), 0)
    pick = jnp.where((row == source) & (row < 7), 1.0, 0.0).astype(BF)
    return lax.dot_general(
        features(offsets), pick, (((0,), (0,)), ((), ())), preferred_element_type=F32
    ).astype(BF)


def tile_kernel(start, near_h, _, *refs):
    if start == 0:
        own_h, prev, after, tiles, mark, spread_x, plain, own, near, sem = refs
        offered = pltpu.make_async_copy(own_h, own, sem.at[1])
        offered.start()
    else:
        plain, spread_x, tiles, mark, near, sem = refs
        own = plain
    listed = pltpu.make_async_copy(near_h, near, sem.at[0])
    listed.start()
    mark[...] = jnp.zeros_like(mark)
    count = tiles.shape[0]
    entries = near.shape[1]
    points = own.shape[2]
    leaves = own.shape[1]
    total = leaves * lax.axis_size("blk") * lax.axis_size("leaf")
    device = lax.axis_index("blk") * lax.axis_size("leaf") + lax.axis_index("leaf")
    anchor = (device - 1) * leaves
    if start == 0:
        offered.wait()
        for side, ref in enumerate((prev, own, after)):
            offsets = ref[...].astype(F32)
            for j in range(leaves):
                spread_x[side * leaves + j] = spread_features(offsets[:, j])
            if side == 1:
                plain[...] = offsets
    listed.wait()
    row = lax.broadcasted_iota(jnp.int32, (16, points), 0)
    lane = lax.broadcasted_iota(jnp.int32, (1, 128), 1)

    def leaf(i, carry):
        g = lax.axis_index("sample") * (leaves // 2) + start + i
        x, y, z = (plain[k, pl.ds(g, 1), :] for k in range(3))
        first = jnp.where((row >= 9) & (row < 12), 1.0, jnp.zeros((16, points), F32))
        at = 0
        for value in (x, y, z):
            for part in thirds(value * (-2.0 * KAPPA)):
                first = jnp.where(row == at, part, first)
                at += 1
        slots = []
        gap = jnp.zeros((16, points), F32)
        for e in range(entries):
            slot = lax.rem(near[g, e] - anchor + 2 * total, total)
            slots.append(slot)
            gap = jnp.where(row == e, (leaves + g - slot).astype(F32) * SPREAD, gap)
        moved = x + gap
        fixed = thirds(KAPPA * (moved * moved + y * y + z * z))
        gaps = thirds(gap * (-2.0 * KAPPA))
        weights = jnp.concatenate(
            [part.astype(BF) for part in (first,) + fixed + gaps + (jnp.zeros_like(first),)],
            axis=0,
        )
        for e in range(entries):
            keep = jnp.where((lane < 16) | (lane % 16 == e), 1.0, 0.0).astype(BF)
            square = jnp.maximum(nn(spread_x[slots[e]] * keep, weights), 1e-30)
            scaled = square * lax.rsqrt(square)
            value = (1.0 + scaled) * jnp.exp2(scaled * (-LOG2E))
            tiles[i, e * points : (e + 1) * points, :] = value.astype(BF)
        return carry

    lax.fori_loop(0, count, leaf, 0)


def after_kernel(_, source, target):
    rank = source.shape[1]
    for i, part in enumerate(thirds(source[...])[:2]):
        target[:, i * rank : (i + 1) * rank] = part.astype(target.dtype)


def collect_kernel(*refs):
    terms, together = refs[:-1], refs[-1]
    for i, term in enumerate(terms):
        together[i] = term[...]


def top_kernel(_, given, *refs):
    terms, (tops, sent) = refs[:-2], refs[-2:]
    rank = tops.shape[2]
    total = terms[0][...].astype(F32)
    for term in terms[1:]:
        total = total + term[...].astype(F32)
    tops[...] = (total[:, :, :rank] + total[:, :, rank:]).astype(tops.dtype)
    sent[...] = given[...]


def window_kernel(given, before, after, window, sent):
    sent[...] = given[...]
    rows, _, lanes = before.shape
    rank = lanes // 2
    for side, packed in enumerate((before, after)):
        for g in range(2 * rows):
            part = packed[g // 2, :, (g % 2) * rank : (g % 2 + 1) * rank]
            window[side * 2 * rows + g] = part


def couple_kernel(window, coupling, list_h, part, coupling_list, sem):
    copy = pltpu.make_async_copy(list_h, coupling_list, sem)
    copy.start()
    leaves, count = coupling.shape[:2]
    total = leaves * lax.axis_size("blk") * lax.axis_size("leaf")
    device = lax.axis_index("blk") * lax.axis_size("leaf") + lax.axis_index("leaf")
    anchor = (device - 1) * leaves
    copy.wait()
    for g in range(leaves):
        rows = []
        for c in range(count):
            slot = lax.rem(coupling_list[c, g] - anchor + 2 * total, total)
            slot = jnp.where(slot >= 2 * leaves, slot - leaves, slot)
            slot = jnp.minimum(slot, 2 * leaves - 1)
            rows.append(window[slot])
        columns = [coupling[g, c] for c in range(count)]
        part[g] = nt(jnp.concatenate(rows, axis=1), jnp.concatenate(columns, axis=1))


def down_kernel(*refs):
    tops, part, leaf_transfer, natural, direction = refs[:5]
    sources, base, targets, sems = refs[5:8], refs[8], refs[9:12], refs[12]
    top_list, top_coupling, node_transfer = targets
    copies = [
        pltpu.make_async_copy(source, target, sems.at[i])
        for i, (source, target) in enumerate(zip(sources, targets))
    ]
    for copy in copies:
        copy.start()
    leaves, samples, points = direction.shape
    rank = natural.shape[1]
    clusters = lax.axis_size("blk")
    here = lax.axis_index("blk")
    for copy in copies:
        copy.wait()
    incoming = jnp.zeros((samples, rank), F32)
    for e in range(top_list.shape[1]):
        index = lax.rem(here - top_list[0, e] + clusters, clusters)
        incoming = incoming + nt(tops[index], top_coupling[0, e])
    down = nn(incoming.astype(BF), node_transfer[0]).astype(BF)
    for g in range(leaves):
        inward = nn(down, leaf_transfer[g]) + part[g]
        far = nn(inward.astype(BF), natural[g])
        base[g] = NUGGET * direction[g].astype(F32) + far


def near_kernel(near_h, *refs):
    pieces, tiles, (kept, given, mark, window, near, sems) = refs[:6], refs[6:8], refs[-6:]
    mark[...] = jnp.zeros_like(mark)
    leaves = window.shape[0] // 3
    samples = kept.shape[1]
    total = leaves * lax.axis_size("blk") * lax.axis_size("leaf")
    device = lax.axis_index("blk") * lax.axis_size("leaf") + lax.axis_index("leaf")
    anchor = (device - 1) * leaves
    copies = [pltpu.make_async_copy(near_h, near, sems.at[6])]
    for i, piece in enumerate(pieces):
        side, columns = i // 2, i % 2
        copies.append(
            pltpu.make_async_copy(
                piece,
                window.at[
                    side * leaves : (side + 1) * leaves,
                    columns * samples : (columns + 1) * samples,
                ],
                sems.at[i],
            )
        )
    for copy in copies:
        copy.start()
    for copy in copies:
        copy.wait()
    at = 0
    for part in tiles:

        def leaf(i, carry, part=part, at=at):
            g = lax.axis_index("sample") * kept.shape[0] + at + i
            values = []
            for e in range(near.shape[1]):
                values.append(window[lax.rem(near[g, e] - anchor + 2 * total, total)])
            field = nn(jnp.concatenate(values, axis=1), part[i]) * AMPLITUDE
            kept[at + i] = field[:samples]
            given[at + i] = field[samples:].astype(BF)
            return carry

        lax.fori_loop(0, part.shape[0], leaf, 0)
        at += part.shape[0]


def residual_kernel(step, base, kept, received, residual, updated_h, updated, norms, sems):
    half = kept.shape[0]
    chunks = sems.shape[1]
    size = half // chunks
    leaving = []
    for c in range(chunks):
        for k in range(2):
            part = pl.ds(k * half + c * size, size)
            leaving.append(
                pltpu.make_async_copy(updated.at[part], updated_h.at[part], sems.at[k, c])
            )
    core = lax.axis_index("sample")
    steps = column(step[...])
    totals = [jnp.zeros((step.shape[1], 1), F32)] * 2
    for i in range(half):
        for theirs in range(2):
            g = (core ^ theirs) * half + i
            near = received[i].astype(F32) if theirs else kept[i]
            old = residual[g]
            new = old - steps * (base[g] + near)
            updated[g] = new
            for k, value in enumerate((old, new)):
                totals[k] = totals[k] + jnp.sum(value * value, axis=1, keepdims=True)
        if i % size == size - 1:
            for k in range(2):
                leaving[2 * (i // size) + k].start()
    samples = steps.shape[0]
    lane = lax.broadcasted_iota(jnp.int32, (samples, 128), 1)
    sub = lax.broadcasted_iota(jnp.int32, (samples, 128), 0)
    rows = [jnp.sum(jnp.where(lane == sub, part, 0.0), axis=0, keepdims=True) for part in totals]
    row = lax.broadcasted_iota(jnp.int32, norms.shape[1:], 0)
    packed = jnp.where(row == 0, rows[0], jnp.where(row == 1, rows[1], 0.0))
    for i in range(norms.shape[0]):
        norms[i] = packed
    for copy in leaving:
        copy.wait()


def direction_kernel(norms, updated, direction, result, held, sems):
    leaves, samples, points = updated.shape
    sums = norms[0]
    for i in range(1, norms.shape[0]):
        sums = sums + norms[i]
    ratio = column((sums[1:2, :] / sums[0:1, :])[:, :samples])
    chunks = sems.shape[0]
    size = leaves // chunks
    copies = []
    for c in range(chunks):
        for g in range(c * size, (c + 1) * size):
            held[g] = (updated[g] + ratio * direction[g].astype(F32)).astype(BF)
        part = pl.ds(c * size, size)
        copies.append(pltpu.make_async_copy(held.at[part], result.at[part], sems.at[c]))
        copies[-1].start()
    for copy in copies:
        copy.wait()


def on_device(
    residual,
    direction,
    step,
    coords,
    order,
    basis,
    leaf_transfer,
    node_transfer,
    near_list,
    coupling_list,
    coupling,
    top_list,
    top_coupling,
):
    leaves, samples, points = direction.shape
    rank = basis.shape[1]
    entries = near_list.shape[1]
    half = leaves // 2
    blk_count = lax.axis_size("blk")
    leaf_count = lax.axis_size("leaf")
    shape = jax.ShapeDtypeStruct
    token = shape((8, 128), F32)
    vmem = pl.BlockSpec(memory_space=pltpu.VMEM)
    anywhere = pl.BlockSpec(memory_space=pl.ANY)
    hbm = pl.BlockSpec(memory_space=pltpu.HBM)

    coords = jnp.transpose(coords, (1, 0, 2))
    coords_prev = shifted(coords, RING, 1)
    coords_after = shifted(coords, RING, -1)
    travelling, first = lax.optimization_barrier((direction, order, coords_prev, coords_after))[:2]
    direction_prev = shifted(travelling, RING, 1)
    direction_after = shifted(travelling, RING, -1)
    natural, coef, lifted, up_mark = call(
        up_kernel,
        (
            pltpu.HBM((leaves, rank, points), BF),
            shape((leaves // 2, samples, 2 * rank), BF),
            shape((samples, rank), F32),
            token,
        ),
        4 * leaves * rank * points * points,
        6 * MIB,
        in_specs=[hbm] * 5,
        out_specs=(hbm, vmem, vmem, vmem),
        scratch_shapes=[
            pltpu.VMEM(order.shape, jnp.int32),
            pltpu.VMEM(basis.shape, BF),
            pltpu.VMEM(direction.shape, BF),
            pltpu.VMEM(leaf_transfer.shape, BF),
            pltpu.VMEM(node_transfer.shape, BF),
            pltpu.VMEM(basis.shape, BF),
            pltpu.SemaphoreType.DMA((5, 4)),
        ],
        vmem=8,
    )(*in_hbm(first, basis, direction, leaf_transfer, node_transfer))

    def make_tiles(start, done, *operands):
        count = half // 2
        outs = (pltpu.VMEM((count, entries * points, points), BF), token)
        if start == 0:
            outs += (shape((3 * leaves, points, 128), BF), shape(coords.shape, F32))
        return call(
            functools.partial(tile_kernel, start),
            outs,
            40 * count * entries * points * points,
            count * entries * points * points * (16 if start == 0 else 1),
            in_specs=[hbm, anywhere, hbm if start == 0 else vmem] + [vmem] * (len(operands) - 1),
            out_specs=(vmem,) * len(outs),
            scratch_shapes=[pltpu.VMEM(coords.shape, BF)] * (start == 0)
            + [pltpu.SMEM(near_list.shape, jnp.int32), pltpu.SemaphoreType.DMA((2,))],
            vmem=8,
        )(*in_hbm(near_list), done, *operands)

    coef_prev = shifted(coef, RING, 1)
    coef_after = shifted(coef, RING, -1)
    tiles_low, low_mark, spread_x, plain = make_tiles(
        0, up_mark, *in_hbm(coords), coords_prev, coords_after
    )
    leaving = call(
        after_kernel,
        shape((samples, 2 * rank), BF),
        MIB,
        MIB,
        in_specs=[anywhere, vmem],
        out_specs=vmem,
        vmem=4,
    )(low_mark, lifted)
    if blk_count <= 8:
        others = [shifted(leaving, "blk", by) for by in range(1, blk_count)]
    else:
        others = lax.all_gather(leaving[None], "blk", axis=0, tiled=True)
        places = jnp.mod(lax.axis_index("blk") - jnp.arange(blk_count, dtype=jnp.int32), blk_count)
        others = list(others[places][1:])
    tiles_high, high_mark = make_tiles(half // 2, low_mark, plain, spread_x)
    direction_other = partner(ordered(direction, high_mark, *others))
    direction_prev = ordered(direction_prev, high_mark, *others)
    direction_after = ordered(direction_after, high_mark, *others)
    together = call(
        collect_kernel,
        shape((blk_count, samples, 2 * rank), BF),
        MIB,
        MIB,
        in_specs=[vmem] * blk_count,
        out_specs=vmem,
        vmem=4,
    )(leaving, *others)
    terms = [shifted(together, "leaf", by) for by in range(1, leaf_count)]
    kept, given, near_mark = call(
        near_kernel,
        (shape((half, samples, points), F32), shape((half, samples, points), BF), token),
        MIB,
        MIB,
        in_specs=[hbm] + [anywhere] * 6 + [vmem] * 2,
        out_specs=(vmem,) * 3,
        scratch_shapes=[
            pltpu.VMEM((3 * leaves, 2 * samples, points), BF),
            pltpu.SMEM(near_list.shape, jnp.int32),
            pltpu.SemaphoreType.DMA((7,)),
        ],
        vmem=8,
    )(
        *in_hbm(near_list),
        direction_prev,
        partner(direction_prev),
        *in_hbm(direction),
        direction_other,
        direction_after,
        partner(direction_after),
        tiles_low,
        tiles_high,
    )

    coef_window, given = call(
        window_kernel,
        (shape((2 * leaves, samples, rank), BF), shape((half, samples, points), BF)),
        MIB,
        MIB,
        in_specs=[vmem] * 3,
        out_specs=(vmem, vmem),
        vmem=4,
    )(given, coef_prev, coef_after)
    part = call(
        couple_kernel,
        shape((leaves, samples, rank), F32),
        2 * leaves * samples * rank * rank * 8,
        4 * MIB,
        in_specs=[vmem] * 2 + [hbm],
        out_specs=vmem,
        scratch_shapes=[
            pltpu.SMEM(coupling_list.shape[::-1], jnp.int32),
            pltpu.SemaphoreType.DMA,
        ],
        vmem=8,
    )(coef_window, coupling, *in_hbm(coupling_list.T))
    tops, given = call(
        top_kernel,
        (shape((blk_count, samples, rank), BF), shape((half, samples, points), BF)),
        MIB,
        MIB,
        in_specs=[anywhere] + [vmem] * (2 + len(terms)),
        out_specs=(vmem, vmem),
        vmem=8,
    )(part, given, together, *terms)
    arrays = (top_list, top_coupling, node_transfer)
    spaces = (pltpu.SMEM, pltpu.VMEM, pltpu.VMEM)
    base = call(
        down_kernel,
        shape((leaves, samples, points), F32),
        2 * leaves * samples * rank * (points + rank),
        4 * MIB,
        in_specs=[vmem] * 5 + [hbm] * 3,
        out_specs=vmem,
        scratch_shapes=[space(array.shape, array.dtype) for space, array in zip(spaces, arrays)]
        + [pltpu.SemaphoreType.DMA((3,))],
        vmem=10,
    )(tops, part, leaf_transfer, natural, direction, *in_hbm(*arrays))
    received = partner(given)

    devices = blk_count * leaf_count
    whole = shape((leaves, samples, points), F32)
    residual_next, updated, norms = call(
        residual_kernel,
        (whole, whole, shape((devices, 8, 128), F32)),
        4 * MIB,
        5 * MIB,
        in_specs=[vmem] * 5,
        out_specs=(hbm, vmem, vmem),
        scratch_shapes=[pltpu.SemaphoreType.DMA((2, 4))],
        vmem=8,
    )(step[None, :], base, kept, received, residual)
    norms = lax.all_to_all(norms, RING, 0, 0)
    direction_next = call(
        direction_kernel,
        shape((leaves, samples, points), BF),
        MIB,
        2 * MIB,
        in_specs=[vmem] * 3,
        out_specs=anywhere,
        scratch_shapes=[
            pltpu.VMEM((leaves, samples, points), BF),
            pltpu.SemaphoreType.DMA((4,)),
        ],
        vmem=8,
    )(norms, updated, direction)
    return (residual_next, direction_next)


def solution(mesh):
    in_specs = (
        P(("groups", "blk", "leaf"), "sample", None),
        P(("groups", "blk", "leaf"), "sample", None),
        P(("groups", "sample")),
        P(("groups", "blk", "leaf"), None, None),
        P(("groups", "blk", "leaf"), None),
        P(("groups", "blk", "leaf"), None, None),
        P(("groups", "blk", "leaf"), None, None),
        P(("groups", "blk", "leaf"), None, None),
        P(("groups", "blk", "leaf"), None),
        P(("groups", "blk", "leaf"), None),
        P(("groups", "blk", "leaf"), None, None, None),
        P(("groups", "blk"), None),
        P(("groups", "blk"), None, None, None),
    )
    out_specs = (
        P(("groups", "blk", "leaf"), "sample", None),
        P(("groups", "blk", "leaf"), "sample", None),
    )
    return jax.shard_map(
        on_device, mesh=mesh, in_specs=in_specs, out_specs=out_specs, check_vma=False
    )
```

```python
import functools
import math

import jax
import jax.numpy as jnp
from jax import lax
from jax.experimental import pallas as pl
from jax.experimental.pallas import tpu as pltpu
from jax.sharding import PartitionSpec as P

LEAF_DEV = 16

ROOT_THREE = math.sqrt(3.0)
LENGTH = 0.3
AMPLITUDE = 0.25
NUGGET = 0.5
SPREAD = 0.5 / LEAF_DEV
KAPPA = (ROOT_THREE / LENGTH) ** 2
LOG2E = 1.4426950408889634

RING = ("blk", "leaf")
BF = jnp.bfloat16
F32 = jnp.float32
MIB = 1 << 20


def shifted(array, axis, by):
    if isinstance(axis, tuple):
        count = math.prod(lax.axis_size(name) for name in axis)
    else:
        count = lax.axis_size(axis)
    return lax.ppermute(array, axis, [(i, (i + by) % count) for i in range(count)])


def partner(array):
    return lax.ppermute(array, "sample", [(0, 1), (1, 0)])


def ordered(array, *first):
    return lax.optimization_barrier((array,) + first)[0]


def column(row):
    size = row.shape[1]
    shape = (size, size)
    here = lax.broadcasted_iota(jnp.int32, shape, 0) == lax.broadcasted_iota(jnp.int32, shape, 1)
    return jnp.sum(jnp.where(here, row, 0.0), axis=1, keepdims=True)


def in_hbm(*arrays):
    return [pltpu.with_memory_space_constraint(array, pltpu.HBM) for array in arrays]


def thirds(value):
    high = value.astype(BF).astype(F32)
    rest = value - high
    middle = rest.astype(BF).astype(F32)
    return high, middle, rest - middle


def nt(left, right):
    return lax.dot_general(left, right, (((1,), (1,)), ((), ())), preferred_element_type=F32)


def nn(left, right):
    return jnp.dot(left, right, preferred_element_type=F32)


def call(kernel, outs, flops, moved, vmem=40, **kwargs):
    return pl.pallas_call(
        kernel,
        out_shape=outs,
        compiler_params=pltpu.CompilerParams(vmem_limit_bytes=vmem * MIB),
        cost_estimate=pl.CostEstimate(flops=flops, bytes_accessed=moved, transcendentals=0),
        **kwargs,
    )


def load_kernel(*refs):
    count = len(refs) // 2
    sources, targets, sems = refs[:count], refs[count:-1], refs[-1]
    copies = [
        pltpu.make_async_copy(source, target, sems.at[i])
        for i, (source, target) in enumerate(zip(sources, targets))
    ]
    for copy in copies:
        copy.start()
    for copy in copies:
        copy.wait()


def up_kernel(order, basis, direction, leaf_transfer, node_transfer, *refs):
    natural_h, coef, lifted, mark, natural, sems = refs
    mark[...] = jnp.zeros_like(mark)
    leaves, rank, points = basis.shape
    samples = direction.shape[1]
    chunks = sems.shape[0]
    size = leaves // chunks
    rows = lax.broadcasted_iota(jnp.int32, (points, points), 0)
    node = jnp.zeros((samples, rank), F32)
    leaving = []
    for g in range(leaves):
        spot = jnp.where(rows == order[g : g + 1, :], 1.0, 0.0).astype(BF)
        own = nt(basis[g], spot).astype(BF)
        natural[g] = own
        weights = nt(direction[g], own).astype(BF)
        coef[g // 2, :, (g % 2) * rank : (g % 2 + 1) * rank] = weights
        node = node + nt(weights, leaf_transfer[g])
        if g % size == size - 1:
            part = pl.ds(g + 1 - size, size)
            copy = pltpu.make_async_copy(natural.at[part], natural_h.at[part], sems.at[g // size])
            copy.start()
            leaving.append(copy)
    lifted[...] = nt(node.astype(BF), node_transfer[0])
    for copy in leaving:
        copy.wait()


def features(offsets):
    x, y, z = (offsets[i : i + 1] for i in range(3))
    square = thirds(KAPPA * (x * x + y * y + z * z))
    row = lax.broadcasted_iota(jnp.int32, (8, x.shape[1]), 0)
    packed = jnp.zeros((8, x.shape[1]), F32)
    for i, value in enumerate((x, y, z, jnp.ones_like(x)) + square):
        packed = jnp.where(row == i, value, packed)
    return packed.astype(BF)


def spread_features(offsets):
    lane = lax.broadcasted_iota(jnp.int32, (8, 128), 1)
    source = jnp.where(
        lane < 9,
        lane // 3,
        jnp.where(lane < 12, lane - 5, jnp.where(lane < 16, 7, jnp.where(lane < 64, 3, 0))),
    )
    source = jnp.where(lane < 112, source, 7)
    row = lax.broadcasted_iota(jnp.int32, (8, 128), 0)
    pick = jnp.where((row == source) & (row < 7), 1.0, 0.0).astype(BF)
    return lax.dot_general(
        features(offsets), pick, (((0,), (0,)), ((), ())), preferred_element_type=F32
    ).astype(BF)


def tile_kernel(start, near_h, _, *refs):
    if start == 0:
        own_h, prev, after, tiles, mark, spread_x, plain, own, near, sem = refs
        offered = pltpu.make_async_copy(own_h, own, sem.at[1])
        offered.start()
    else:
        plain, spread_x, tiles, mark, near, sem = refs
        own = plain
    listed = pltpu.make_async_copy(near_h, near, sem.at[0])
    listed.start()
    mark[...] = jnp.zeros_like(mark)
    count = tiles.shape[0]
    entries = near.shape[1]
    points = own.shape[2]
    leaves = own.shape[1]
    total = leaves * lax.axis_size("blk") * lax.axis_size("leaf")
    device = lax.axis_index("blk") * lax.axis_size("leaf") + lax.axis_index("leaf")
    anchor = (device - 1) * leaves
    if start == 0:
        offered.wait()
        for side, ref in enumerate((prev, own, after)):
            offsets = ref[...].astype(F32)
            for j in range(leaves):
                spread_x[side * leaves + j] = spread_features(offsets[:, j])
            if side == 1:
                plain[...] = offsets
    listed.wait()
    row = lax.broadcasted_iota(jnp.int32, (16, points), 0)
    lane = lax.broadcasted_iota(jnp.int32, (1, 128), 1)

    def leaf(i, carry):
        g = lax.axis_index("sample") * (leaves // 2) + start + i
        x, y, z = (plain[k, pl.ds(g, 1), :] for k in range(3))
        first = jnp.where((row >= 9) & (row < 12), 1.0, jnp.zeros((16, points), F32))
        at = 0
        for value in (x, y, z):
            for part in thirds(value * (-2.0 * KAPPA)):
                first = jnp.where(row == at, part, first)
                at += 1
        slots = []
        gap = jnp.zeros((16, points), F32)
        for e in range(entries):
            slot = lax.rem(near[g, e] - anchor + 2 * total, total)
            slots.append(slot)
            gap = jnp.where(row == e, (leaves + g - slot).astype(F32) * SPREAD, gap)
        moved = x + gap
        fixed = thirds(KAPPA * (moved * moved + y * y + z * z))
        gaps = thirds(gap * (-2.0 * KAPPA))
        weights = jnp.concatenate(
            [part.astype(BF) for part in (first,) + fixed + gaps + (jnp.zeros_like(first),)],
            axis=0,
        )
        for e in range(entries):
            keep = jnp.where((lane < 16) | (lane % 16 == e), 1.0, 0.0).astype(BF)
            square = jnp.maximum(nn(spread_x[slots[e]] * keep, weights), 1e-30)
            scaled = square * lax.rsqrt(square)
            value = (1.0 + scaled) * jnp.exp2(scaled * (-LOG2E))
            tiles[i, e * points : (e + 1) * points, :] = value.astype(BF)
        return carry

    lax.fori_loop(0, count, leaf, 0)


def after_kernel(_, source, target):
    rank = source.shape[1]
    for i, part in enumerate(thirds(source[...])[:2]):
        target[:, i * rank : (i + 1) * rank] = part.astype(target.dtype)


def collect_kernel(*refs):
    terms, together = refs[:-1], refs[-1]
    for i, term in enumerate(terms):
        together[i] = term[...]


def top_kernel(_, given, *refs):
    terms, (tops, sent) = refs[:-2], refs[-2:]
    rank = tops.shape[2]
    total = terms[0][...].astype(F32)
    for term in terms[1:]:
        total = total + term[...].astype(F32)
    tops[...] = (total[:, :, :rank] + total[:, :, rank:]).astype(tops.dtype)
    sent[...] = given[...]


def window_kernel(given, before, after, window, sent):
    sent[...] = given[...]
    rows, _, lanes = before.shape
    rank = lanes // 2
    for side, packed in enumerate((before, after)):
        for g in range(2 * rows):
            part = packed[g // 2, :, (g % 2) * rank : (g % 2 + 1) * rank]
            window[side * 2 * rows + g] = part


def couple_kernel(window, coupling, list_h, part, coupling_list, sem):
    copy = pltpu.make_async_copy(list_h, coupling_list, sem)
    copy.start()
    leaves, count = coupling.shape[:2]
    total = leaves * lax.axis_size("blk") * lax.axis_size("leaf")
    device = lax.axis_index("blk") * lax.axis_size("leaf") + lax.axis_index("leaf")
    anchor = (device - 1) * leaves
    copy.wait()
    for g in range(leaves):
        rows = []
        for c in range(count):
            slot = lax.rem(coupling_list[c, g] - anchor + 2 * total, total)
            slot = jnp.where(slot >= 2 * leaves, slot - leaves, slot)
            slot = jnp.minimum(slot, 2 * leaves - 1)
            rows.append(window[slot])
        columns = [coupling[g, c] for c in range(count)]
        part[g] = nt(jnp.concatenate(rows, axis=1), jnp.concatenate(columns, axis=1))


def down_kernel(*refs):
    tops, part, leaf_transfer, natural, direction = refs[:5]
    sources, base, targets, sems = refs[5:8], refs[8], refs[9:12], refs[12]
    top_list, top_coupling, node_transfer = targets
    copies = [
        pltpu.make_async_copy(source, target, sems.at[i])
        for i, (source, target) in enumerate(zip(sources, targets))
    ]
    for copy in copies:
        copy.start()
    leaves, samples, points = direction.shape
    rank = natural.shape[1]
    clusters = lax.axis_size("blk")
    here = lax.axis_index("blk")
    for copy in copies:
        copy.wait()
    incoming = jnp.zeros((samples, rank), F32)
    for e in range(top_list.shape[1]):
        index = lax.rem(here - top_list[0, e] + clusters, clusters)
        incoming = incoming + nt(tops[index], top_coupling[0, e])
    down = nn(incoming.astype(BF), node_transfer[0]).astype(BF)
    for g in range(leaves):
        inward = nn(down, leaf_transfer[g]) + part[g]
        far = nn(inward.astype(BF), natural[g])
        base[g] = NUGGET * direction[g].astype(F32) + far


def near_kernel(near_h, *refs):
    pieces, tiles, (kept, given, mark, window, near, sems) = refs[:6], refs[6:8], refs[-6:]
    mark[...] = jnp.zeros_like(mark)
    leaves = window.shape[0] // 3
    samples = kept.shape[1]
    total = leaves * lax.axis_size("blk") * lax.axis_size("leaf")
    device = lax.axis_index("blk") * lax.axis_size("leaf") + lax.axis_index("leaf")
    anchor = (device - 1) * leaves
    copies = [pltpu.make_async_copy(near_h, near, sems.at[6])]
    for i, piece in enumerate(pieces):
        side, columns = i // 2, i % 2
        copies.append(
            pltpu.make_async_copy(
                piece,
                window.at[
                    side * leaves : (side + 1) * leaves,
                    columns * samples : (columns + 1) * samples,
                ],
                sems.at[i],
            )
        )
    for copy in copies:
        copy.start()
    for copy in copies:
        copy.wait()
    at = 0
    for part in tiles:

        def leaf(i, carry, part=part, at=at):
            g = lax.axis_index("sample") * kept.shape[0] + at + i
            values = []
            for e in range(near.shape[1]):
                values.append(window[lax.rem(near[g, e] - anchor + 2 * total, total)])
            field = nn(jnp.concatenate(values, axis=1), part[i]) * AMPLITUDE
            kept[at + i] = field[:samples]
            given[at + i] = field[samples:].astype(BF)
            return carry

        lax.fori_loop(0, part.shape[0], leaf, 0)
        at += part.shape[0]


def residual_kernel(step, base, kept, received, residual, updated_h, updated, norms, sems):
    half = kept.shape[0]
    chunks = sems.shape[1]
    size = half // chunks
    leaving = []
    for c in range(chunks):
        for k in range(2):
            part = pl.ds(k * half + c * size, size)
            leaving.append(
                pltpu.make_async_copy(updated.at[part], updated_h.at[part], sems.at[k, c])
            )
    core = lax.axis_index("sample")
    steps = column(step[...])
    totals = [jnp.zeros((step.shape[1], 1), F32)] * 2
    for i in range(half):
        for theirs in range(2):
            g = (core ^ theirs) * half + i
            near = received[i].astype(F32) if theirs else kept[i]
            old = residual[g]
            new = old - steps * (base[g] + near)
            updated[g] = new
            for k, value in enumerate((old, new)):
                totals[k] = totals[k] + jnp.sum(value * value, axis=1, keepdims=True)
        if i % size == size - 1:
            for k in range(2):
                leaving[2 * (i // size) + k].start()
    samples = steps.shape[0]
    lane = lax.broadcasted_iota(jnp.int32, (samples, 128), 1)
    sub = lax.broadcasted_iota(jnp.int32, (samples, 128), 0)
    rows = [jnp.sum(jnp.where(lane == sub, part, 0.0), axis=0, keepdims=True) for part in totals]
    row = lax.broadcasted_iota(jnp.int32, norms.shape[1:], 0)
    packed = jnp.where(row == 0, rows[0], jnp.where(row == 1, rows[1], 0.0))
    for i in range(norms.shape[0]):
        norms[i] = packed
    for copy in leaving:
        copy.wait()


def direction_kernel(norms, updated, direction, result, held, sems):
    leaves, samples, points = updated.shape
    sums = norms[0]
    for i in range(1, norms.shape[0]):
        sums = sums + norms[i]
    ratio = column((sums[1:2, :] / sums[0:1, :])[:, :samples])
    chunks = sems.shape[0]
    size = leaves // chunks
    copies = []
    for c in range(chunks):
        for g in range(c * size, (c + 1) * size):
            held[g] = (updated[g] + ratio * direction[g].astype(F32)).astype(BF)
        part = pl.ds(c * size, size)
        copies.append(pltpu.make_async_copy(held.at[part], result.at[part], sems.at[c]))
        copies[-1].start()
    for copy in copies:
        copy.wait()


def on_device(
    residual,
    direction,
    step,
    coords,
    order,
    basis,
    leaf_transfer,
    node_transfer,
    near_list,
    coupling_list,
    coupling,
    top_list,
    top_coupling,
):
    leaves, samples, points = direction.shape
    rank = basis.shape[1]
    entries = near_list.shape[1]
    half = leaves // 2
    blk_count = lax.axis_size("blk")
    leaf_count = lax.axis_size("leaf")
    shape = jax.ShapeDtypeStruct
    token = shape((8, 128), F32)
    vmem = pl.BlockSpec(memory_space=pltpu.VMEM)
    anywhere = pl.BlockSpec(memory_space=pl.ANY)
    hbm = pl.BlockSpec(memory_space=pltpu.HBM)

    coords = jnp.transpose(coords, (1, 0, 2))
    coords_prev = shifted(coords, RING, 1)
    coords_after = shifted(coords, RING, -1)
    operands = (order, basis, direction, leaf_transfer, node_transfer)
    resident = call(
        load_kernel,
        tuple(shape(array.shape, array.dtype) for array in operands),
        MIB,
        2 * MIB,
        in_specs=[hbm] * 5,
        out_specs=(vmem,) * 5,
        scratch_shapes=[pltpu.SemaphoreType.DMA((5,))],
        vmem=4,
    )(*in_hbm(*operands))
    travelling = ordered(direction, coords_prev, coords_after, resident[0])
    direction_prev = shifted(travelling, RING, 1)
    direction_after = shifted(travelling, RING, -1)
    natural, coef, lifted, up_mark = call(
        up_kernel,
        (
            pltpu.HBM((leaves, rank, points), BF),
            shape((leaves // 2, samples, 2 * rank), BF),
            shape((samples, rank), F32),
            token,
        ),
        4 * leaves * rank * points * points,
        6 * MIB,
        in_specs=[vmem] * 5,
        out_specs=(hbm, vmem, vmem, vmem),
        scratch_shapes=[pltpu.VMEM(basis.shape, BF), pltpu.SemaphoreType.DMA((4,))],
        vmem=8,
    )(ordered(resident[0], coords_prev, coords_after), *resident[1:])

    def make_tiles(start, done, *operands):
        count = half // 2
        outs = (pltpu.VMEM((count, entries * points, points), BF), token)
        if start == 0:
            outs += (shape((3 * leaves, points, 128), BF), shape(coords.shape, F32))
        return call(
            functools.partial(tile_kernel, start),
            outs,
            40 * count * entries * points * points,
            count * entries * points * points * (16 if start == 0 else 1),
            in_specs=[hbm, anywhere, hbm if start == 0 else vmem] + [vmem] * (len(operands) - 1),
            out_specs=(vmem,) * len(outs),
            scratch_shapes=[pltpu.VMEM(coords.shape, BF)] * (start == 0)
            + [pltpu.SMEM(near_list.shape, jnp.int32), pltpu.SemaphoreType.DMA((2,))],
            vmem=8,
        )(*in_hbm(near_list), done, *operands)

    coef_prev = shifted(coef, RING, 1)
    coef_after = shifted(coef, RING, -1)
    tiles_low, low_mark, spread_x, plain = make_tiles(
        0, up_mark, *in_hbm(coords), coords_prev, coords_after
    )
    leaving = call(
        after_kernel,
        shape((samples, 2 * rank), BF),
        MIB,
        MIB,
        in_specs=[anywhere, vmem],
        out_specs=vmem,
        vmem=4,
    )(low_mark, lifted)
    if blk_count <= 8:
        others = [shifted(leaving, "blk", by) for by in range(1, blk_count)]
    else:
        others = lax.all_gather(leaving[None], "blk", axis=0, tiled=True)
        places = jnp.mod(lax.axis_index("blk") - jnp.arange(blk_count, dtype=jnp.int32), blk_count)
        others = list(others[places][1:])
    tiles_high, high_mark = make_tiles(half // 2, low_mark, plain, spread_x)
    direction_other = partner(ordered(direction, high_mark, *others))
    direction_prev = ordered(direction_prev, high_mark, *others)
    direction_after = ordered(direction_after, high_mark, *others)
    together = call(
        collect_kernel,
        shape((blk_count, samples, 2 * rank), BF),
        MIB,
        MIB,
        in_specs=[vmem] * blk_count,
        out_specs=vmem,
        vmem=4,
    )(leaving, *others)
    terms = [shifted(together, "leaf", by) for by in range(1, leaf_count)]
    kept, given, near_mark = call(
        near_kernel,
        (shape((half, samples, points), F32), shape((half, samples, points), BF), token),
        MIB,
        MIB,
        in_specs=[hbm] + [anywhere] * 6 + [vmem] * 2,
        out_specs=(vmem,) * 3,
        scratch_shapes=[
            pltpu.VMEM((3 * leaves, 2 * samples, points), BF),
            pltpu.SMEM(near_list.shape, jnp.int32),
            pltpu.SemaphoreType.DMA((7,)),
        ],
        vmem=8,
    )(
        *in_hbm(near_list),
        direction_prev,
        partner(direction_prev),
        *in_hbm(direction),
        direction_other,
        direction_after,
        partner(direction_after),
        tiles_low,
        tiles_high,
    )

    coef_window, given = call(
        window_kernel,
        (shape((2 * leaves, samples, rank), BF), shape((half, samples, points), BF)),
        MIB,
        MIB,
        in_specs=[vmem] * 3,
        out_specs=(vmem, vmem),
        vmem=4,
    )(given, coef_prev, coef_after)
    part = call(
        couple_kernel,
        shape((leaves, samples, rank), F32),
        2 * leaves * samples * rank * rank * 8,
        4 * MIB,
        in_specs=[vmem] * 2 + [hbm],
        out_specs=vmem,
        scratch_shapes=[
            pltpu.SMEM(coupling_list.shape[::-1], jnp.int32),
            pltpu.SemaphoreType.DMA,
        ],
        vmem=8,
    )(coef_window, coupling, *in_hbm(coupling_list.T))
    tops, given = call(
        top_kernel,
        (shape((blk_count, samples, rank), BF), shape((half, samples, points), BF)),
        MIB,
        MIB,
        in_specs=[anywhere] + [vmem] * (2 + len(terms)),
        out_specs=(vmem, vmem),
        vmem=8,
    )(part, given, together, *terms)
    arrays = (top_list, top_coupling, node_transfer)
    spaces = (pltpu.SMEM, pltpu.VMEM, pltpu.VMEM)
    base = call(
        down_kernel,
        shape((leaves, samples, points), F32),
        2 * leaves * samples * rank * (points + rank),
        4 * MIB,
        in_specs=[vmem] * 5 + [hbm] * 3,
        out_specs=vmem,
        scratch_shapes=[space(array.shape, array.dtype) for space, array in zip(spaces, arrays)]
        + [pltpu.SemaphoreType.DMA((3,))],
        vmem=10,
    )(tops, part, leaf_transfer, natural, direction, *in_hbm(*arrays))
    received = partner(given)

    devices = blk_count * leaf_count
    whole = shape((leaves, samples, points), F32)
    residual_next, updated, norms = call(
        residual_kernel,
        (whole, whole, shape((devices, 8, 128), F32)),
        4 * MIB,
        5 * MIB,
        in_specs=[vmem] * 5,
        out_specs=(hbm, vmem, vmem),
        scratch_shapes=[pltpu.SemaphoreType.DMA((2, 4))],
        vmem=8,
    )(step[None, :], base, kept, received, residual)
    norms = lax.all_to_all(norms, RING, 0, 0)
    direction_next = call(
        direction_kernel,
        shape((leaves, samples, points), BF),
        MIB,
        2 * MIB,
        in_specs=[vmem] * 3,
        out_specs=anywhere,
        scratch_shapes=[
            pltpu.VMEM((leaves, samples, points), BF),
            pltpu.SemaphoreType.DMA((4,)),
        ],
        vmem=8,
    )(norms, updated, direction)
    return (residual_next, direction_next)


def solution(mesh):
    in_specs = (
        P(("groups", "blk", "leaf"), "sample", None),
        P(("groups", "blk", "leaf"), "sample", None),
        P(("groups", "sample")),
        P(("groups", "blk", "leaf"), None, None),
        P(("groups", "blk", "leaf"), None),
        P(("groups", "blk", "leaf"), None, None),
        P(("groups", "blk", "leaf"), None, None),
        P(("groups", "blk", "leaf"), None, None),
        P(("groups", "blk", "leaf"), None),
        P(("groups", "blk", "leaf"), None),
        P(("groups", "blk", "leaf"), None, None, None),
        P(("groups", "blk"), None),
        P(("groups", "blk"), None, None, None),
    )
    out_specs = (
        P(("groups", "blk", "leaf"), "sample", None),
        P(("groups", "blk", "leaf"), "sample", None),
    )
    return jax.shard_map(
        on_device, mesh=mesh, in_specs=in_specs, out_specs=out_specs, check_vma=False
    )
```

```python
import functools
import math

import jax
import jax.numpy as jnp
from jax import lax
from jax.experimental import pallas as pl
from jax.experimental.pallas import tpu as pltpu
from jax.sharding import PartitionSpec as P

LEAF_DEV = 16

ROOT_THREE = math.sqrt(3.0)
LENGTH = 0.3
AMPLITUDE = 0.25
NUGGET = 0.5
SPREAD = 0.5 / LEAF_DEV
KAPPA = (ROOT_THREE / LENGTH) ** 2
LOG2E = 1.4426950408889634

RING = ("blk", "leaf")
BF = jnp.bfloat16
F32 = jnp.float32
MIB = 1 << 20


def shifted(array, axis, by):
    if isinstance(axis, tuple):
        count = math.prod(lax.axis_size(name) for name in axis)
    else:
        count = lax.axis_size(axis)
    return lax.ppermute(array, axis, [(i, (i + by) % count) for i in range(count)])


def partner(array):
    return lax.ppermute(array, "sample", [(0, 1), (1, 0)])


def ordered(array, *first):
    return lax.optimization_barrier((array,) + first)[0]


def column(row):
    size = row.shape[1]
    shape = (size, size)
    here = lax.broadcasted_iota(jnp.int32, shape, 0) == lax.broadcasted_iota(jnp.int32, shape, 1)
    return jnp.sum(jnp.where(here, row, 0.0), axis=1, keepdims=True)


def in_hbm(*arrays):
    return [pltpu.with_memory_space_constraint(array, pltpu.HBM) for array in arrays]


def thirds(value):
    high = value.astype(BF).astype(F32)
    rest = value - high
    middle = rest.astype(BF).astype(F32)
    return high, middle, rest - middle


def nt(left, right):
    return lax.dot_general(left, right, (((1,), (1,)), ((), ())), preferred_element_type=F32)


def nn(left, right):
    return jnp.dot(left, right, preferred_element_type=F32)


def call(kernel, outs, flops, moved, vmem=40, **kwargs):
    return pl.pallas_call(
        kernel,
        out_shape=outs,
        compiler_params=pltpu.CompilerParams(vmem_limit_bytes=vmem * MIB),
        cost_estimate=pl.CostEstimate(flops=flops, bytes_accessed=moved, transcendentals=0),
        **kwargs,
    )


def load_kernel(*refs):
    count = len(refs) // 2
    sources, targets, sems = refs[:count], refs[count:-1], refs[-1]
    copies = [
        pltpu.make_async_copy(source, target, sems.at[i])
        for i, (source, target) in enumerate(zip(sources, targets))
    ]
    for copy in copies:
        copy.start()
    for copy in copies:
        copy.wait()


def up_kernel(order, basis, direction, leaf_transfer, node_transfer, *refs):
    natural_h, coef, lifted, mark, natural, sems = refs
    mark[...] = jnp.zeros_like(mark)
    leaves, rank, points = basis.shape
    samples = direction.shape[1]
    chunks = sems.shape[0]
    size = leaves // chunks
    rows = lax.broadcasted_iota(jnp.int32, (points, points), 0)
    node = jnp.zeros((samples, rank), F32)
    leaving = []
    for g in range(leaves):
        spot = jnp.where(rows == order[g : g + 1, :], 1.0, 0.0).astype(BF)
        own = nt(basis[g], spot).astype(BF)
        natural[g] = own
        weights = nt(direction[g], own).astype(BF)
        coef[g // 2, :, (g % 2) * rank : (g % 2 + 1) * rank] = weights
        node = node + nt(weights, leaf_transfer[g])
        if g % size == size - 1:
            part = pl.ds(g + 1 - size, size)
            copy = pltpu.make_async_copy(natural.at[part], natural_h.at[part], sems.at[g // size])
            copy.start()
            leaving.append(copy)
    lifted[...] = nt(node.astype(BF), node_transfer[0])
    for copy in leaving:
        copy.wait()


def features(offsets):
    x, y, z = (offsets[i : i + 1] for i in range(3))
    square = thirds(KAPPA * (x * x + y * y + z * z))
    row = lax.broadcasted_iota(jnp.int32, (8, x.shape[1]), 0)
    packed = jnp.zeros((8, x.shape[1]), F32)
    for i, value in enumerate((x, y, z, jnp.ones_like(x)) + square):
        packed = jnp.where(row == i, value, packed)
    return packed.astype(BF)


def spread_features(offsets):
    lane = lax.broadcasted_iota(jnp.int32, (8, 128), 1)
    source = jnp.where(
        lane < 9,
        lane // 3,
        jnp.where(lane < 12, lane - 5, jnp.where(lane < 16, 7, jnp.where(lane < 64, 3, 0))),
    )
    source = jnp.where(lane < 112, source, 7)
    row = lax.broadcasted_iota(jnp.int32, (8, 128), 0)
    pick = jnp.where((row == source) & (row < 7), 1.0, 0.0).astype(BF)
    return lax.dot_general(
        features(offsets), pick, (((0,), (0,)), ((), ())), preferred_element_type=F32
    ).astype(BF)


def tile_kernel(start, near_h, _, *refs):
    if start == 0:
        own_h, prev, after, tiles, mark, spread_x, plain, own, near, sem = refs
        offered = pltpu.make_async_copy(own_h, own, sem.at[1])
        offered.start()
    else:
        plain, spread_x, tiles, mark, near, sem = refs
        own = plain
    listed = pltpu.make_async_copy(near_h, near, sem.at[0])
    listed.start()
    mark[...] = jnp.zeros_like(mark)
    count = tiles.shape[0]
    entries = near.shape[1]
    points = own.shape[2]
    leaves = own.shape[1]
    total = leaves * lax.axis_size("blk") * lax.axis_size("leaf")
    device = lax.axis_index("blk") * lax.axis_size("leaf") + lax.axis_index("leaf")
    anchor = (device - 1) * leaves
    if start == 0:
        offered.wait()
        for side, ref in enumerate((prev, own, after)):
            offsets = ref[...].astype(F32)
            for j in range(leaves):
                spread_x[side * leaves + j] = spread_features(offsets[:, j])
            if side == 1:
                plain[...] = offsets
    listed.wait()
    row = lax.broadcasted_iota(jnp.int32, (16, points), 0)
    lane = lax.broadcasted_iota(jnp.int32, (1, 128), 1)

    def leaf(i, carry):
        g = lax.axis_index("sample") * (leaves // 2) + start + i
        x, y, z = (plain[k, pl.ds(g, 1), :] for k in range(3))
        first = jnp.where((row >= 9) & (row < 12), 1.0, jnp.zeros((16, points), F32))
        at = 0
        for value in (x, y, z):
            for part in thirds(value * (-2.0 * KAPPA)):
                first = jnp.where(row == at, part, first)
                at += 1
        slots = []
        gap = jnp.zeros((16, points), F32)
        for e in range(entries):
            slot = lax.rem(near[g, e] - anchor + 2 * total, total)
            slots.append(slot)
            gap = jnp.where(row == e, (leaves + g - slot).astype(F32) * SPREAD, gap)
        moved = x + gap
        fixed = thirds(KAPPA * (moved * moved + y * y + z * z))
        gaps = thirds(gap * (-2.0 * KAPPA))
        weights = jnp.concatenate(
            [part.astype(BF) for part in (first,) + fixed + gaps + (jnp.zeros_like(first),)],
            axis=0,
        )
        for e in range(entries):
            keep = jnp.where((lane < 16) | (lane % 16 == e), 1.0, 0.0).astype(BF)
            square = jnp.maximum(nn(spread_x[slots[e]] * keep, weights), 1e-30)
            scaled = square * lax.rsqrt(square)
            value = (1.0 + scaled) * jnp.exp2(scaled * (-LOG2E))
            tiles[i, e * points : (e + 1) * points, :] = value.astype(BF)
        return carry

    lax.fori_loop(0, count, leaf, 0)


def after_kernel(_, source, target):
    rank = source.shape[1]
    for i, part in enumerate(thirds(source[...])[:2]):
        target[:, i * rank : (i + 1) * rank] = part.astype(target.dtype)


def collect_kernel(*refs):
    terms, together = refs[:-1], refs[-1]
    at = 0
    for term in terms:
        if len(term.shape) == 2:
            together[at] = term[...]
            at += 1
        else:
            together[at : at + term.shape[0]] = term[...]
            at += term.shape[0]


def top_kernel(_, given, *refs):
    terms, (tops, sent) = refs[:-2], refs[-2:]
    rank = tops.shape[2]
    total = terms[0][...].astype(F32)
    for term in terms[1:]:
        total = total + term[...].astype(F32)
    tops[...] = (total[:, :, :rank] + total[:, :, rank:]).astype(tops.dtype)
    sent[...] = given[...]


def window_kernel(given, before, after, window, sent):
    sent[...] = given[...]
    rows, _, lanes = before.shape
    rank = lanes // 2
    for side, packed in enumerate((before, after)):
        for g in range(2 * rows):
            part = packed[g // 2, :, (g % 2) * rank : (g % 2 + 1) * rank]
            window[side * 2 * rows + g] = part


def couple_kernel(window, coupling, list_h, part, coupling_list, sem):
    copy = pltpu.make_async_copy(list_h, coupling_list, sem)
    copy.start()
    leaves, count = coupling.shape[:2]
    total = leaves * lax.axis_size("blk") * lax.axis_size("leaf")
    device = lax.axis_index("blk") * lax.axis_size("leaf") + lax.axis_index("leaf")
    anchor = (device - 1) * leaves
    copy.wait()
    for g in range(leaves):
        rows = []
        for c in range(count):
            slot = lax.rem(coupling_list[c, g] - anchor + 2 * total, total)
            slot = jnp.where(slot >= 2 * leaves, slot - leaves, slot)
            slot = jnp.minimum(slot, 2 * leaves - 1)
            rows.append(window[slot])
        columns = [coupling[g, c] for c in range(count)]
        part[g] = nt(jnp.concatenate(rows, axis=1), jnp.concatenate(columns, axis=1))


def down_kernel(*refs):
    tops, part, leaf_transfer, natural, direction = refs[:5]
    sources, base, targets, sems = refs[5:8], refs[8], refs[9:12], refs[12]
    top_list, top_coupling, node_transfer = targets
    copies = [
        pltpu.make_async_copy(source, target, sems.at[i])
        for i, (source, target) in enumerate(zip(sources, targets))
    ]
    for copy in copies:
        copy.start()
    leaves, samples, points = direction.shape
    rank = natural.shape[1]
    clusters = lax.axis_size("blk")
    here = lax.axis_index("blk")
    for copy in copies:
        copy.wait()
    incoming = jnp.zeros((samples, rank), F32)
    for e in range(top_list.shape[1]):
        index = lax.rem(here - top_list[0, e] + clusters, clusters)
        if clusters == 4:
            index = here ^ top_list[0, e]
        incoming = incoming + nt(tops[index], top_coupling[0, e])
    down = nn(incoming.astype(BF), node_transfer[0]).astype(BF)
    for g in range(leaves):
        inward = nn(down, leaf_transfer[g]) + part[g]
        far = nn(inward.astype(BF), natural[g])
        base[g] = NUGGET * direction[g].astype(F32) + far


def near_kernel(near_h, *refs):
    pieces, tiles, (kept, given, mark, window, near, sems) = refs[:6], refs[6:8], refs[-6:]
    mark[...] = jnp.zeros_like(mark)
    leaves = window.shape[0] // 3
    samples = kept.shape[1]
    total = leaves * lax.axis_size("blk") * lax.axis_size("leaf")
    device = lax.axis_index("blk") * lax.axis_size("leaf") + lax.axis_index("leaf")
    anchor = (device - 1) * leaves
    copies = [pltpu.make_async_copy(near_h, near, sems.at[6])]
    for i, piece in enumerate(pieces):
        side, columns = i // 2, i % 2
        copies.append(
            pltpu.make_async_copy(
                piece,
                window.at[
                    side * leaves : (side + 1) * leaves,
                    columns * samples : (columns + 1) * samples,
                ],
                sems.at[i],
            )
        )
    for copy in copies:
        copy.start()
    for copy in copies:
        copy.wait()
    at = 0
    for part in tiles:

        def leaf(i, carry, part=part, at=at):
            g = lax.axis_index("sample") * kept.shape[0] + at + i
            values = []
            for e in range(near.shape[1]):
                values.append(window[lax.rem(near[g, e] - anchor + 2 * total, total)])
            field = nn(jnp.concatenate(values, axis=1), part[i]) * AMPLITUDE
            kept[at + i] = field[:samples]
            given[at + i] = field[samples:].astype(BF)
            return carry

        lax.fori_loop(0, part.shape[0], leaf, 0)
        at += part.shape[0]


def residual_kernel(step, base, kept, received, residual, updated_h, updated, norms, sems):
    half = kept.shape[0]
    chunks = sems.shape[1]
    size = half // chunks
    leaving = []
    for c in range(chunks):
        for k in range(2):
            part = pl.ds(k * half + c * size, size)
            leaving.append(
                pltpu.make_async_copy(updated.at[part], updated_h.at[part], sems.at[k, c])
            )
    core = lax.axis_index("sample")
    steps = column(step[...])
    totals = [jnp.zeros((step.shape[1], 1), F32)] * 2
    for i in range(half):
        for theirs in range(2):
            g = (core ^ theirs) * half + i
            near = received[i].astype(F32) if theirs else kept[i]
            old = residual[g]
            new = old - steps * (base[g] + near)
            updated[g] = new
            for k, value in enumerate((old, new)):
                totals[k] = totals[k] + jnp.sum(value * value, axis=1, keepdims=True)
        if i % size == size - 1:
            for k in range(2):
                leaving[2 * (i // size) + k].start()
    samples = steps.shape[0]
    lane = lax.broadcasted_iota(jnp.int32, (samples, 128), 1)
    sub = lax.broadcasted_iota(jnp.int32, (samples, 128), 0)
    rows = [jnp.sum(jnp.where(lane == sub, part, 0.0), axis=0, keepdims=True) for part in totals]
    row = lax.broadcasted_iota(jnp.int32, norms.shape[1:], 0)
    packed = jnp.where(row == 0, rows[0], jnp.where(row == 1, rows[1], 0.0))
    for i in range(norms.shape[0]):
        norms[i] = packed
    for copy in leaving:
        copy.wait()


def direction_kernel(norms, updated, direction, result, held, sems):
    leaves, samples, points = updated.shape
    sums = norms[0]
    for i in range(1, norms.shape[0]):
        sums = sums + norms[i]
    ratio = column((sums[1:2, :] / sums[0:1, :])[:, :samples])
    chunks = sems.shape[0]
    size = leaves // chunks
    copies = []
    for c in range(chunks):
        for g in range(c * size, (c + 1) * size):
            held[g] = (updated[g] + ratio * direction[g].astype(F32)).astype(BF)
        part = pl.ds(c * size, size)
        copies.append(pltpu.make_async_copy(held.at[part], result.at[part], sems.at[c]))
        copies[-1].start()
    for copy in copies:
        copy.wait()


def on_device(
    residual,
    direction,
    step,
    coords,
    order,
    basis,
    leaf_transfer,
    node_transfer,
    near_list,
    coupling_list,
    coupling,
    top_list,
    top_coupling,
):
    leaves, samples, points = direction.shape
    rank = basis.shape[1]
    entries = near_list.shape[1]
    half = leaves // 2
    blk_count = lax.axis_size("blk")
    leaf_count = lax.axis_size("leaf")
    shape = jax.ShapeDtypeStruct
    token = shape((8, 128), F32)
    vmem = pl.BlockSpec(memory_space=pltpu.VMEM)
    anywhere = pl.BlockSpec(memory_space=pl.ANY)
    hbm = pl.BlockSpec(memory_space=pltpu.HBM)

    coords = jnp.transpose(coords, (1, 0, 2))
    coords_prev = shifted(coords, RING, 1)
    coords_after = shifted(coords, RING, -1)
    operands = (order, basis, direction, leaf_transfer, node_transfer)
    resident = call(
        load_kernel,
        tuple(shape(array.shape, array.dtype) for array in operands),
        MIB,
        2 * MIB,
        in_specs=[hbm] * 5,
        out_specs=(vmem,) * 5,
        scratch_shapes=[pltpu.SemaphoreType.DMA((5,))],
        vmem=4,
    )(*in_hbm(*operands))
    travelling = ordered(direction, coords_prev, coords_after, resident[0])
    direction_prev = shifted(travelling, RING, 1)
    direction_after = shifted(travelling, RING, -1)
    natural, coef, lifted, up_mark = call(
        up_kernel,
        (
            pltpu.HBM((leaves, rank, points), BF),
            shape((leaves // 2, samples, 2 * rank), BF),
            shape((samples, rank), F32),
            token,
        ),
        4 * leaves * rank * points * points,
        6 * MIB,
        in_specs=[vmem] * 5,
        out_specs=(hbm, vmem, vmem, vmem),
        scratch_shapes=[pltpu.VMEM(basis.shape, BF), pltpu.SemaphoreType.DMA((4,))],
        vmem=8,
    )(ordered(resident[0], coords_prev, coords_after), *resident[1:])

    def make_tiles(start, done, *operands):
        count = half // 2
        outs = (pltpu.VMEM((count, entries * points, points), BF), token)
        if start == 0:
            outs += (shape((3 * leaves, points, 128), BF), shape(coords.shape, F32))
        return call(
            functools.partial(tile_kernel, start),
            outs,
            40 * count * entries * points * points,
            count * entries * points * points * (16 if start == 0 else 1),
            in_specs=[hbm, anywhere, hbm if start == 0 else vmem] + [vmem] * (len(operands) - 1),
            out_specs=(vmem,) * len(outs),
            scratch_shapes=[pltpu.VMEM(coords.shape, BF)] * (start == 0)
            + [pltpu.SMEM(near_list.shape, jnp.int32), pltpu.SemaphoreType.DMA((2,))],
            vmem=8,
        )(*in_hbm(near_list), done, *operands)

    coef_prev = shifted(coef, RING, 1)
    coef_after = shifted(coef, RING, -1)
    tiles_low, low_mark, spread_x, plain = make_tiles(
        0, up_mark, *in_hbm(coords), coords_prev, coords_after
    )
    leaving = call(
        after_kernel,
        shape((samples, 2 * rank), BF),
        MIB,
        MIB,
        in_specs=[anywhere, vmem],
        out_specs=vmem,
        vmem=4,
    )(low_mark, lifted)
    if blk_count == 4:
        others = [lax.ppermute(leaving, "blk", [(i, i ^ 1) for i in range(4)])]
    elif blk_count <= 8:
        others = [shifted(leaving, "blk", by) for by in range(1, blk_count)]
    else:
        others = lax.all_gather(leaving[None], "blk", axis=0, tiled=True)
        places = jnp.mod(lax.axis_index("blk") - jnp.arange(blk_count, dtype=jnp.int32), blk_count)
        others = list(others[places][1:])
    tiles_high, high_mark = make_tiles(half // 2, low_mark, plain, spread_x)
    direction_other = partner(ordered(direction, high_mark, *others))
    direction_prev = ordered(direction_prev, high_mark, *others)
    direction_after = ordered(direction_after, high_mark, *others)
    def collect(parts):
        count = sum(1 if part.ndim == 2 else part.shape[0] for part in parts)
        return call(
            collect_kernel,
            shape((count, samples, 2 * rank), BF),
            MIB,
            MIB,
            in_specs=[vmem] * len(parts),
            out_specs=vmem,
            vmem=4,
        )(*parts)

    together = collect([leaving] + others)
    if blk_count == 4:
        beyond = lax.ppermute(together, "blk", [(i, i ^ 2) for i in range(4)])
        together = collect([together, beyond])
    terms = [shifted(together, "leaf", by) for by in range(1, leaf_count)]
    kept, given, near_mark = call(
        near_kernel,
        (shape((half, samples, points), F32), shape((half, samples, points), BF), token),
        MIB,
        MIB,
        in_specs=[hbm] + [anywhere] * 6 + [vmem] * 2,
        out_specs=(vmem,) * 3,
        scratch_shapes=[
            pltpu.VMEM((3 * leaves, 2 * samples, points), BF),
            pltpu.SMEM(near_list.shape, jnp.int32),
            pltpu.SemaphoreType.DMA((7,)),
        ],
        vmem=8,
    )(
        *in_hbm(near_list),
        direction_prev,
        partner(direction_prev),
        *in_hbm(direction),
        direction_other,
        direction_after,
        partner(direction_after),
        tiles_low,
        tiles_high,
    )

    coef_window, given = call(
        window_kernel,
        (shape((2 * leaves, samples, rank), BF), shape((half, samples, points), BF)),
        MIB,
        MIB,
        in_specs=[vmem] * 3,
        out_specs=(vmem, vmem),
        vmem=4,
    )(given, coef_prev, coef_after)
    part = call(
        couple_kernel,
        shape((leaves, samples, rank), F32),
        2 * leaves * samples * rank * rank * 8,
        4 * MIB,
        in_specs=[vmem] * 2 + [hbm],
        out_specs=vmem,
        scratch_shapes=[
            pltpu.SMEM(coupling_list.shape[::-1], jnp.int32),
            pltpu.SemaphoreType.DMA,
        ],
        vmem=8,
    )(coef_window, coupling, *in_hbm(coupling_list.T))
    tops, given = call(
        top_kernel,
        (shape((blk_count, samples, rank), BF), shape((half, samples, points), BF)),
        MIB,
        MIB,
        in_specs=[anywhere] + [vmem] * (2 + len(terms)),
        out_specs=(vmem, vmem),
        vmem=8,
    )(part, given, together, *terms)
    arrays = (top_list, top_coupling, node_transfer)
    spaces = (pltpu.SMEM, pltpu.VMEM, pltpu.VMEM)
    base = call(
        down_kernel,
        shape((leaves, samples, points), F32),
        2 * leaves * samples * rank * (points + rank),
        4 * MIB,
        in_specs=[vmem] * 5 + [hbm] * 3,
        out_specs=vmem,
        scratch_shapes=[space(array.shape, array.dtype) for space, array in zip(spaces, arrays)]
        + [pltpu.SemaphoreType.DMA((3,))],
        vmem=10,
    )(tops, part, leaf_transfer, natural, direction, *in_hbm(*arrays))
    received = partner(given)

    devices = blk_count * leaf_count
    whole = shape((leaves, samples, points), F32)
    residual_next, updated, norms = call(
        residual_kernel,
        (whole, whole, shape((devices, 8, 128), F32)),
        4 * MIB,
        5 * MIB,
        in_specs=[vmem] * 5,
        out_specs=(hbm, vmem, vmem),
        scratch_shapes=[pltpu.SemaphoreType.DMA((2, 4))],
        vmem=8,
    )(step[None, :], base, kept, received, residual)
    norms = lax.all_to_all(norms, RING, 0, 0)
    direction_next = call(
        direction_kernel,
        shape((leaves, samples, points), BF),
        MIB,
        2 * MIB,
        in_specs=[vmem] * 3,
        out_specs=anywhere,
        scratch_shapes=[
            pltpu.VMEM((leaves, samples, points), BF),
            pltpu.SemaphoreType.DMA((4,)),
        ],
        vmem=8,
    )(norms, updated, direction)
    return (residual_next, direction_next)


def solution(mesh):
    in_specs = (
        P(("groups", "blk", "leaf"), "sample", None),
        P(("groups", "blk", "leaf"), "sample", None),
        P(("groups", "sample")),
        P(("groups", "blk", "leaf"), None, None),
        P(("groups", "blk", "leaf"), None),
        P(("groups", "blk", "leaf"), None, None),
        P(("groups", "blk", "leaf"), None, None),
        P(("groups", "blk", "leaf"), None, None),
        P(("groups", "blk", "leaf"), None),
        P(("groups", "blk", "leaf"), None),
        P(("groups", "blk", "leaf"), None, None, None),
        P(("groups", "blk"), None),
        P(("groups", "blk"), None, None, None),
    )
    out_specs = (
        P(("groups", "blk", "leaf"), "sample", None),
        P(("groups", "blk", "leaf"), "sample", None),
    )
    return jax.shard_map(
        on_device, mesh=mesh, in_specs=in_specs, out_specs=out_specs, check_vma=False
    )
```

```python
import functools
import math

import jax
import jax.numpy as jnp
from jax import lax
from jax.experimental import pallas as pl
from jax.experimental.pallas import tpu as pltpu
from jax.sharding import PartitionSpec as P

LEAF_DEV = 16

ROOT_THREE = math.sqrt(3.0)
LENGTH = 0.3
AMPLITUDE = 0.25
NUGGET = 0.5
SPREAD = 0.5 / LEAF_DEV
KAPPA = (ROOT_THREE / LENGTH) ** 2
LOG2E = 1.4426950408889634

RING = ("blk", "leaf")
BF = jnp.bfloat16
F32 = jnp.float32
MIB = 1 << 20


def shifted(array, axis, by):
    if isinstance(axis, tuple):
        count = math.prod(lax.axis_size(name) for name in axis)
    else:
        count = lax.axis_size(axis)
    return lax.ppermute(array, axis, [(i, (i + by) % count) for i in range(count)])


def partner(array):
    return lax.ppermute(array, "sample", [(0, 1), (1, 0)])


def ordered(array, *first):
    return lax.optimization_barrier((array,) + first)[0]


def column(row):
    size = row.shape[1]
    shape = (size, size)
    here = lax.broadcasted_iota(jnp.int32, shape, 0) == lax.broadcasted_iota(jnp.int32, shape, 1)
    return jnp.sum(jnp.where(here, row, 0.0), axis=1, keepdims=True)


def in_hbm(*arrays):
    return [pltpu.with_memory_space_constraint(array, pltpu.HBM) for array in arrays]


def thirds(value):
    high = value.astype(BF).astype(F32)
    rest = value - high
    middle = rest.astype(BF).astype(F32)
    return high, middle, rest - middle


def nt(left, right):
    return lax.dot_general(left, right, (((1,), (1,)), ((), ())), preferred_element_type=F32)


def nn(left, right):
    return jnp.dot(left, right, preferred_element_type=F32)


def call(kernel, outs, flops, moved, vmem=40, **kwargs):
    return pl.pallas_call(
        kernel,
        out_shape=outs,
        compiler_params=pltpu.CompilerParams(vmem_limit_bytes=vmem * MIB),
        cost_estimate=pl.CostEstimate(flops=flops, bytes_accessed=moved, transcendentals=0),
        **kwargs,
    )


def load_kernel(*refs):
    count = len(refs) // 2
    sources, targets, sems = refs[:count], refs[count:-1], refs[-1]
    copies = [
        pltpu.make_async_copy(source, target, sems.at[i])
        for i, (source, target) in enumerate(zip(sources, targets))
    ]
    for copy in copies:
        copy.start()
    for copy in copies:
        copy.wait()


def up_kernel(order, basis, direction, leaf_transfer, node_transfer, *refs):
    natural_h, coef, lifted, mark, natural, sems = refs
    mark[...] = jnp.zeros_like(mark)
    leaves, rank, points = basis.shape
    samples = direction.shape[1]
    chunks = sems.shape[0]
    size = leaves // chunks
    rows = lax.broadcasted_iota(jnp.int32, (points, points), 0)
    node = jnp.zeros((samples, rank), F32)
    leaving = []
    for g in range(leaves):
        spot = jnp.where(rows == order[g : g + 1, :], 1.0, 0.0).astype(BF)
        own = nt(basis[g], spot).astype(BF)
        natural[g] = own
        weights = nt(direction[g], own).astype(BF)
        coef[g // 2, :, (g % 2) * rank : (g % 2 + 1) * rank] = weights
        node = node + nt(weights, leaf_transfer[g])
        if g % size == size - 1:
            part = pl.ds(g + 1 - size, size)
            copy = pltpu.make_async_copy(natural.at[part], natural_h.at[part], sems.at[g // size])
            copy.start()
            leaving.append(copy)
    lifted[...] = nt(node.astype(BF), node_transfer[0])
    for copy in leaving:
        copy.wait()


def features(offsets):
    x, y, z = (offsets[i : i + 1] for i in range(3))
    square = thirds(KAPPA * (x * x + y * y + z * z))
    row = lax.broadcasted_iota(jnp.int32, (8, x.shape[1]), 0)
    packed = jnp.zeros((8, x.shape[1]), F32)
    for i, value in enumerate((x, y, z, jnp.ones_like(x)) + square):
        packed = jnp.where(row == i, value, packed)
    return packed.astype(BF)


def spread_features(offsets):
    lane = lax.broadcasted_iota(jnp.int32, (8, 128), 1)
    source = jnp.where(
        lane < 9,
        lane // 3,
        jnp.where(lane < 12, lane - 5, jnp.where(lane < 16, 7, jnp.where(lane < 64, 3, 0))),
    )
    source = jnp.where(lane < 112, source, 7)
    row = lax.broadcasted_iota(jnp.int32, (8, 128), 0)
    pick = jnp.where((row == source) & (row < 7), 1.0, 0.0).astype(BF)
    return lax.dot_general(
        features(offsets), pick, (((0,), (0,)), ((), ())), preferred_element_type=F32
    ).astype(BF)


def tile_kernel(start, near_h, _, *refs):
    if start == 0:
        own_h, prev, after, tiles, mark, spread_x, plain, own, near, sem = refs
        offered = pltpu.make_async_copy(own_h, own, sem.at[1])
        offered.start()
    else:
        plain, spread_x, tiles, mark, near, sem = refs
        own = plain
    listed = pltpu.make_async_copy(near_h, near, sem.at[0])
    listed.start()
    mark[...] = jnp.zeros_like(mark)
    count = tiles.shape[0]
    entries = near.shape[1]
    points = own.shape[2]
    leaves = own.shape[1]
    total = leaves * lax.axis_size("blk") * lax.axis_size("leaf")
    device = lax.axis_index("blk") * lax.axis_size("leaf") + lax.axis_index("leaf")
    anchor = (device - 1) * leaves
    if start == 0:
        offered.wait()
        for side, ref in enumerate((prev, own, after)):
            offsets = ref[...].astype(F32)
            for j in range(leaves):
                spread_x[side * leaves + j] = spread_features(offsets[:, j])
            if side == 1:
                plain[...] = offsets
    listed.wait()
    row = lax.broadcasted_iota(jnp.int32, (16, points), 0)
    lane = lax.broadcasted_iota(jnp.int32, (1, 128), 1)

    def leaf(i, carry):
        g = lax.axis_index("sample") * (leaves // 2) + start + i
        x, y, z = (plain[k, pl.ds(g, 1), :] for k in range(3))
        first = jnp.where((row >= 9) & (row < 12), 1.0, jnp.zeros((16, points), F32))
        at = 0
        for value in (x, y, z):
            for part in thirds(value * (-2.0 * KAPPA)):
                first = jnp.where(row == at, part, first)
                at += 1
        slots = []
        gap = jnp.zeros((16, points), F32)
        for e in range(entries):
            slot = lax.rem(near[g, e] - anchor + 2 * total, total)
            slots.append(slot)
            gap = jnp.where(row == e, (leaves + g - slot).astype(F32) * SPREAD, gap)
        moved = x + gap
        fixed = thirds(KAPPA * (moved * moved + y * y + z * z))
        gaps = thirds(gap * (-2.0 * KAPPA))
        weights = jnp.concatenate(
            [part.astype(BF) for part in (first,) + fixed + gaps + (jnp.zeros_like(first),)],
            axis=0,
        )
        for e in range(entries):
            keep = jnp.where((lane < 16) | (lane % 16 == e), 1.0, 0.0).astype(BF)
            square = jnp.maximum(nn(spread_x[slots[e]] * keep, weights), 1e-30)
            scaled = square * lax.rsqrt(square)
            value = (1.0 + scaled) * jnp.exp2(scaled * (-LOG2E))
            tiles[i, e * points : (e + 1) * points, :] = value.astype(BF)
        return carry

    lax.fori_loop(0, count, leaf, 0)


def after_kernel(_, source, target):
    rank = source.shape[1]
    for i, part in enumerate(thirds(source[...])[:2]):
        target[:, i * rank : (i + 1) * rank] = part.astype(target.dtype)


def collect_kernel(*refs):
    terms, together = refs[:-1], refs[-1]
    for i, term in enumerate(terms):
        together[i] = term[...]


def top_kernel(_, given, *refs):
    terms, (tops, sent) = refs[:-2], refs[-2:]
    rank = tops.shape[2]
    total = terms[0][...].astype(F32)
    for term in terms[1:]:
        total = total + term[...].astype(F32)
    tops[...] = (total[:, :, :rank] + total[:, :, rank:]).astype(tops.dtype)
    sent[...] = given[...]


def window_kernel(given, before, after, window, sent):
    sent[...] = given[...]
    rows, _, lanes = before.shape
    rank = lanes // 2
    for side, packed in enumerate((before, after)):
        for g in range(2 * rows):
            part = packed[g // 2, :, (g % 2) * rank : (g % 2 + 1) * rank]
            window[side * 2 * rows + g] = part


def couple_kernel(window, coupling, list_h, part, coupling_list, sem):
    copy = pltpu.make_async_copy(list_h, coupling_list, sem)
    copy.start()
    leaves, count = coupling.shape[:2]
    total = leaves * lax.axis_size("blk") * lax.axis_size("leaf")
    device = lax.axis_index("blk") * lax.axis_size("leaf") + lax.axis_index("leaf")
    anchor = (device - 1) * leaves
    copy.wait()
    for g in range(leaves):
        rows = []
        for c in range(count):
            slot = lax.rem(coupling_list[c, g] - anchor + 2 * total, total)
            slot = jnp.where(slot >= 2 * leaves, slot - leaves, slot)
            slot = jnp.minimum(slot, 2 * leaves - 1)
            rows.append(window[slot])
        columns = [coupling[g, c] for c in range(count)]
        part[g] = nt(jnp.concatenate(rows, axis=1), jnp.concatenate(columns, axis=1))


def down_kernel(
    tops, part, leaf_transfer, natural, direction, top_list, top_coupling, node_transfer, base
):
    leaves, samples, points = direction.shape
    rank = natural.shape[1]
    clusters = lax.axis_size("blk")
    here = lax.axis_index("blk")
    behind = here - top_list[...]
    behind = jnp.where(behind < 0, behind + clusters, behind)
    incoming = jnp.zeros((samples, rank), F32)
    for e in range(top_list.shape[1]):
        chosen = jnp.zeros((samples, rank), F32)
        for i in range(clusters):
            chosen = jnp.where(behind[:, e : e + 1] == i, tops[i].astype(F32), chosen)
        incoming = incoming + nt(chosen.astype(BF), top_coupling[0, e])
    down = nn(incoming.astype(BF), node_transfer[0]).astype(BF)
    for g in range(leaves):
        inward = nn(down, leaf_transfer[g]) + part[g]
        far = nn(inward.astype(BF), natural[g])
        base[g] = NUGGET * direction[g].astype(F32) + far


def near_kernel(near_h, *refs):
    pieces, tiles, (kept, given, mark, window, near, sems) = refs[:6], refs[6:8], refs[-6:]
    mark[...] = jnp.zeros_like(mark)
    leaves = window.shape[0] // 3
    samples = kept.shape[1]
    total = leaves * lax.axis_size("blk") * lax.axis_size("leaf")
    device = lax.axis_index("blk") * lax.axis_size("leaf") + lax.axis_index("leaf")
    anchor = (device - 1) * leaves
    copies = [pltpu.make_async_copy(near_h, near, sems.at[6])]
    for i, piece in enumerate(pieces):
        side, columns = i // 2, i % 2
        copies.append(
            pltpu.make_async_copy(
                piece,
                window.at[
                    side * leaves : (side + 1) * leaves,
                    columns * samples : (columns + 1) * samples,
                ],
                sems.at[i],
            )
        )
    for copy in copies:
        copy.start()
    for copy in copies:
        copy.wait()
    at = 0
    for part in tiles:

        def leaf(i, carry, part=part, at=at):
            g = lax.axis_index("sample") * kept.shape[0] + at + i
            values = []
            for e in range(near.shape[1]):
                values.append(window[lax.rem(near[g, e] - anchor + 2 * total, total)])
            field = nn(jnp.concatenate(values, axis=1), part[i]) * AMPLITUDE
            kept[at + i] = field[:samples]
            given[at + i] = field[samples:].astype(BF)
            return carry

        lax.fori_loop(0, part.shape[0], leaf, 0)
        at += part.shape[0]


def residual_kernel(step, base, kept, received, residual, updated_h, updated, norms, sems):
    half = kept.shape[0]
    chunks = sems.shape[1]
    size = half // chunks
    leaving = []
    for c in range(chunks):
        for k in range(2):
            part = pl.ds(k * half + c * size, size)
            leaving.append(
                pltpu.make_async_copy(updated.at[part], updated_h.at[part], sems.at[k, c])
            )
    core = lax.axis_index("sample")
    steps = column(step[...])
    totals = [jnp.zeros((step.shape[1], 1), F32)] * 2
    for i in range(half):
        for theirs in range(2):
            g = (core ^ theirs) * half + i
            near = received[i].astype(F32) if theirs else kept[i]
            old = residual[g]
            new = old - steps * (base[g] + near)
            updated[g] = new
            for k, value in enumerate((old, new)):
                totals[k] = totals[k] + jnp.sum(value * value, axis=1, keepdims=True)
        if i % size == size - 1:
            for k in range(2):
                leaving[2 * (i // size) + k].start()
    samples = steps.shape[0]
    lane = lax.broadcasted_iota(jnp.int32, (samples, 128), 1)
    sub = lax.broadcasted_iota(jnp.int32, (samples, 128), 0)
    rows = [jnp.sum(jnp.where(lane == sub, part, 0.0), axis=0, keepdims=True) for part in totals]
    row = lax.broadcasted_iota(jnp.int32, norms.shape[1:], 0)
    packed = jnp.where(row == 0, rows[0], jnp.where(row == 1, rows[1], 0.0))
    for i in range(norms.shape[0]):
        norms[i] = packed
    for copy in leaving:
        copy.wait()


def direction_kernel(norms, updated, direction, result, held, sems):
    leaves, samples, points = updated.shape
    sums = norms[0]
    for i in range(1, norms.shape[0]):
        sums = sums + norms[i]
    ratio = column((sums[1:2, :] / sums[0:1, :])[:, :samples])
    chunks = sems.shape[0]
    size = leaves // chunks
    copies = []
    for c in range(chunks):
        for g in range(c * size, (c + 1) * size):
            held[g] = (updated[g] + ratio * direction[g].astype(F32)).astype(BF)
        part = pl.ds(c * size, size)
        copies.append(pltpu.make_async_copy(held.at[part], result.at[part], sems.at[c]))
        copies[-1].start()
    for copy in copies:
        copy.wait()


def on_device(
    residual,
    direction,
    step,
    coords,
    order,
    basis,
    leaf_transfer,
    node_transfer,
    near_list,
    coupling_list,
    coupling,
    top_list,
    top_coupling,
):
    leaves, samples, points = direction.shape
    rank = basis.shape[1]
    entries = near_list.shape[1]
    half = leaves // 2
    blk_count = lax.axis_size("blk")
    leaf_count = lax.axis_size("leaf")
    shape = jax.ShapeDtypeStruct
    token = shape((8, 128), F32)
    vmem = pl.BlockSpec(memory_space=pltpu.VMEM)
    anywhere = pl.BlockSpec(memory_space=pl.ANY)
    hbm = pl.BlockSpec(memory_space=pltpu.HBM)

    coords = jnp.transpose(coords, (1, 0, 2))
    coords_prev = shifted(coords, RING, 1)
    coords_after = shifted(coords, RING, -1)
    operands = (order, basis, direction, leaf_transfer, node_transfer)
    resident = call(
        load_kernel,
        tuple(shape(array.shape, array.dtype) for array in operands),
        MIB,
        2 * MIB,
        in_specs=[hbm] * 5,
        out_specs=(vmem,) * 5,
        scratch_shapes=[pltpu.SemaphoreType.DMA((5,))],
        vmem=4,
    )(*in_hbm(*operands))
    travelling = ordered(direction, coords_prev, coords_after, resident[0])
    direction_prev = shifted(travelling, RING, 1)
    direction_after = shifted(travelling, RING, -1)
    natural, coef, lifted, up_mark = call(
        up_kernel,
        (
            pltpu.HBM((leaves, rank, points), BF),
            shape((leaves // 2, samples, 2 * rank), BF),
            shape((samples, rank), F32),
            token,
        ),
        4 * leaves * rank * points * points,
        6 * MIB,
        in_specs=[vmem] * 5,
        out_specs=(hbm, vmem, vmem, vmem),
        scratch_shapes=[pltpu.VMEM(basis.shape, BF), pltpu.SemaphoreType.DMA((4,))],
        vmem=8,
    )(ordered(resident[0], coords_prev, coords_after), *resident[1:])

    def make_tiles(start, done, *operands):
        count = half // 2
        outs = (pltpu.VMEM((count, entries * points, points), BF), token)
        if start == 0:
            outs += (shape((3 * leaves, points, 128), BF), shape(coords.shape, F32))
        return call(
            functools.partial(tile_kernel, start),
            outs,
            40 * count * entries * points * points,
            count * entries * points * points * (16 if start == 0 else 1),
            in_specs=[hbm, anywhere, hbm if start == 0 else vmem] + [vmem] * (len(operands) - 1),
            out_specs=(vmem,) * len(outs),
            scratch_shapes=[pltpu.VMEM(coords.shape, BF)] * (start == 0)
            + [pltpu.SMEM(near_list.shape, jnp.int32), pltpu.SemaphoreType.DMA((2,))],
            vmem=8,
        )(*in_hbm(near_list), done, *operands)

    coef_prev = shifted(coef, RING, 1)
    coef_after = shifted(coef, RING, -1)
    tiles_low, low_mark, spread_x, plain = make_tiles(
        0, up_mark, *in_hbm(coords), coords_prev, coords_after
    )
    leaving = call(
        after_kernel,
        shape((samples, 2 * rank), BF),
        MIB,
        MIB,
        in_specs=[anywhere, vmem],
        out_specs=vmem,
        vmem=4,
    )(low_mark, lifted)
    if blk_count <= 8:
        others = [shifted(leaving, "blk", by) for by in range(1, blk_count)]
    else:
        others = lax.all_gather(leaving[None], "blk", axis=0, tiled=True)
        places = jnp.mod(lax.axis_index("blk") - jnp.arange(blk_count, dtype=jnp.int32), blk_count)
        others = list(others[places][1:])
    tiles_high, high_mark = make_tiles(half // 2, low_mark, plain, spread_x)
    direction_other = partner(ordered(direction, high_mark, *others))
    direction_prev = ordered(direction_prev, high_mark, *others)
    direction_after = ordered(direction_after, high_mark, *others)
    together = call(
        collect_kernel,
        shape((blk_count, samples, 2 * rank), BF),
        MIB,
        MIB,
        in_specs=[vmem] * blk_count,
        out_specs=vmem,
        vmem=4,
    )(leaving, *others)
    terms = [shifted(together, "leaf", by) for by in range(1, leaf_count)]
    kept, given, near_mark = call(
        near_kernel,
        (shape((half, samples, points), F32), shape((half, samples, points), BF), token),
        MIB,
        MIB,
        in_specs=[hbm] + [anywhere] * 6 + [vmem] * 2,
        out_specs=(vmem,) * 3,
        scratch_shapes=[
            pltpu.VMEM((3 * leaves, 2 * samples, points), BF),
            pltpu.SMEM(near_list.shape, jnp.int32),
            pltpu.SemaphoreType.DMA((7,)),
        ],
        vmem=8,
    )(
        *in_hbm(near_list),
        direction_prev,
        partner(direction_prev),
        *in_hbm(direction),
        direction_other,
        direction_after,
        partner(direction_after),
        tiles_low,
        tiles_high,
    )

    coef_window, given = call(
        window_kernel,
        (shape((2 * leaves, samples, rank), BF), shape((half, samples, points), BF)),
        MIB,
        MIB,
        in_specs=[vmem] * 3,
        out_specs=(vmem, vmem),
        vmem=4,
    )(given, coef_prev, coef_after)
    part = call(
        couple_kernel,
        shape((leaves, samples, rank), F32),
        2 * leaves * samples * rank * rank * 8,
        4 * MIB,
        in_specs=[vmem] * 2 + [hbm],
        out_specs=vmem,
        scratch_shapes=[
            pltpu.SMEM(coupling_list.shape[::-1], jnp.int32),
            pltpu.SemaphoreType.DMA,
        ],
        vmem=8,
    )(coef_window, coupling, *in_hbm(coupling_list.T))
    tops, given = call(
        top_kernel,
        (shape((blk_count, samples, rank), BF), shape((half, samples, points), BF)),
        MIB,
        MIB,
        in_specs=[anywhere] + [vmem] * (2 + len(terms)),
        out_specs=(vmem, vmem),
        vmem=8,
    )(part, given, together, *terms)
    base = call(
        down_kernel,
        shape((leaves, samples, points), F32),
        2 * leaves * samples * rank * (points + rank),
        4 * MIB,
        in_specs=[vmem] * 8,
        out_specs=vmem,
        vmem=10,
    )(
        tops,
        part,
        leaf_transfer,
        natural,
        direction,
        top_list,
        top_coupling,
        node_transfer,
    )
    received = partner(given)

    devices = blk_count * leaf_count
    whole = shape((leaves, samples, points), F32)
    residual_next, updated, norms = call(
        residual_kernel,
        (whole, whole, shape((devices, 8, 128), F32)),
        4 * MIB,
        5 * MIB,
        in_specs=[vmem] * 5,
        out_specs=(hbm, vmem, vmem),
        scratch_shapes=[pltpu.SemaphoreType.DMA((2, 4))],
        vmem=8,
    )(step[None, :], base, kept, received, residual)
    norms = lax.all_to_all(norms, RING, 0, 0)
    direction_next = call(
        direction_kernel,
        shape((leaves, samples, points), BF),
        MIB,
        2 * MIB,
        in_specs=[vmem] * 3,
        out_specs=anywhere,
        scratch_shapes=[
            pltpu.VMEM((leaves, samples, points), BF),
            pltpu.SemaphoreType.DMA((4,)),
        ],
        vmem=8,
    )(norms, updated, direction)
    return (residual_next, direction_next)


def solution(mesh):
    in_specs = (
        P(("groups", "blk", "leaf"), "sample", None),
        P(("groups", "blk", "leaf"), "sample", None),
        P(("groups", "sample")),
        P(("groups", "blk", "leaf"), None, None),
        P(("groups", "blk", "leaf"), None),
        P(("groups", "blk", "leaf"), None, None),
        P(("groups", "blk", "leaf"), None, None),
        P(("groups", "blk", "leaf"), None, None),
        P(("groups", "blk", "leaf"), None),
        P(("groups", "blk", "leaf"), None),
        P(("groups", "blk", "leaf"), None, None, None),
        P(("groups", "blk"), None),
        P(("groups", "blk"), None, None, None),
    )
    out_specs = (
        P(("groups", "blk", "leaf"), "sample", None),
        P(("groups", "blk", "leaf"), "sample", None),
    )
    return jax.shard_map(
        on_device, mesh=mesh, in_specs=in_specs, out_specs=out_specs, check_vma=False
    )
```

```python
import functools
import math

import jax
import jax.numpy as jnp
from jax import lax
from jax.experimental import pallas as pl
from jax.experimental.pallas import tpu as pltpu
from jax.sharding import PartitionSpec as P

LEAF_DEV = 16

ROOT_THREE = math.sqrt(3.0)
LENGTH = 0.3
AMPLITUDE = 0.25
NUGGET = 0.5
SPREAD = 0.5 / LEAF_DEV
KAPPA = (ROOT_THREE / LENGTH) ** 2
LOG2E = 1.4426950408889634

RING = ("blk", "leaf")
BF = jnp.bfloat16
F32 = jnp.float32
MIB = 1 << 20


def shifted(array, axis, by):
    if isinstance(axis, tuple):
        count = math.prod(lax.axis_size(name) for name in axis)
    else:
        count = lax.axis_size(axis)
    return lax.ppermute(array, axis, [(i, (i + by) % count) for i in range(count)])


def partner(array):
    return lax.ppermute(array, "sample", [(0, 1), (1, 0)])


def ordered(array, *first):
    return lax.optimization_barrier((array,) + first)[0]


def column(row):
    size = row.shape[1]
    shape = (size, size)
    here = lax.broadcasted_iota(jnp.int32, shape, 0) == lax.broadcasted_iota(jnp.int32, shape, 1)
    return jnp.sum(jnp.where(here, row, 0.0), axis=1, keepdims=True)


def in_hbm(*arrays):
    return [pltpu.with_memory_space_constraint(array, pltpu.HBM) for array in arrays]


def thirds(value):
    high = value.astype(BF).astype(F32)
    rest = value - high
    middle = rest.astype(BF).astype(F32)
    return high, middle, rest - middle


def nt(left, right):
    return lax.dot_general(left, right, (((1,), (1,)), ((), ())), preferred_element_type=F32)


def nn(left, right):
    return jnp.dot(left, right, preferred_element_type=F32)


def call(kernel, outs, flops, moved, vmem=40, **kwargs):
    return pl.pallas_call(
        kernel,
        out_shape=outs,
        compiler_params=pltpu.CompilerParams(vmem_limit_bytes=vmem * MIB),
        cost_estimate=pl.CostEstimate(flops=flops, bytes_accessed=moved, transcendentals=0),
        **kwargs,
    )


def load_kernel(*refs):
    count = len(refs) // 2
    sources, targets, sems = refs[:count], refs[count:-1], refs[-1]
    copies = [
        pltpu.make_async_copy(source, target, sems.at[i])
        for i, (source, target) in enumerate(zip(sources, targets))
    ]
    for copy in copies:
        copy.start()
    for copy in copies:
        copy.wait()


def up_kernel(order, basis, direction, leaf_transfer, node_transfer, *refs):
    natural_h, coef, lifted, mark, natural, sems = refs
    mark[...] = jnp.zeros_like(mark)
    leaves, rank, points = basis.shape
    samples = direction.shape[1]
    chunks = sems.shape[0]
    size = leaves // chunks
    rows = lax.broadcasted_iota(jnp.int32, (points, points), 0)
    node = jnp.zeros((samples, rank), F32)
    leaving = []
    for g in range(leaves):
        spot = jnp.where(rows == order[g : g + 1, :], 1.0, 0.0).astype(BF)
        own = nt(basis[g], spot).astype(BF)
        natural[g] = own
        weights = nt(direction[g], own).astype(BF)
        coef[g // 2, :, (g % 2) * rank : (g % 2 + 1) * rank] = weights
        node = node + nt(weights, leaf_transfer[g])
        if g % size == size - 1:
            part = pl.ds(g + 1 - size, size)
            copy = pltpu.make_async_copy(natural.at[part], natural_h.at[part], sems.at[g // size])
            copy.start()
            leaving.append(copy)
    lifted[...] = nt(node.astype(BF), node_transfer[0])
    for copy in leaving:
        copy.wait()


def features(offsets):
    x, y, z = (offsets[i : i + 1] for i in range(3))
    square = thirds(KAPPA * (x * x + y * y + z * z))
    row = lax.broadcasted_iota(jnp.int32, (8, x.shape[1]), 0)
    packed = jnp.zeros((8, x.shape[1]), F32)
    for i, value in enumerate((x, y, z, jnp.ones_like(x)) + square):
        packed = jnp.where(row == i, value, packed)
    return packed.astype(BF)


def spread_features(offsets):
    lane = lax.broadcasted_iota(jnp.int32, (8, 128), 1)
    source = jnp.where(
        lane < 9,
        lane // 3,
        jnp.where(lane < 12, lane - 5, jnp.where(lane < 16, 7, jnp.where(lane < 64, 3, 0))),
    )
    source = jnp.where(lane < 112, source, 7)
    row = lax.broadcasted_iota(jnp.int32, (8, 128), 0)
    pick = jnp.where((row == source) & (row < 7), 1.0, 0.0).astype(BF)
    return lax.dot_general(
        features(offsets), pick, (((0,), (0,)), ((), ())), preferred_element_type=F32
    ).astype(BF)


def tile_kernel(start, near_h, _, *refs):
    if start == 0:
        own_h, prev, after, tiles, mark, spread_x, plain, own, near, sem = refs
        offered = pltpu.make_async_copy(own_h, own, sem.at[1])
        offered.start()
    else:
        plain, spread_x, tiles, mark, near, sem = refs
        own = plain
    listed = pltpu.make_async_copy(near_h, near, sem.at[0])
    listed.start()
    mark[...] = jnp.zeros_like(mark)
    count = tiles.shape[0]
    entries = near.shape[1]
    points = own.shape[2]
    leaves = own.shape[1]
    total = leaves * lax.axis_size("blk") * lax.axis_size("leaf")
    device = lax.axis_index("blk") * lax.axis_size("leaf") + lax.axis_index("leaf")
    anchor = (device - 1) * leaves
    if start == 0:
        offered.wait()
        for side, ref in enumerate((prev, own, after)):
            offsets = ref[...].astype(F32)
            for j in range(leaves):
                spread_x[side * leaves + j] = spread_features(offsets[:, j])
            if side == 1:
                plain[...] = offsets
    listed.wait()
    row = lax.broadcasted_iota(jnp.int32, (16, points), 0)
    lane = lax.broadcasted_iota(jnp.int32, (1, 128), 1)

    def leaf(i, carry):
        g = lax.axis_index("sample") * (leaves // 2) + start + i
        x, y, z = (plain[k, pl.ds(g, 1), :] for k in range(3))
        first = jnp.where((row >= 9) & (row < 12), 1.0, jnp.zeros((16, points), F32))
        at = 0
        for value in (x, y, z):
            for part in thirds(value * (-2.0 * KAPPA)):
                first = jnp.where(row == at, part, first)
                at += 1
        slots = []
        gap = jnp.zeros((16, points), F32)
        for e in range(entries):
            slot = lax.rem(near[g, e] - anchor + 2 * total, total)
            slots.append(slot)
            gap = jnp.where(row == e, (leaves + g - slot).astype(F32) * SPREAD, gap)
        moved = x + gap
        fixed = thirds(KAPPA * (moved * moved + y * y + z * z))
        gaps = thirds(gap * (-2.0 * KAPPA))
        weights = jnp.concatenate(
            [part.astype(BF) for part in (first,) + fixed + gaps + (jnp.zeros_like(first),)],
            axis=0,
        )
        for e in range(entries):
            keep = jnp.where((lane < 16) | (lane % 16 == e), 1.0, 0.0).astype(BF)
            square = jnp.maximum(nn(spread_x[slots[e]] * keep, weights), 1e-30)
            scaled = square * lax.rsqrt(square)
            value = (1.0 + scaled) * jnp.exp2(scaled * (-LOG2E))
            tiles[i, e * points : (e + 1) * points, :] = value.astype(BF)
        return carry

    lax.fori_loop(0, count, leaf, 0)


def after_kernel(_, source, target):
    rank = source.shape[1]
    for i, part in enumerate(thirds(source[...])[:2]):
        target[:, i * rank : (i + 1) * rank] = part.astype(target.dtype)


def collect_kernel(*refs):
    terms, together = refs[:-1], refs[-1]
    for i, term in enumerate(terms):
        together[i] = term[...]


def top_kernel(_, given, *refs):
    terms, (tops, sent) = refs[:-2], refs[-2:]
    rank = tops.shape[2]
    total = terms[0][...].astype(F32)
    for term in terms[1:]:
        total = total + term[...].astype(F32)
    tops[...] = (total[:, :, :rank] + total[:, :, rank:]).astype(tops.dtype)
    sent[...] = given[...]


def couple_kernel(
    given, before, after, coupling, list_h, part, sent, window, coupling_list, sem
):
    copy = pltpu.make_async_copy(list_h, coupling_list, sem)
    copy.start()
    sent[...] = given[...]
    rows, _, lanes = before.shape
    rank = lanes // 2
    for side, packed in enumerate((before, after)):
        for g in range(2 * rows):
            piece = packed[g // 2, :, (g % 2) * rank : (g % 2 + 1) * rank]
            window[side * 2 * rows + g] = piece
    leaves, count = coupling.shape[:2]
    total = leaves * lax.axis_size("blk") * lax.axis_size("leaf")
    device = lax.axis_index("blk") * lax.axis_size("leaf") + lax.axis_index("leaf")
    anchor = (device - 1) * leaves
    copy.wait()
    for g in range(leaves):
        rows = []
        for c in range(count):
            slot = lax.rem(coupling_list[c, g] - anchor + 2 * total, total)
            slot = jnp.where(slot >= 2 * leaves, slot - leaves, slot)
            slot = jnp.minimum(slot, 2 * leaves - 1)
            rows.append(window[slot])
        columns = [coupling[g, c] for c in range(count)]
        part[g] = nt(jnp.concatenate(rows, axis=1), jnp.concatenate(columns, axis=1))


def down_kernel(
    tops, part, leaf_transfer, natural, direction, top_list, top_coupling, node_transfer, base
):
    leaves, samples, points = direction.shape
    rank = natural.shape[1]
    clusters = lax.axis_size("blk")
    here = lax.axis_index("blk")
    behind = here - top_list[...]
    behind = jnp.where(behind < 0, behind + clusters, behind)
    incoming = jnp.zeros((samples, rank), F32)
    for e in range(top_list.shape[1]):
        chosen = jnp.zeros((samples, rank), F32)
        for i in range(clusters):
            chosen = jnp.where(behind[:, e : e + 1] == i, tops[i].astype(F32), chosen)
        incoming = incoming + nt(chosen.astype(BF), top_coupling[0, e])
    down = nn(incoming.astype(BF), node_transfer[0]).astype(BF)
    for g in range(leaves):
        inward = nn(down, leaf_transfer[g]) + part[g]
        far = nn(inward.astype(BF), natural[g])
        base[g] = NUGGET * direction[g].astype(F32) + far


def near_kernel(near_h, *refs):
    pieces, tiles, (kept, given, mark, window, near, sems) = refs[:6], refs[6:8], refs[-6:]
    mark[...] = jnp.zeros_like(mark)
    leaves = window.shape[0] // 3
    samples = kept.shape[1]
    total = leaves * lax.axis_size("blk") * lax.axis_size("leaf")
    device = lax.axis_index("blk") * lax.axis_size("leaf") + lax.axis_index("leaf")
    anchor = (device - 1) * leaves
    copies = [pltpu.make_async_copy(near_h, near, sems.at[6])]
    for i, piece in enumerate(pieces):
        side, columns = i // 2, i % 2
        copies.append(
            pltpu.make_async_copy(
                piece,
                window.at[
                    side * leaves : (side + 1) * leaves,
                    columns * samples : (columns + 1) * samples,
                ],
                sems.at[i],
            )
        )
    for copy in copies:
        copy.start()
    for copy in copies:
        copy.wait()
    at = 0
    for part in tiles:

        def leaf(i, carry, part=part, at=at):
            g = lax.axis_index("sample") * kept.shape[0] + at + i
            values = []
            for e in range(near.shape[1]):
                values.append(window[lax.rem(near[g, e] - anchor + 2 * total, total)])
            field = nn(jnp.concatenate(values, axis=1), part[i]) * AMPLITUDE
            kept[at + i] = field[:samples]
            given[at + i] = field[samples:].astype(BF)
            return carry

        lax.fori_loop(0, part.shape[0], leaf, 0)
        at += part.shape[0]


def residual_kernel(step, base, kept, received, residual, updated_h, updated, norms, sems):
    half = kept.shape[0]
    chunks = sems.shape[1]
    size = half // chunks
    leaving = []
    for c in range(chunks):
        for k in range(2):
            part = pl.ds(k * half + c * size, size)
            leaving.append(
                pltpu.make_async_copy(updated.at[part], updated_h.at[part], sems.at[k, c])
            )
    core = lax.axis_index("sample")
    steps = column(step[...])
    totals = [jnp.zeros((step.shape[1], 1), F32)] * 2
    for i in range(half):
        for theirs in range(2):
            g = (core ^ theirs) * half + i
            near = received[i].astype(F32) if theirs else kept[i]
            old = residual[g]
            new = old - steps * (base[g] + near)
            updated[g] = new
            for k, value in enumerate((old, new)):
                totals[k] = totals[k] + jnp.sum(value * value, axis=1, keepdims=True)
        if i % size == size - 1:
            for k in range(2):
                leaving[2 * (i // size) + k].start()
    samples = steps.shape[0]
    lane = lax.broadcasted_iota(jnp.int32, (samples, 128), 1)
    sub = lax.broadcasted_iota(jnp.int32, (samples, 128), 0)
    rows = [jnp.sum(jnp.where(lane == sub, part, 0.0), axis=0, keepdims=True) for part in totals]
    row = lax.broadcasted_iota(jnp.int32, norms.shape[1:], 0)
    packed = jnp.where(row == 0, rows[0], jnp.where(row == 1, rows[1], 0.0))
    for i in range(norms.shape[0]):
        norms[i] = packed
    for copy in leaving:
        copy.wait()


def direction_kernel(norms, updated, direction, result, held, sems):
    leaves, samples, points = updated.shape
    sums = norms[0]
    for i in range(1, norms.shape[0]):
        sums = sums + norms[i]
    ratio = column((sums[1:2, :] / sums[0:1, :])[:, :samples])
    chunks = sems.shape[0]
    size = leaves // chunks
    copies = []
    for c in range(chunks):
        for g in range(c * size, (c + 1) * size):
            held[g] = (updated[g] + ratio * direction[g].astype(F32)).astype(BF)
        part = pl.ds(c * size, size)
        copies.append(pltpu.make_async_copy(held.at[part], result.at[part], sems.at[c]))
        copies[-1].start()
    for copy in copies:
        copy.wait()


def on_device(
    residual,
    direction,
    step,
    coords,
    order,
    basis,
    leaf_transfer,
    node_transfer,
    near_list,
    coupling_list,
    coupling,
    top_list,
    top_coupling,
):
    leaves, samples, points = direction.shape
    rank = basis.shape[1]
    entries = near_list.shape[1]
    half = leaves // 2
    blk_count = lax.axis_size("blk")
    leaf_count = lax.axis_size("leaf")
    shape = jax.ShapeDtypeStruct
    token = shape((8, 128), F32)
    vmem = pl.BlockSpec(memory_space=pltpu.VMEM)
    anywhere = pl.BlockSpec(memory_space=pl.ANY)
    hbm = pl.BlockSpec(memory_space=pltpu.HBM)

    coords = jnp.transpose(coords, (1, 0, 2))
    coords_prev = shifted(coords, RING, 1)
    coords_after = shifted(coords, RING, -1)
    operands = (order, basis, direction, leaf_transfer, node_transfer)
    resident = call(
        load_kernel,
        tuple(shape(array.shape, array.dtype) for array in operands),
        MIB,
        2 * MIB,
        in_specs=[hbm] * 5,
        out_specs=(vmem,) * 5,
        scratch_shapes=[pltpu.SemaphoreType.DMA((5,))],
        vmem=4,
    )(*in_hbm(*operands))
    travelling = ordered(direction, coords_prev, coords_after, resident[0])
    direction_prev = shifted(travelling, RING, 1)
    direction_after = shifted(travelling, RING, -1)
    natural, coef, lifted, up_mark = call(
        up_kernel,
        (
            pltpu.HBM((leaves, rank, points), BF),
            shape((leaves // 2, samples, 2 * rank), BF),
            shape((samples, rank), F32),
            token,
        ),
        4 * leaves * rank * points * points,
        6 * MIB,
        in_specs=[vmem] * 5,
        out_specs=(hbm, vmem, vmem, vmem),
        scratch_shapes=[pltpu.VMEM(basis.shape, BF), pltpu.SemaphoreType.DMA((4,))],
        vmem=8,
    )(ordered(resident[0], coords_prev, coords_after), *resident[1:])

    def make_tiles(start, done, *operands):
        count = half // 2
        outs = (pltpu.VMEM((count, entries * points, points), BF), token)
        if start == 0:
            outs += (shape((3 * leaves, points, 128), BF), shape(coords.shape, F32))
        return call(
            functools.partial(tile_kernel, start),
            outs,
            40 * count * entries * points * points,
            count * entries * points * points * (16 if start == 0 else 1),
            in_specs=[hbm, anywhere, hbm if start == 0 else vmem] + [vmem] * (len(operands) - 1),
            out_specs=(vmem,) * len(outs),
            scratch_shapes=[pltpu.VMEM(coords.shape, BF)] * (start == 0)
            + [pltpu.SMEM(near_list.shape, jnp.int32), pltpu.SemaphoreType.DMA((2,))],
            vmem=8,
        )(*in_hbm(near_list), done, *operands)

    coef_prev = shifted(coef, RING, 1)
    coef_after = shifted(coef, RING, -1)
    tiles_low, low_mark, spread_x, plain = make_tiles(
        0, up_mark, *in_hbm(coords), coords_prev, coords_after
    )
    leaving = call(
        after_kernel,
        shape((samples, 2 * rank), BF),
        MIB,
        MIB,
        in_specs=[anywhere, vmem],
        out_specs=vmem,
        vmem=4,
    )(low_mark, lifted)
    if blk_count <= 8:
        others = [shifted(leaving, "blk", by) for by in range(1, blk_count)]
    else:
        others = lax.all_gather(leaving[None], "blk", axis=0, tiled=True)
        places = jnp.mod(lax.axis_index("blk") - jnp.arange(blk_count, dtype=jnp.int32), blk_count)
        others = list(others[places][1:])
    tiles_high, high_mark = make_tiles(half // 2, low_mark, plain, spread_x)
    direction_other = partner(ordered(direction, high_mark, *others))
    direction_prev = ordered(direction_prev, high_mark, *others)
    direction_after = ordered(direction_after, high_mark, *others)
    together = call(
        collect_kernel,
        shape((blk_count, samples, 2 * rank), BF),
        MIB,
        MIB,
        in_specs=[vmem] * blk_count,
        out_specs=vmem,
        vmem=4,
    )(leaving, *others)
    terms = [shifted(together, "leaf", by) for by in range(1, leaf_count)]
    kept, given, near_mark = call(
        near_kernel,
        (shape((half, samples, points), F32), shape((half, samples, points), BF), token),
        MIB,
        MIB,
        in_specs=[hbm] + [anywhere] * 6 + [vmem] * 2,
        out_specs=(vmem,) * 3,
        scratch_shapes=[
            pltpu.VMEM((3 * leaves, 2 * samples, points), BF),
            pltpu.SMEM(near_list.shape, jnp.int32),
            pltpu.SemaphoreType.DMA((7,)),
        ],
        vmem=8,
    )(
        *in_hbm(near_list),
        direction_prev,
        partner(direction_prev),
        *in_hbm(direction),
        direction_other,
        direction_after,
        partner(direction_after),
        tiles_low,
        tiles_high,
    )

    part, given = call(
        couple_kernel,
        (shape((leaves, samples, rank), F32), shape((half, samples, points), BF)),
        2 * leaves * samples * rank * rank * 8,
        4 * MIB,
        in_specs=[vmem] * 4 + [hbm],
        out_specs=(vmem, vmem),
        scratch_shapes=[
            pltpu.VMEM((2 * leaves, samples, rank), BF),
            pltpu.SMEM(coupling_list.shape[::-1], jnp.int32),
            pltpu.SemaphoreType.DMA,
        ],
        vmem=8,
    )(given, coef_prev, coef_after, coupling, *in_hbm(coupling_list.T))
    tops, given = call(
        top_kernel,
        (shape((blk_count, samples, rank), BF), shape((half, samples, points), BF)),
        MIB,
        MIB,
        in_specs=[anywhere] + [vmem] * (2 + len(terms)),
        out_specs=(vmem, vmem),
        vmem=8,
    )(part, given, together, *terms)
    base = call(
        down_kernel,
        shape((leaves, samples, points), F32),
        2 * leaves * samples * rank * (points + rank),
        4 * MIB,
        in_specs=[vmem] * 8,
        out_specs=vmem,
        vmem=10,
    )(
        tops,
        part,
        leaf_transfer,
        natural,
        direction,
        top_list,
        top_coupling,
        node_transfer,
    )
    received = partner(given)

    devices = blk_count * leaf_count
    whole = shape((leaves, samples, points), F32)
    residual_next, updated, norms = call(
        residual_kernel,
        (whole, whole, shape((devices, 8, 128), F32)),
        4 * MIB,
        5 * MIB,
        in_specs=[vmem] * 5,
        out_specs=(hbm, vmem, vmem),
        scratch_shapes=[pltpu.SemaphoreType.DMA((2, 4))],
        vmem=8,
    )(step[None, :], base, kept, received, residual)
    norms = lax.all_to_all(norms, RING, 0, 0)
    direction_next = call(
        direction_kernel,
        shape((leaves, samples, points), BF),
        MIB,
        2 * MIB,
        in_specs=[vmem] * 3,
        out_specs=anywhere,
        scratch_shapes=[
            pltpu.VMEM((leaves, samples, points), BF),
            pltpu.SemaphoreType.DMA((4,)),
        ],
        vmem=8,
    )(norms, updated, direction)
    return (residual_next, direction_next)


def solution(mesh):
    in_specs = (
        P(("groups", "blk", "leaf"), "sample", None),
        P(("groups", "blk", "leaf"), "sample", None),
        P(("groups", "sample")),
        P(("groups", "blk", "leaf"), None, None),
        P(("groups", "blk", "leaf"), None),
        P(("groups", "blk", "leaf"), None, None),
        P(("groups", "blk", "leaf"), None, None),
        P(("groups", "blk", "leaf"), None, None),
        P(("groups", "blk", "leaf"), None),
        P(("groups", "blk", "leaf"), None),
        P(("groups", "blk", "leaf"), None, None, None),
        P(("groups", "blk"), None),
        P(("groups", "blk"), None, None, None),
    )
    out_specs = (
        P(("groups", "blk", "leaf"), "sample", None),
        P(("groups", "blk", "leaf"), "sample", None),
    )
    return jax.shard_map(
        on_device, mesh=mesh, in_specs=in_specs, out_specs=out_specs, check_vma=False
    )
```

```python
import functools
import math

import jax
import jax.numpy as jnp
from jax import lax
from jax.experimental import pallas as pl
from jax.experimental.pallas import tpu as pltpu
from jax.sharding import PartitionSpec as P

LEAF_DEV = 16

ROOT_THREE = math.sqrt(3.0)
LENGTH = 0.3
AMPLITUDE = 0.25
NUGGET = 0.5
SPREAD = 0.5 / LEAF_DEV
KAPPA = (ROOT_THREE / LENGTH) ** 2
LOG2E = 1.4426950408889634

RING = ("blk", "leaf")
BF = jnp.bfloat16
F32 = jnp.float32
MIB = 1 << 20


def shifted(array, axis, by):
    if isinstance(axis, tuple):
        count = math.prod(lax.axis_size(name) for name in axis)
    else:
        count = lax.axis_size(axis)
    return lax.ppermute(array, axis, [(i, (i + by) % count) for i in range(count)])


def partner(array):
    return lax.ppermute(array, "sample", [(0, 1), (1, 0)])


def ordered(array, *first):
    return lax.optimization_barrier((array,) + first)[0]


def column(row):
    size = row.shape[1]
    shape = (size, size)
    here = lax.broadcasted_iota(jnp.int32, shape, 0) == lax.broadcasted_iota(jnp.int32, shape, 1)
    return jnp.sum(jnp.where(here, row, 0.0), axis=1, keepdims=True)


def in_hbm(*arrays):
    return [pltpu.with_memory_space_constraint(array, pltpu.HBM) for array in arrays]


def thirds(value):
    high = value.astype(BF).astype(F32)
    rest = value - high
    middle = rest.astype(BF).astype(F32)
    return high, middle, rest - middle


def nt(left, right):
    return lax.dot_general(left, right, (((1,), (1,)), ((), ())), preferred_element_type=F32)


def nn(left, right):
    return jnp.dot(left, right, preferred_element_type=F32)


def call(kernel, outs, flops, moved, vmem=40, **kwargs):
    return pl.pallas_call(
        kernel,
        out_shape=outs,
        compiler_params=pltpu.CompilerParams(vmem_limit_bytes=vmem * MIB),
        cost_estimate=pl.CostEstimate(flops=flops, bytes_accessed=moved, transcendentals=0),
        **kwargs,
    )


def load_kernel(*refs):
    count = len(refs) // 2
    sources, targets, sems = refs[:count], refs[count:-1], refs[-1]
    copies = [
        pltpu.make_async_copy(source, target, sems.at[i])
        for i, (source, target) in enumerate(zip(sources, targets))
    ]
    for copy in copies:
        copy.start()
    for copy in copies:
        copy.wait()


def up_kernel(order, basis, direction, leaf_transfer, node_transfer, *refs):
    natural_h, coef, lifted, mark, natural, sems = refs
    mark[...] = jnp.zeros_like(mark)
    leaves, rank, points = basis.shape
    samples = direction.shape[1]
    chunks = sems.shape[0]
    size = leaves // chunks
    rows = lax.broadcasted_iota(jnp.int32, (points, points), 0)
    node = jnp.zeros((samples, rank), F32)
    leaving = []
    for g in range(leaves):
        spot = jnp.where(rows == order[g : g + 1, :], 1.0, 0.0).astype(BF)
        own = nt(basis[g], spot).astype(BF)
        natural[g] = own
        weights = nt(direction[g], own).astype(BF)
        coef[g // 2, :, (g % 2) * rank : (g % 2 + 1) * rank] = weights
        node = node + nt(weights, leaf_transfer[g])
        if g % size == size - 1:
            part = pl.ds(g + 1 - size, size)
            copy = pltpu.make_async_copy(natural.at[part], natural_h.at[part], sems.at[g // size])
            copy.start()
            leaving.append(copy)
    lifted[...] = nt(node.astype(BF), node_transfer[0])
    for copy in leaving:
        copy.wait()


def features(offsets):
    x, y, z = (offsets[i : i + 1] for i in range(3))
    square = thirds(KAPPA * (x * x + y * y + z * z))
    row = lax.broadcasted_iota(jnp.int32, (8, x.shape[1]), 0)
    packed = jnp.zeros((8, x.shape[1]), F32)
    for i, value in enumerate((x, y, z, jnp.ones_like(x)) + square):
        packed = jnp.where(row == i, value, packed)
    return packed.astype(BF)


def spread_features(offsets):
    lane = lax.broadcasted_iota(jnp.int32, (8, 128), 1)
    source = jnp.where(
        lane < 9,
        lane // 3,
        jnp.where(lane < 12, lane - 5, jnp.where(lane < 16, 7, jnp.where(lane < 64, 3, 0))),
    )
    source = jnp.where(lane < 112, source, 7)
    row = lax.broadcasted_iota(jnp.int32, (8, 128), 0)
    pick = jnp.where((row == source) & (row < 7), 1.0, 0.0).astype(BF)
    return lax.dot_general(
        features(offsets), pick, (((0,), (0,)), ((), ())), preferred_element_type=F32
    ).astype(BF)


def tile_kernel(start, near_h, _, *refs):
    if start == 0:
        own_h, prev, after, tiles, mark, spread_x, plain, listing, own, near, sem = refs
        handed = pltpu.make_async_copy(near_h, listing, sem.at[2])
        handed.start()
        offered = pltpu.make_async_copy(own_h, own, sem.at[1])
        offered.start()
    else:
        plain, spread_x, tiles, mark, near, sem = refs
        own = plain
    listed = pltpu.make_async_copy(near_h, near, sem.at[0])
    listed.start()
    mark[...] = jnp.zeros_like(mark)
    count = tiles.shape[0]
    entries = near.shape[1]
    points = own.shape[2]
    leaves = own.shape[1]
    total = leaves * lax.axis_size("blk") * lax.axis_size("leaf")
    device = lax.axis_index("blk") * lax.axis_size("leaf") + lax.axis_index("leaf")
    anchor = (device - 1) * leaves
    if start == 0:
        offered.wait()
        handed.wait()
        for side, ref in enumerate((prev, own, after)):
            offsets = ref[...].astype(F32)
            for j in range(leaves):
                spread_x[side * leaves + j] = spread_features(offsets[:, j])
            if side == 1:
                plain[...] = offsets
    listed.wait()
    row = lax.broadcasted_iota(jnp.int32, (16, points), 0)
    lane = lax.broadcasted_iota(jnp.int32, (1, 128), 1)

    def leaf(i, carry):
        g = lax.axis_index("sample") * (leaves // 2) + start + i
        x, y, z = (plain[k, pl.ds(g, 1), :] for k in range(3))
        first = jnp.where((row >= 9) & (row < 12), 1.0, jnp.zeros((16, points), F32))
        at = 0
        for value in (x, y, z):
            for part in thirds(value * (-2.0 * KAPPA)):
                first = jnp.where(row == at, part, first)
                at += 1
        slots = []
        gap = jnp.zeros((16, points), F32)
        for e in range(entries):
            slot = lax.rem(near[g, e] - anchor + 2 * total, total)
            slots.append(slot)
            gap = jnp.where(row == e, (leaves + g - slot).astype(F32) * SPREAD, gap)
        moved = x + gap
        fixed = thirds(KAPPA * (moved * moved + y * y + z * z))
        gaps = thirds(gap * (-2.0 * KAPPA))
        weights = jnp.concatenate(
            [part.astype(BF) for part in (first,) + fixed + gaps + (jnp.zeros_like(first),)],
            axis=0,
        )
        for e in range(entries):
            keep = jnp.where((lane < 16) | (lane % 16 == e), 1.0, 0.0).astype(BF)
            square = jnp.maximum(nn(spread_x[slots[e]] * keep, weights), 1e-30)
            scaled = square * lax.rsqrt(square)
            value = (1.0 + scaled) * jnp.exp2(scaled * (-LOG2E))
            tiles[i, e * points : (e + 1) * points, :] = value.astype(BF)
        return carry

    lax.fori_loop(0, count, leaf, 0)


def after_kernel(_, source, target):
    rank = source.shape[1]
    for i, part in enumerate(thirds(source[...])[:2]):
        target[:, i * rank : (i + 1) * rank] = part.astype(target.dtype)


def collect_kernel(*refs):
    terms, together = refs[:-1], refs[-1]
    for i, term in enumerate(terms):
        together[i] = term[...]


def top_kernel(_, given, *refs):
    terms, (tops, sent) = refs[:-2], refs[-2:]
    rank = tops.shape[2]
    total = terms[0][...].astype(F32)
    for term in terms[1:]:
        total = total + term[...].astype(F32)
    tops[...] = (total[:, :, :rank] + total[:, :, rank:]).astype(tops.dtype)
    sent[...] = given[...]


def couple_kernel(
    given, before, after, coupling, list_h, part, sent, window, coupling_list, sem
):
    copy = pltpu.make_async_copy(list_h, coupling_list, sem)
    copy.start()
    sent[...] = given[...]
    rows, _, lanes = before.shape
    rank = lanes // 2
    for side, packed in enumerate((before, after)):
        for g in range(2 * rows):
            piece = packed[g // 2, :, (g % 2) * rank : (g % 2 + 1) * rank]
            window[side * 2 * rows + g] = piece
    leaves, count = coupling.shape[:2]
    total = leaves * lax.axis_size("blk") * lax.axis_size("leaf")
    device = lax.axis_index("blk") * lax.axis_size("leaf") + lax.axis_index("leaf")
    anchor = (device - 1) * leaves
    copy.wait()
    for g in range(leaves):
        rows = []
        for c in range(count):
            slot = lax.rem(coupling_list[c, g] - anchor + 2 * total, total)
            slot = jnp.where(slot >= 2 * leaves, slot - leaves, slot)
            slot = jnp.minimum(slot, 2 * leaves - 1)
            rows.append(window[slot])
        columns = [coupling[g, c] for c in range(count)]
        part[g] = nt(jnp.concatenate(rows, axis=1), jnp.concatenate(columns, axis=1))


def down_kernel(
    tops, part, leaf_transfer, natural, direction, top_list, top_coupling, node_transfer, base
):
    leaves, samples, points = direction.shape
    rank = natural.shape[1]
    clusters = lax.axis_size("blk")
    here = lax.axis_index("blk")
    behind = here - top_list[...]
    behind = jnp.where(behind < 0, behind + clusters, behind)
    incoming = jnp.zeros((samples, rank), F32)
    for e in range(top_list.shape[1]):
        chosen = jnp.zeros((samples, rank), F32)
        for i in range(clusters):
            chosen = jnp.where(behind[:, e : e + 1] == i, tops[i].astype(F32), chosen)
        incoming = incoming + nt(chosen.astype(BF), top_coupling[0, e])
    down = nn(incoming.astype(BF), node_transfer[0]).astype(BF)
    for g in range(leaves):
        inward = nn(down, leaf_transfer[g]) + part[g]
        far = nn(inward.astype(BF), natural[g])
        base[g] = NUGGET * direction[g].astype(F32) + far


def near_kernel(near_h, *refs):
    pieces, tiles, (kept, given, mark, window, near, sems) = refs[:6], refs[6:8], refs[-6:]
    mark[...] = jnp.zeros_like(mark)
    leaves = window.shape[0] // 3
    samples = kept.shape[1]
    total = leaves * lax.axis_size("blk") * lax.axis_size("leaf")
    device = lax.axis_index("blk") * lax.axis_size("leaf") + lax.axis_index("leaf")
    anchor = (device - 1) * leaves
    copies = [pltpu.make_async_copy(near_h, near, sems.at[6])]
    for i, piece in enumerate(pieces):
        side, columns = i // 2, i % 2
        copies.append(
            pltpu.make_async_copy(
                piece,
                window.at[
                    side * leaves : (side + 1) * leaves,
                    columns * samples : (columns + 1) * samples,
                ],
                sems.at[i],
            )
        )
    for copy in copies:
        copy.start()
    for copy in copies:
        copy.wait()
    at = 0
    for part in tiles:

        def leaf(i, carry, part=part, at=at):
            g = lax.axis_index("sample") * kept.shape[0] + at + i
            values = []
            for e in range(near.shape[1]):
                values.append(window[lax.rem(near[g, e] - anchor + 2 * total, total)])
            field = nn(jnp.concatenate(values, axis=1), part[i]) * AMPLITUDE
            kept[at + i] = field[:samples]
            given[at + i] = field[samples:].astype(BF)
            return carry

        lax.fori_loop(0, part.shape[0], leaf, 0)
        at += part.shape[0]


def residual_kernel(step, base, kept, received, residual, updated_h, updated, norms, sems):
    half = kept.shape[0]
    chunks = sems.shape[1]
    size = half // chunks
    leaving = []
    for c in range(chunks):
        for k in range(2):
            part = pl.ds(k * half + c * size, size)
            leaving.append(
                pltpu.make_async_copy(updated.at[part], updated_h.at[part], sems.at[k, c])
            )
    core = lax.axis_index("sample")
    steps = column(step[...])
    totals = [jnp.zeros((step.shape[1], 1), F32)] * 2
    for i in range(half):
        for theirs in range(2):
            g = (core ^ theirs) * half + i
            near = received[i].astype(F32) if theirs else kept[i]
            old = residual[g]
            new = old - steps * (base[g] + near)
            updated[g] = new
            for k, value in enumerate((old, new)):
                totals[k] = totals[k] + jnp.sum(value * value, axis=1, keepdims=True)
        if i % size == size - 1:
            for k in range(2):
                leaving[2 * (i // size) + k].start()
    samples = steps.shape[0]
    lane = lax.broadcasted_iota(jnp.int32, (samples, 128), 1)
    sub = lax.broadcasted_iota(jnp.int32, (samples, 128), 0)
    rows = [jnp.sum(jnp.where(lane == sub, part, 0.0), axis=0, keepdims=True) for part in totals]
    row = lax.broadcasted_iota(jnp.int32, norms.shape[1:], 0)
    packed = jnp.where(row == 0, rows[0], jnp.where(row == 1, rows[1], 0.0))
    for i in range(norms.shape[0]):
        norms[i] = packed
    for copy in leaving:
        copy.wait()


def direction_kernel(norms, updated, direction, result, held, sems):
    leaves, samples, points = updated.shape
    sums = norms[0]
    for i in range(1, norms.shape[0]):
        sums = sums + norms[i]
    ratio = column((sums[1:2, :] / sums[0:1, :])[:, :samples])
    chunks = sems.shape[0]
    size = leaves // chunks
    copies = []
    for c in range(chunks):
        for g in range(c * size, (c + 1) * size):
            held[g] = (updated[g] + ratio * direction[g].astype(F32)).astype(BF)
        part = pl.ds(c * size, size)
        copies.append(pltpu.make_async_copy(held.at[part], result.at[part], sems.at[c]))
        copies[-1].start()
    for copy in copies:
        copy.wait()


def on_device(
    residual,
    direction,
    step,
    coords,
    order,
    basis,
    leaf_transfer,
    node_transfer,
    near_list,
    coupling_list,
    coupling,
    top_list,
    top_coupling,
):
    leaves, samples, points = direction.shape
    rank = basis.shape[1]
    entries = near_list.shape[1]
    half = leaves // 2
    blk_count = lax.axis_size("blk")
    leaf_count = lax.axis_size("leaf")
    shape = jax.ShapeDtypeStruct
    token = shape((8, 128), F32)
    vmem = pl.BlockSpec(memory_space=pltpu.VMEM)
    anywhere = pl.BlockSpec(memory_space=pl.ANY)
    hbm = pl.BlockSpec(memory_space=pltpu.HBM)

    coords = jnp.transpose(coords, (1, 0, 2))
    coords_prev = shifted(coords, RING, 1)
    coords_after = shifted(coords, RING, -1)
    operands = (order, basis, direction, leaf_transfer, node_transfer)
    resident = call(
        load_kernel,
        tuple(shape(array.shape, array.dtype) for array in operands),
        MIB,
        2 * MIB,
        in_specs=[hbm] * 5,
        out_specs=(vmem,) * 5,
        scratch_shapes=[pltpu.SemaphoreType.DMA((5,))],
        vmem=4,
    )(*in_hbm(*operands))
    travelling = ordered(direction, coords_prev, coords_after, resident[0])
    direction_prev = shifted(travelling, RING, 1)
    direction_after = shifted(travelling, RING, -1)
    natural, coef, lifted, up_mark = call(
        up_kernel,
        (
            pltpu.HBM((leaves, rank, points), BF),
            shape((leaves // 2, samples, 2 * rank), BF),
            shape((samples, rank), F32),
            token,
        ),
        4 * leaves * rank * points * points,
        6 * MIB,
        in_specs=[vmem] * 5,
        out_specs=(hbm, vmem, vmem, vmem),
        scratch_shapes=[pltpu.VMEM(basis.shape, BF), pltpu.SemaphoreType.DMA((4,))],
        vmem=8,
    )(ordered(resident[0], coords_prev, coords_after), *resident[1:])

    def make_tiles(start, listing, done, *operands):
        count = half // 2
        outs = (pltpu.VMEM((count, entries * points, points), BF), token)
        if start == 0:
            outs += (shape((3 * leaves, points, 128), BF), shape(coords.shape, F32))
            outs += (shape(near_list.shape, jnp.int32),)
        return call(
            functools.partial(tile_kernel, start),
            outs,
            40 * count * entries * points * points,
            count * entries * points * points * (16 if start == 0 else 1),
            in_specs=([hbm, anywhere, hbm] if start == 0 else [vmem, anywhere, vmem])
            + [vmem] * (len(operands) - 1),
            out_specs=(vmem,) * len(outs),
            scratch_shapes=[pltpu.VMEM(coords.shape, BF)] * (start == 0)
            + [pltpu.SMEM(near_list.shape, jnp.int32), pltpu.SemaphoreType.DMA((3,))],
            vmem=8,
        )(listing, done, *operands)

    coef_prev = shifted(coef, RING, 1)
    coef_after = shifted(coef, RING, -1)
    tiles_low, low_mark, spread_x, plain, listing = make_tiles(
        0, *in_hbm(near_list), up_mark, *in_hbm(coords), coords_prev, coords_after
    )
    leaving = call(
        after_kernel,
        shape((samples, 2 * rank), BF),
        MIB,
        MIB,
        in_specs=[anywhere, vmem],
        out_specs=vmem,
        vmem=4,
    )(low_mark, lifted)
    if blk_count <= 8:
        others = [shifted(leaving, "blk", by) for by in range(1, blk_count)]
    else:
        others = lax.all_gather(leaving[None], "blk", axis=0, tiled=True)
        places = jnp.mod(lax.axis_index("blk") - jnp.arange(blk_count, dtype=jnp.int32), blk_count)
        others = list(others[places][1:])
    tiles_high, high_mark = make_tiles(half // 2, listing, low_mark, plain, spread_x)
    direction_other = partner(ordered(direction, high_mark, *others))
    direction_prev = ordered(direction_prev, high_mark, *others)
    direction_after = ordered(direction_after, high_mark, *others)
    together = call(
        collect_kernel,
        shape((blk_count, samples, 2 * rank), BF),
        MIB,
        MIB,
        in_specs=[vmem] * blk_count,
        out_specs=vmem,
        vmem=4,
    )(leaving, *others)
    terms = [shifted(together, "leaf", by) for by in range(1, leaf_count)]
    kept, given, near_mark = call(
        near_kernel,
        (shape((half, samples, points), F32), shape((half, samples, points), BF), token),
        MIB,
        MIB,
        in_specs=[hbm] + [anywhere] * 6 + [vmem] * 2,
        out_specs=(vmem,) * 3,
        scratch_shapes=[
            pltpu.VMEM((3 * leaves, 2 * samples, points), BF),
            pltpu.SMEM(near_list.shape, jnp.int32),
            pltpu.SemaphoreType.DMA((7,)),
        ],
        vmem=8,
    )(
        *in_hbm(near_list),
        direction_prev,
        partner(direction_prev),
        *in_hbm(direction),
        direction_other,
        direction_after,
        partner(direction_after),
        tiles_low,
        tiles_high,
    )

    part, given = call(
        couple_kernel,
        (shape((leaves, samples, rank), F32), shape((half, samples, points), BF)),
        2 * leaves * samples * rank * rank * 8,
        4 * MIB,
        in_specs=[vmem] * 4 + [hbm],
        out_specs=(vmem, vmem),
        scratch_shapes=[
            pltpu.VMEM((2 * leaves, samples, rank), BF),
            pltpu.SMEM(coupling_list.shape[::-1], jnp.int32),
            pltpu.SemaphoreType.DMA,
        ],
        vmem=8,
    )(given, coef_prev, coef_after, coupling, *in_hbm(coupling_list.T))
    tops, given = call(
        top_kernel,
        (shape((blk_count, samples, rank), BF), shape((half, samples, points), BF)),
        MIB,
        MIB,
        in_specs=[anywhere] + [vmem] * (2 + len(terms)),
        out_specs=(vmem, vmem),
        vmem=8,
    )(part, given, together, *terms)
    base = call(
        down_kernel,
        shape((leaves, samples, points), F32),
        2 * leaves * samples * rank * (points + rank),
        4 * MIB,
        in_specs=[vmem] * 8,
        out_specs=vmem,
        vmem=10,
    )(
        tops,
        part,
        leaf_transfer,
        natural,
        direction,
        top_list,
        top_coupling,
        node_transfer,
    )
    received = partner(given)

    devices = blk_count * leaf_count
    whole = shape((leaves, samples, points), F32)
    residual_next, updated, norms = call(
        residual_kernel,
        (whole, whole, shape((devices, 8, 128), F32)),
        4 * MIB,
        5 * MIB,
        in_specs=[vmem] * 5,
        out_specs=(hbm, vmem, vmem),
        scratch_shapes=[pltpu.SemaphoreType.DMA((2, 4))],
        vmem=8,
    )(step[None, :], base, kept, received, residual)
    norms = lax.all_to_all(norms, RING, 0, 0)
    direction_next = call(
        direction_kernel,
        shape((leaves, samples, points), BF),
        MIB,
        2 * MIB,
        in_specs=[vmem] * 3,
        out_specs=anywhere,
        scratch_shapes=[
            pltpu.VMEM((leaves, samples, points), BF),
            pltpu.SemaphoreType.DMA((4,)),
        ],
        vmem=8,
    )(norms, updated, direction)
    return (residual_next, direction_next)


def solution(mesh):
    in_specs = (
        P(("groups", "blk", "leaf"), "sample", None),
        P(("groups", "blk", "leaf"), "sample", None),
        P(("groups", "sample")),
        P(("groups", "blk", "leaf"), None, None),
        P(("groups", "blk", "leaf"), None),
        P(("groups", "blk", "leaf"), None, None),
        P(("groups", "blk", "leaf"), None, None),
        P(("groups", "blk", "leaf"), None, None),
        P(("groups", "blk", "leaf"), None),
        P(("groups", "blk", "leaf"), None),
        P(("groups", "blk", "leaf"), None, None, None),
        P(("groups", "blk"), None),
        P(("groups", "blk"), None, None, None),
    )
    out_specs = (
        P(("groups", "blk", "leaf"), "sample", None),
        P(("groups", "blk", "leaf"), "sample", None),
    )
    return jax.shard_map(
        on_device, mesh=mesh, in_specs=in_specs, out_specs=out_specs, check_vma=False
    )
```
